32 devices in a mesh: groups: 2 (over x), dom: 16 (over z, y, core).
Axes of the slice: x: 2, y: 2, z: 4, core: 2. Of those that a mesh axis runs over, the one named last changes fastest.
Arguments:
- cells: bfloat16 [32768, 256], P(('groups', 'dom')), parts along dimension 0, may hold values from -6 to 6
- counts: int32 [32], P(('groups', 'dom')), parts along dimension 0, may hold values from 256 to 1024, as said below
- w_x: bfloat16 [256, 256], replicated, may hold values from -0.375 to 0.375
- w_fx: bfloat16 [256, 256], replicated, may hold values from -0.375 to 0.375
- w_slice: bfloat16 [32, 64], replicated, may hold values from -3.59375 to 3.59375
- w_temp: bfloat16 [32], replicated, may hold values from -1.1953125 to 1.1953125
- w_qkv: bfloat16 [3, 32, 32], replicated, may hold values from -1 to 1
- w_out: bfloat16 [256, 256], replicated, may hold values from -0.375 to 0.375
- cotangent: bfloat16 [32768, 256], P(('groups', 'dom')), parts along dimension 0, may hold values from -6 to 6
Outputs:
- result: bfloat16 [32768, 256], P(('groups', 'dom')), parts along dimension 0
- grad_cells: bfloat16 [32768, 256], P(('groups', 'dom')), parts along dimension 0
- grad_w_x: float32 [512, 256], P('groups'), parts along dimension 0
- grad_w_fx: float32 [512, 256], P('groups'), parts along dimension 0
- grad_w_slice: float32 [64, 64], P('groups'), parts along dimension 0
- grad_w_temp: float32 [64], P('groups'), parts along dimension 0
- grad_w_qkv: float32 [6, 32, 32], P('groups'), parts along dimension 0
- grad_w_out: float32 [512, 256], P('groups'), parts along dimension 0
The draws below stay inside these ranges and needn't reach their ends.
There are 2 independent parts, one for each index of `groups`. The reference program is written for one: setup_inputs(seed, part) draws one part's arguments, and reference() takes and returns one part's arrays. A program takes and returns all parts, laid end to end along the dimension named above; an argument that names none is the same for every part. Nothing has to cross between parts.
Inputs may be any that keep to these rules, and one draw needn't show every extreme that they name: `counts`: entry p is the number of live cells of partition p; they are its first rows, the rest of its 1024 rows are padding; some partition is full.
All inputs are finite; a program needn't handle non-finite values.
Results may differ from the reference program's by a relative error of at most 0.012.
The reference program's roundings to bfloat16 on the way count: a program that leaves them out, or rounds other values in their place, can miss the bound.
Values may be sent and summed in bfloat16 or wider, within the bound.
No kernel may reach another device: no remote copies, remote signals or barrier semaphores. Data moves between devices by JAX's collectives and lax.ppermute only.
A program may use at most 64 MiB of HBM per device.

```python
import math
import jax
import jax.numpy as jnp
from jax import lax

HEAD_DIM = 32
SLICES = 64
WIDTH = 256
ROW_CAPACITY = 1024
TOKENS = 16384
N_DOM = 16


def draw_counts(key, part):
    base = jax.random.randint(jax.random.fold_in(key, 11), (N_DOM,), ROW_CAPACITY // 4, ROW_CAPACITY + 1, dtype=jnp.int32)
    where = jax.random.randint(jax.random.fold_in(key, 23), (), 0, N_DOM, dtype=jnp.int32)
    return base.at[where].set(ROW_CAPACITY)


def block_levels(key, extent, split, smallest, high):
    level, own = 1.0, jax.random.fold_in(key, 6)
    for dim, parts in split:
        steps = jnp.exp(jax.random.uniform(jax.random.fold_in(own, dim), (parts,), jnp.float32, smallest / len(split), high / len(split)))
        level = level * jnp.repeat(steps, extent[dim] // parts).reshape([-1 if axis == dim else 1 for axis in range(len(extent))])
    return level


def scatter_about(stream_key, extent, width, bound, pieces=(), kind=jnp.bfloat16):
    array = jax.random.normal(stream_key, extent, jnp.float32) * width
    if len(pieces) > 0:
        array = block_levels(stream_key, extent, pieces, -0.22, 0.18) * array
    return jnp.clip(array, min=-bound, max=bound).astype(kind)


def setup_inputs(seed: int = 0, part: int = 0) -> dict:
    arg_keys = jax.random.split(jax.random.key(seed), 10)
    part_splits = jax.random.split(jax.random.fold_in(arg_keys[9], part), 10)
    cells = scatter_about(part_splits[0], (TOKENS, WIDTH), 1.0, 6.0, ((0, 16),))
    counts = draw_counts(jax.random.fold_in(jax.random.fold_in(arg_keys[9], part), 71), part)
    w_x = scatter_about(arg_keys[2], (WIDTH, WIDTH), WIDTH ** -0.5, 0.375)
    w_fx = scatter_about(arg_keys[3], (WIDTH, WIDTH), WIDTH ** -0.5, 0.375)
    w_slice = scatter_about(arg_keys[4], (HEAD_DIM, SLICES), 0.6, 3.59375)
    w_temp = scatter_about(arg_keys[5], (HEAD_DIM,), 0.3, 1.1953125)
    w_qkv = scatter_about(arg_keys[6], (3, HEAD_DIM, HEAD_DIM), HEAD_DIM ** -0.5, 1.0)
    w_out = scatter_about(arg_keys[7], (WIDTH, WIDTH), WIDTH ** -0.5, 0.375)
    cotangent = scatter_about(part_splits[8], (TOKENS, WIDTH), 1.0, 6.0, ((0, 16),))
    return dict(cells=cells, counts=counts, w_x=w_x, w_fx=w_fx, w_slice=w_slice, w_temp=w_temp, w_qkv=w_qkv, w_out=w_out, cotangent=cotangent)


def matrix_product(form, left, right):
    return jnp.einsum(form, left.astype(jnp.float32), right.astype(jnp.float32))

def slice_softmax(logits, temp_lin):
    temper = 0.5 + jax.nn.softplus(temp_lin)
    scaled = 10.0 * jnp.tanh(logits / 10.0) / temper
    powers = jnp.exp(scaled)
    return powers / lax.optimization_barrier(jnp.sum(powers, axis=-1, keepdims=True))

def make_tokens(numerator_sums, denominators):
    return numerator_sums / (denominators[:, None] + 1e-05)

def project_tokens(tokens, qkv_weight):
    return jnp.einsum('rd,kde->kre', tokens, qkv_weight, precision=lax.Precision.HIGHEST)

def attend(query_rows, key_matrix, value_matrix):
    score_matrix = jnp.einsum('zir,zjr->zij', query_rows, key_matrix, precision=lax.Precision.HIGHEST)
    score_matrix = score_matrix / math.sqrt(query_rows.shape[-1])
    powers = jnp.exp(10.0 * jnp.tanh(score_matrix / 10.0))
    attention_matrix = powers / lax.optimization_barrier(jnp.sum(powers, axis=-1, keepdims=True))
    return jnp.einsum('xwu,xut->xwt', attention_matrix, value_matrix, precision=lax.Precision.HIGHEST)

def mix_tokens(numerator_sums, denominators, qkv_weight):
    head_width = numerator_sums.shape[-1]
    maps = project_tokens(make_tokens(numerator_sums, denominators), qkv_weight)
    maps = maps.reshape(3, -1, SLICES, head_width)
    return attend(maps[0], maps[1], maps[2])

def cell_forward(cells, live_rows, w_x, w_fx, w_slice, w_temp):
    count_of_rows = cells.shape[0]
    head_width = w_slice.shape[0]
    count_of_heads = w_x.shape[1] // head_width
    projected = jnp.dot(cells, w_x, preferred_element_type=jnp.float32).astype(jnp.bfloat16)
    feature_rows = jnp.dot(cells, w_fx, preferred_element_type=jnp.float32).astype(jnp.bfloat16)
    per_head = projected.reshape(count_of_rows * count_of_heads, head_width)
    logits = jnp.dot(per_head, w_slice, preferred_element_type=jnp.float32)
    temp_lin = jnp.dot(per_head, w_temp.reshape(head_width, 1), preferred_element_type=jnp.float32)
    live_heads = jnp.repeat(live_rows, count_of_heads, axis=0)
    weight_matrix = (slice_softmax(logits, temp_lin) * live_heads).astype(jnp.bfloat16)
    weight_matrix = weight_matrix.reshape(count_of_rows, count_of_heads, -1)
    return (per_head, logits, temp_lin, live_heads, weight_matrix, feature_rows.reshape(count_of_rows, count_of_heads, head_width))

def cell_backward(cells, per_head, logits, temp_lin, live_heads, weight_matrix, feature_rows, hidden_gradient3, mixed_lowp, numerator_gradient_lowp, denominator_gradient, w_x, w_fx, w_slice, w_temp):
    count_of_rows, count_of_heads, slice_count = weight_matrix.shape
    head_width = w_slice.shape[0]
    weight_gradient = matrix_product('fvo,vxo->fvx', hidden_gradient3, mixed_lowp)
    weight_gradient = weight_gradient + matrix_product('fvo,vxo->fvx', feature_rows, numerator_gradient_lowp) + denominator_gradient[None]
    feature_gradient = matrix_product('rpc,pce->rpe', weight_matrix, numerator_gradient_lowp).astype(jnp.bfloat16).reshape(count_of_rows, -1)
    _, soft_back = jax.vjp(slice_softmax, logits, temp_lin)
    d_logits, d_temp = soft_back(weight_gradient.reshape(count_of_rows * count_of_heads, slice_count) * live_heads)
    d_logits = d_logits.astype(jnp.bfloat16)
    d_temp = d_temp.astype(jnp.bfloat16)
    d_head = jnp.dot(d_logits, w_slice.T, preferred_element_type=jnp.float32)
    d_head = d_head + jnp.dot(d_temp, w_temp.reshape(1, head_width), preferred_element_type=jnp.float32)
    d_proj = d_head.reshape(count_of_rows, -1).astype(jnp.bfloat16)
    grad_cells = jnp.dot(d_proj, w_x.T, preferred_element_type=jnp.float32)
    grad_cells = (grad_cells + jnp.dot(feature_gradient, w_fx.T, preferred_element_type=jnp.float32)).astype(jnp.bfloat16)
    grad_wx = jnp.dot(cells.T, d_proj, preferred_element_type=jnp.float32)
    grad_wfx = jnp.dot(cells.T, feature_gradient, preferred_element_type=jnp.float32)
    grad_slice = jnp.dot(per_head.T, d_logits, preferred_element_type=jnp.float32)
    grad_temp = jnp.dot(per_head.T, d_temp, preferred_element_type=jnp.float32).reshape(head_width)
    return (grad_cells, grad_wx, grad_wfx, grad_slice, grad_temp)

def reference(cells, counts, w_x, w_fx, w_slice, w_temp, w_qkv, w_out, cotangent):
    model_width = w_x.shape[0]
    head_width = w_slice.shape[0]
    count_of_heads = model_width // head_width
    blocks = cells.reshape(N_DOM, ROW_CAPACITY, model_width)
    cot_blocks = cotangent.reshape(N_DOM, ROW_CAPACITY, model_width)
    positions = jnp.arange(ROW_CAPACITY, dtype=jnp.int32)

    def live_of(count):
        return (positions < count).astype(jnp.float32)[:, None]

    def sums_of(item):
        block, count = item
        outs_fwd = cell_forward(block, live_of(count), w_x, w_fx, w_slice, w_temp)
        weight_matrix, feature_rows = (outs_fwd[4], outs_fwd[5])
        return (matrix_product('skb,sko->kbo', weight_matrix, feature_rows), lax.optimization_barrier(jnp.sum(weight_matrix.astype(jnp.float32), axis=0)))
    numer_all, denom_all = lax.map(sums_of, (blocks, counts.astype(jnp.int32)))
    numerator_sums = lax.optimization_barrier(jnp.sum(numer_all, axis=0))
    denominators = lax.optimization_barrier(jnp.sum(denom_all, axis=0))
    qkv_weight = w_qkv.astype(jnp.float32)
    mixed, mix_back = jax.vjp(mix_tokens, numerator_sums.reshape(-1, head_width), denominators.reshape(-1), qkv_weight)
    mixed_lowp = mixed.astype(jnp.bfloat16)

    def forward_of(item):
        block, count, cot_block = item
        outs_fwd = cell_forward(block, live_of(count), w_x, w_fx, w_slice, w_temp)
        weight_matrix = outs_fwd[4]
        hidden_rows = matrix_product('rpc,pce->rpe', weight_matrix, mixed_lowp).astype(jnp.bfloat16).reshape(ROW_CAPACITY, model_width)
        result = jnp.dot(hidden_rows, w_out, preferred_element_type=jnp.float32).astype(jnp.bfloat16)
        hidden_gradient = jnp.dot(cot_block, w_out.T, preferred_element_type=jnp.float32).astype(jnp.bfloat16)
        out_grad = jnp.dot(hidden_rows.T, cot_block, preferred_element_type=jnp.float32)
        mixed_gradient = matrix_product('skb,sko->kbo', weight_matrix, hidden_gradient.reshape(ROW_CAPACITY, count_of_heads, head_width))
        return (result, out_grad, mixed_gradient)
    results, out_grads, d_mixed_all = lax.map(forward_of, (blocks, counts.astype(jnp.int32), cot_blocks))
    d_numer, denominator_gradient, d_qkv = mix_back(lax.optimization_barrier(jnp.sum(d_mixed_all, axis=0)))
    numerator_gradient_lowp = d_numer.reshape(count_of_heads, -1, head_width).astype(jnp.bfloat16)
    denominator_gradient = denominator_gradient.reshape(count_of_heads, -1)

    def backward_of(item):
        block, count, cot_block = item
        per_head, logits, temp_lin, live_heads, weight_matrix, feature_rows = cell_forward(block, live_of(count), w_x, w_fx, w_slice, w_temp)
        hidden_gradient = jnp.dot(cot_block, w_out.T, preferred_element_type=jnp.float32).astype(jnp.bfloat16)
        return cell_backward(block, per_head, logits, temp_lin, live_heads, weight_matrix, feature_rows, hidden_gradient.reshape(ROW_CAPACITY, count_of_heads, head_width), mixed_lowp, numerator_gradient_lowp, denominator_gradient, w_x, w_fx, w_slice, w_temp)
    grad_cells, grad_wx, grad_wfx, grad_slice, grad_temp = lax.map(backward_of, (blocks, counts.astype(jnp.int32), cot_blocks))
    scale = 1.0 / math.sqrt(TOKENS)
    return (results.reshape(TOKENS, model_width), grad_cells.reshape(TOKENS, model_width), lax.optimization_barrier(jnp.sum(grad_wx, axis=0)) * scale, lax.optimization_barrier(jnp.sum(grad_wfx, axis=0)) * scale, lax.optimization_barrier(jnp.sum(grad_slice, axis=0)) * scale, lax.optimization_barrier(jnp.sum(grad_temp, axis=0)) * scale, d_qkv * scale, lax.optimization_barrier(jnp.sum(out_grads, axis=0)) * scale)
```

```python
import functools
import math

import jax
import jax.numpy as jnp
from jax import lax
from jax.experimental import pallas as pl
from jax.experimental.pallas import tpu as pltpu
from jax.sharding import PartitionSpec as P

F32 = jnp.float32
BF16 = jnp.bfloat16
HIGHEST = lax.Precision.HIGHEST
HEADS = 8
SLICES = 64
HEAD = 32
WIDTH = HEADS * HEAD
ROWS1 = 144
LOG2E = math.log2(math.e)
CHUNK = 256


def nn(a, b, precision=None):
    return lax.dot_general(
        a, b, (((1,), (0,)), ((), ())), precision=precision, preferred_element_type=F32
    )


def nt(a, b, precision=None):
    return lax.dot_general(
        a, b, (((1,), (1,)), ((), ())), precision=precision, preferred_element_type=F32
    )


def iota(shape, dim):
    return lax.broadcasted_iota(jnp.int32, shape, dim)


def slice_blocks(w_slice):
    tall = jnp.concatenate([w_slice] * 4, axis=0)
    pick = (iota((SLICES, 256), 1) % SLICES == iota((SLICES, 256), 0)).astype(BF16)
    wide = nn(tall, pick)
    same = iota((128, 256), 0) // HEAD == iota((128, 256), 1) // SLICES
    return jnp.where(same, wide, 0.0)


def temp_blocks(w_temp):
    pick = (iota((HEAD, WIDTH), 1) % HEAD == iota((HEAD, WIDTH), 0)).astype(BF16)
    wide = nn(jnp.broadcast_to(w_temp, (HEADS, HEAD)), pick)
    same = iota((HEADS, WIDTH), 0) == iota((HEADS, WIDTH), 1) // HEAD
    return jnp.where(same, wide, 0.0).astype(BF16)


def forward_kernel(
    counts, cells, cot, w_x, w_fx, w_slice, w_temp, w_out,
    weights, proj, fd, stats, keep, send,
    wxt, wft, wsb,
):
    core = lax.rem(lax.axis_index("dom"), 2)
    rows = cells.shape[0]
    wxt[...] = w_x[...].T
    wft[...] = w_fx[...].T
    wsb[...] = slice_blocks(w_slice[...]).T.astype(BF16)
    wtb = temp_blocks(w_temp[...])
    count = counts[0]

    def chunk(j, carry):
        at = pl.ds(pl.multiple_of(j * CHUNK, CHUNK), CHUNK)
        c = cells[at, :]
        projected = nt(wxt[...], c).astype(BF16)
        proj[:, at] = projected
        feat = nt(wft[...], c).astype(BF16)
        dhid = nt(w_out[...], cot[at, :]).astype(BF16)
        for h in range(HEADS):
            mine = slice(HEAD * h, HEAD * h + HEAD)
            fd[2 * HEAD * h : 2 * HEAD * h + HEAD, at] = feat[mine]
            fd[2 * HEAD * h + HEAD : 2 * HEAD * h + 2 * HEAD, at] = dhid[mine]
        lin = nn(wtb, projected)
        e = jnp.exp(-jnp.abs(lin))
        soft = jnp.maximum(lin, 0.0) + jnp.log(1.0 + e)
        inv = 1.0 / (0.5 + soft)
        sig = jnp.where(lin >= 0, 1.0, e) / (1.0 + e)
        a = inv * (10.0 * LOG2E)
        live = jnp.where(j * CHUNK + iota((1, CHUNK), 1) < count, 1.0, 0.0)
        norms = []
        for g in range(2):
            x = nn(wsb[...], projected[128 * g : 128 * g + 128])
            for k in range(4):
                h = 4 * g + k
                t = jnp.tanh(x[SLICES * k : SLICES * k + SLICES] * 0.1)
                p = jnp.exp2(t * a[h : h + 1])
                r = live / jnp.sum(p, axis=0, keepdims=True)
                weights[SLICES * h : SLICES * h + SLICES, at] = (p * r).astype(BF16)
                norms.append(r)
        stats[0:8, at] = a
        stats[8:16, at] = inv
        stats[16:24, at] = inv * inv * sig * (-10.0)
        stats[24:32, at] = jnp.concatenate(norms, axis=0)
        return carry

    lax.fori_loop(0, rows // CHUNK, chunk, 0)
    ones = jnp.ones((16, rows), BF16)
    first = iota((64, 128), 1) < SLICES
    blocks, sums = [], []
    for q in range(4):
        mine = slice(128 * q, 128 * q + 128)
        out = nt(jnp.concatenate([fd[mine, :], ones], axis=0), weights[mine, :])
        blocks.append(jnp.where(first, out[0:64], out[64:128]))
        sums.append(out[128:129])
    zero = jnp.zeros((14, 128), F32)
    halves = [
        jnp.concatenate([blocks[2 * s], blocks[2 * s + 1], sums[2 * s], sums[2 * s + 1], zero], 0)
        for s in range(2)
    ]
    keep[...] = jnp.where(core == 0, halves[0], halves[1])
    send[...] = jnp.where(core == 0, halves[1], halves[0])


def spread_kernel(mine, other, out):
    total = (mine[...] + other[...]).astype(BF16)
    n = mine.shape[0]
    for k in range(out.shape[0] // n):
        out[n * k : n * k + n, :] = total


def sum_blocks(ref, n):
    total = ref[0:n, :].astype(F32)
    for k in range(1, ref.shape[0] // n):
        total = total + ref[n * k : n * k + n, :].astype(F32)
    return total


def mix_kernel(parts, w_qkv, out):
    total = sum_blocks(parts, ROWS1)
    numer = jnp.concatenate([total[0:32], total[64:96]], axis=1)
    d_mixed = jnp.concatenate([total[32:64], total[96:128]], axis=1)
    denom = jnp.concatenate([total[128:129], total[129:130]], axis=1) + 1e-05
    inverse = 1.0 / denom
    tokens = numer * inverse
    maps = [w_qkv[k].astype(F32) for k in range(3)]
    q, key, val = [nn(m.T, tokens, HIGHEST) for m in maps]
    key_rows, val_rows = key.T, val.T
    scores = nn(key_rows, q, HIGHEST) * (1.0 / math.sqrt(HEAD))
    same = iota((256, 256), 0) // SLICES == iota((256, 256), 1) // SLICES
    t = jnp.tanh(scores * 0.1)
    powers = jnp.where(same, jnp.exp2(t * (10.0 * LOG2E)), 0.0)
    att = powers * (1.0 / jnp.sum(powers, axis=0, keepdims=True))
    mixed = nn(val, att, HIGHEST)
    d_att = nn(val_rows, d_mixed, HIGHEST)
    d_val = nt(d_mixed, att, HIGHEST)
    inner = jnp.sum(att * d_att, axis=0, keepdims=True)
    d_scores = att * (d_att - inner) * ((1.0 - t * t) * (1.0 / math.sqrt(HEAD)))
    d_q = nn(key, d_scores, HIGHEST)
    d_key = nt(q, d_scores, HIGHEST)
    grads = (d_q, d_key, d_val)
    d_tokens = sum(nn(m, g, HIGHEST) for m, g in zip(maps, grads))
    d_numer = d_tokens * inverse
    d_denom = -jnp.sum(d_numer * tokens, axis=0, keepdims=True)
    out[0:32, :] = d_numer.astype(BF16).astype(F32)
    out[32:64, :] = mixed.astype(BF16).astype(F32)
    out[64:72, :] = jnp.broadcast_to(d_denom, (8, 256))
    for k in range(3):
        out[72 + 32 * k : 104 + 32 * k, 0:32] = nt(tokens, grads[k], HIGHEST)
        out[72 + 32 * k : 104 + 32 * k, 32:256] = jnp.zeros((32, 224), F32)


def backward_kernel(
    scale,
    cells, cot, weights, proj, fd, stats, mine, other, w_x, w_fx, w_slice, w_temp, w_out,
    result, grad_cells, keep, send, grad_qkv,
    hid, dpf, dlog, dtemp, lhs_h, lhs_w, dden, wsb, wsd, wxf, wot,
):
    core = lax.rem(lax.axis_index("dom"), 2)
    rows = cells.shape[0]
    lower = core == 0
    blocks = slice_blocks(w_slice[...])
    wsd[...] = blocks.astype(BF16)
    wsb[...] = blocks.T.astype(BF16)
    wtb = temp_blocks(w_temp[...]).astype(F32).T
    wxf[:, 0:WIDTH] = w_x[...]
    wxf[:, WIDTH : 2 * WIDTH] = w_fx[...]
    wot[...] = w_out[...].T
    diag64 = iota((256, 256), 0) // 64 == iota((256, 256), 1) // 64
    diag32 = iota((128, 256), 0) // 32 == iota((128, 256), 1) // 64
    for g in range(2):
        e = jnp.where(lower == (g == 0), mine[0:72, :], other[0:72, :])
        both = jnp.where(diag64, jnp.concatenate([e[0:64]] * 4, axis=0), 0.0)
        lhs_w[g] = both.T.astype(BF16)
        lhs_h[g, 0:128, :] = jnp.where(
            diag32, jnp.concatenate([e[32:64]] * 4, axis=0), 0.0
        ).astype(BF16)
        lhs_h[g, 128:256, :] = jnp.where(
            diag32, jnp.concatenate([e[0:32]] * 4, axis=0), 0.0
        ).astype(BF16)
        column = e[64:72].T[:, 0:1]
        dden[256 * g : 256 * g + 256, :] = jnp.broadcast_to(column, (256, CHUNK))
    for k in range(3):
        block = slice(72 + 32 * k, 104 + 32 * k)
        grad_qkv[k] = (mine[block, 0:32] + other[block, 0:32]) * scale

    def chunk(j, carry):
        at = pl.ds(pl.multiple_of(j * CHUNK, CHUNK), CHUNK)
        a = stats[0:8, at]
        inv = stats[8:16, at]
        slope = stats[16:24, at]
        norm = stats[24:32, at]
        for g in range(2):
            half = slice(128 * g, 128 * g + 128)
            wide = slice(256 * g, 256 * g + 256)
            hf = nn(lhs_h[g], weights[wide, at])
            hid[half, at] = hf[0:128].astype(BF16)
            dpf[WIDTH + 128 * g : WIDTH + 128 * g + 128, at] = hf[128:256].astype(BF16)
            dw = nn(lhs_w[g], fd[wide, at])
            x = nn(wsb[...], proj[half, at])
            outer = []
            for k in range(4):
                h = 4 * g + k
                sub = slice(SLICES * k, SLICES * k + SLICES)
                rng = slice(SLICES * h, SLICES * h + SLICES)
                one = slice(h, h + 1)
                t = jnp.tanh(x[sub] * 0.1)
                soft = jnp.exp2(t * a[one]) * norm[one]
                d = dw[sub] + dden[rng, :]
                inner = jnp.sum(soft * d, axis=0, keepdims=True)
                ds = soft * (d - inner)
                dlog[rng, at] = (ds * ((1.0 - t * t) * inv[one])).astype(BF16)
                dt = jnp.sum(ds * t, axis=0, keepdims=True) * slope[one]
                dt = dt.astype(BF16).astype(F32)
                dtemp[one, at] = dt
                outer.append(wtb[HEAD * h : HEAD * h + HEAD, h : h + 1] * dt)
            dp = nn(wsd[...], dlog[wide, at]) + jnp.concatenate(outer, axis=0)
            dpf[half, at] = dp.astype(BF16)
        gct = nn(wxf[...], dpf[:, at])
        grad_cells[at, :] = gct.T.astype(BF16)
        rst = nn(wot[...], hid[:, at])
        result[at, :] = rst.T.astype(BF16)
        return carry

    lax.fori_loop(0, rows // CHUNK, chunk, 0)
    d_out = nn(hid[...], cot[...])
    d_in = nn(dpf[...], cells[...])
    d_x = d_in[0:WIDTH].T
    d_fx = d_in[WIDTH : 2 * WIDTH].T
    even = jnp.zeros((HEAD, 128), F32)
    odd = jnp.zeros((HEAD, 128), F32)
    for q in range(4):
        pair = dlog[128 * q : 128 * q + 128, :]
        even = even + nt(proj[64 * q : 64 * q + 32, :], pair)
        odd = odd + nt(proj[64 * q + 32 : 64 * q + 64, :], pair)
    d_slice = jnp.where(iota((HEAD, 128), 1) < SLICES, even, odd)
    d_slice = jnp.concatenate([d_slice[0:16], d_slice[16:32]], axis=1)
    d_temp = nt(dtemp[...].astype(BF16), proj[...])
    own = iota((HEADS, WIDTH), 0) == iota((HEADS, WIDTH), 1) // HEAD
    d_temp = jnp.where(own, d_temp, 0.0)
    d_temp = jnp.broadcast_to(jnp.sum(d_temp, axis=0, keepdims=True), (HEADS, WIDTH))
    for ref, first in ((keep, lower), (send, jnp.logical_not(lower))):
        for i, grad in enumerate((d_out, d_x, d_fx)):
            ref[128 * i : 128 * i + 128, :] = jnp.where(first, grad[0:128], grad[128:256]).astype(
                BF16
            )
        ref[384:400, :] = jnp.concatenate(
            [jnp.where(first, d_slice[0:8], d_slice[8:16]), d_temp], axis=0
        ).astype(BF16)
        ref[400:, :] = jnp.zeros((ref.shape[0] - 400, WIDTH), BF16)


def add_kernel(mine, other, out):
    out[...] = (mine[...].astype(F32) + other[...].astype(F32)).astype(BF16)


def place_kernel(mine, other, d_x, d_fx, d_slice, d_temp, d_out):
    core = lax.rem(lax.axis_index("dom"), 2)
    lower = core == 0
    small = []
    for s in range(2):
        src = jnp.where(lower == (s == 0), mine[0:400, :], other[0:400, :]).astype(F32)
        for i, ref in enumerate((d_out, d_x, d_fx)):
            ref[128 * s : 128 * s + 128, :] = src[128 * i : 128 * i + 128]
        small.append(src[384:392])
        if s == 0:
            v = src[392:400]
            v = v[:, 0:128] + v[:, 128:256]
            v = v + pltpu.roll(v, 64, 1)
            v = v + pltpu.roll(v, 32, 1)
            d_temp[...] = v[0:1, 0:32]
    rows = jnp.concatenate(
        [small[0][:, 0:128], small[1][:, 0:128], small[0][:, 128:256], small[1][:, 128:256]], axis=0
    )
    rows = rows + pltpu.roll(rows, 64, 1)
    d_slice[...] = rows[:, 0:SLICES]


VMEM = pl.BlockSpec(memory_space=pltpu.VMEM)
SMEM = pl.BlockSpec(memory_space=pltpu.SMEM)


def call(kernel, shapes, args, scratch=(), scalars=0, name=None):
    return pl.pallas_call(
        kernel,
        out_shape=[jax.ShapeDtypeStruct(s, d) for s, d in shapes],
        in_specs=[SMEM] * scalars + [VMEM] * (len(args) - scalars),
        out_specs=[VMEM] * len(shapes),
        scratch_shapes=[pltpu.VMEM(s, d) for s, d in scratch],
        name=name,
    )(*args)


def body(devices, cells, counts, w_x, w_fx, w_slice, w_temp, w_qkv, w_out, cotangent):
    rows = cells.shape[0]
    peers = devices // 2
    pairs = [(i, i ^ 1) for i in range(devices)]
    groups = [list(range(c, devices, 2)) for c in range(2)]
    scale = 1.0 / math.sqrt(rows * devices)
    temp = w_temp.reshape(1, HEAD)
    hm = HEADS * SLICES

    def exchange(x):
        return lax.all_to_all(x, "dom", 0, 0, axis_index_groups=groups, tiled=True)

    weights, proj, fd, stats, keep, send = call(
        forward_kernel,
        [
            ((hm, rows), BF16),
            ((WIDTH, rows), BF16),
            ((2 * WIDTH, rows), BF16),
            ((32, rows), F32),
            ((ROWS1, 128), F32),
            ((ROWS1, 128), F32),
        ],
        (counts, cells, cotangent, w_x, w_fx, w_slice, temp, w_out),
        scratch=[((256, 256), BF16), ((256, 256), BF16), ((256, 128), BF16)],
        scalars=1,
        name="forward",
    )
    other = lax.ppermute(send, "dom", pairs)
    (spread,) = call(
        spread_kernel, [((peers * ROWS1, 128), BF16)], (keep, other), name="spread"
    )
    parts = exchange(spread)
    (mine,) = call(mix_kernel, [((168, 256), F32)], (parts, w_qkv), name="mix")
    other = lax.ppermute(mine, "dom", pairs)
    chunk = -(-400 // peers)
    chunk = -(-chunk // 8) * 8
    half = chunk * peers
    result, grad_cells, keep, send, grad_qkv = call(
        functools.partial(backward_kernel, scale),
        [
            ((rows, WIDTH), BF16),
            ((rows, WIDTH), BF16),
            ((half, WIDTH), BF16),
            ((half, WIDTH), BF16),
            ((3, HEAD, HEAD), F32),
        ],
        (cells, cotangent, weights, proj, fd, stats, mine, other)
        + (w_x, w_fx, w_slice, temp, w_out),
        scratch=[
            ((WIDTH, rows), BF16),
            ((2 * WIDTH, rows), BF16),
            ((hm, rows), BF16),
            ((8, rows), F32),
            ((2, 256, 256), BF16),
            ((2, 256, 256), BF16),
            ((hm, CHUNK), F32),
            ((256, 128), BF16),
            ((128, 256), BF16),
            ((256, 512), BF16),
            ((256, 256), BF16),
        ],
        name="backward",
    )
    other = lax.ppermute(send, "dom", pairs)
    (summed,) = call(add_kernel, [((half, WIDTH), BF16)], (keep, other), name="pair_add")
    parts = exchange(summed)

    def gather(parts_ref, out):
        total = (sum_blocks(parts_ref, chunk) * scale).astype(BF16)
        for k in range(peers):
            out[chunk * k : chunk * k + chunk, :] = total

    (spread,) = call(gather, [((half, WIDTH), BF16)], (parts,), name="gather")
    mine = exchange(spread)
    other = lax.ppermute(mine, "dom", pairs)
    d_x, d_fx, d_slice, d_temp, d_out = call(
        place_kernel,
        [
            ((WIDTH, WIDTH), F32),
            ((WIDTH, WIDTH), F32),
            ((HEAD, SLICES), F32),
            ((1, HEAD), F32),
            ((WIDTH, WIDTH), F32),
        ],
        (mine, other),
        name="place",
    )
    return result, grad_cells, d_x, d_fx, d_slice, d_temp.reshape(HEAD), grad_qkv, d_out


def solution(mesh):
    cell = P(("groups", "dom"), None)
    return jax.shard_map(
        functools.partial(body, mesh.shape["dom"]),
        mesh=mesh,
        in_specs=(cell, P(("groups", "dom")), P(), P(), P(), P(), P(), P(), cell),
        out_specs=(
            cell,
            cell,
            P("groups", None),
            P("groups", None),
            P("groups", None),
            P("groups"),
            P("groups", None, None),
            P("groups", None),
        ),
        check_vma=False,
    )
```

```python
import functools
import math

import jax
import jax.numpy as jnp
from jax import lax
from jax.experimental import pallas as pl
from jax.experimental.pallas import tpu as pltpu
from jax.sharding import PartitionSpec as P

F32 = jnp.float32
BF16 = jnp.bfloat16
HIGHEST = lax.Precision.HIGHEST
HEADS = 8
SLICES = 64
HEAD = 32
WIDTH = HEADS * HEAD
ROWS1 = 144
LOG2E = math.log2(math.e)
CHUNK = 256


def nn(a, b, precision=None):
    return lax.dot_general(
        a, b, (((1,), (0,)), ((), ())), precision=precision, preferred_element_type=F32
    )


def nt(a, b, precision=None):
    return lax.dot_general(
        a, b, (((1,), (1,)), ((), ())), precision=precision, preferred_element_type=F32
    )


def iota(shape, dim):
    return lax.broadcasted_iota(jnp.int32, shape, dim)


def slice_blocks(w_slice):
    tall = jnp.concatenate([w_slice] * 4, axis=0)
    pick = (iota((SLICES, 256), 1) % SLICES == iota((SLICES, 256), 0)).astype(BF16)
    wide = nn(tall, pick)
    same = iota((128, 256), 0) // HEAD == iota((128, 256), 1) // SLICES
    return jnp.where(same, wide, 0.0)


def temp_blocks(w_temp):
    pick = (iota((HEAD, WIDTH), 1) % HEAD == iota((HEAD, WIDTH), 0)).astype(BF16)
    wide = nn(jnp.broadcast_to(w_temp, (HEADS, HEAD)), pick)
    same = iota((HEADS, WIDTH), 0) == iota((HEADS, WIDTH), 1) // HEAD
    return jnp.where(same, wide, 0.0).astype(BF16)


def forward_kernel(
    counts, cells_hbm, cot_hbm, *refs,
):
    hbm, refs = refs[:5], refs[5:]
    (weights, proj, fd, stats, keep, send), refs = refs[:6], refs[6:]
    cells, cot, w_x, w_fx, w_slice, w_temp, w_out, small, big, wxt, wft, wsb = refs
    core = lax.rem(lax.axis_index("dom"), 2)
    rows = cells.shape[0]
    steps = rows // CHUNK

    def load(source, target, slot, j):
        at = pl.ds(pl.multiple_of(j * CHUNK, CHUNK), CHUNK)
        return pltpu.make_async_copy(source.at[at, :], target.at[at, :], big.at[slot, j])

    tables = [
        pltpu.make_async_copy(source, target, small.at[i])
        for i, (source, target) in enumerate(zip(hbm, (w_x, w_fx, w_slice, w_temp, w_out)))
    ]
    for table in tables:
        table.start()
    for j in range(steps):
        load(cells_hbm, cells, 0, j).start()
        load(cot_hbm, cot, 1, j).start()
    for table in tables:
        table.wait()
    wtb = temp_blocks(w_temp[...])
    wxt[...] = w_x[...].T
    wft[...] = w_fx[...].T
    wsb[...] = slice_blocks(w_slice[...]).T.astype(BF16)
    count = counts[0]

    def chunk(j, carry):
        at = pl.ds(pl.multiple_of(j * CHUNK, CHUNK), CHUNK)
        load(cells_hbm, cells, 0, j).wait()
        load(cot_hbm, cot, 1, j).wait()
        c = cells[at, :]
        projected = nt(wxt[...], c).astype(BF16)
        proj[:, at] = projected
        feat = nt(wft[...], c).astype(BF16)
        dhid = nt(w_out[...], cot[at, :]).astype(BF16)
        for h in range(HEADS):
            mine = slice(HEAD * h, HEAD * h + HEAD)
            fd[2 * HEAD * h : 2 * HEAD * h + HEAD, at] = feat[mine]
            fd[2 * HEAD * h + HEAD : 2 * HEAD * h + 2 * HEAD, at] = dhid[mine]
        lin = nn(wtb, projected)
        e = jnp.exp(-jnp.abs(lin))
        soft = jnp.maximum(lin, 0.0) + jnp.log(1.0 + e)
        inv = 1.0 / (0.5 + soft)
        sig = jnp.where(lin >= 0, 1.0, e) / (1.0 + e)
        a = inv * (10.0 * LOG2E)
        live = jnp.where(j * CHUNK + iota((1, CHUNK), 1) < count, 1.0, 0.0)
        norms = []
        for g in range(2):
            x = nn(wsb[...], projected[128 * g : 128 * g + 128])
            for k in range(4):
                h = 4 * g + k
                t = jnp.tanh(x[SLICES * k : SLICES * k + SLICES] * 0.1)
                p = jnp.exp2(t * a[h : h + 1])
                r = live / jnp.sum(p, axis=0, keepdims=True)
                weights[SLICES * h : SLICES * h + SLICES, at] = (p * r).astype(BF16)
                norms.append(r)
        stats[0:8, at] = a
        stats[8:16, at] = inv
        stats[16:24, at] = inv * inv * sig * (-10.0)
        stats[24:32, at] = jnp.concatenate(norms, axis=0)
        return carry

    lax.fori_loop(0, rows // CHUNK, chunk, 0)
    ones = jnp.ones((16, rows), BF16)
    first = iota((64, 128), 1) < SLICES
    blocks, sums = [], []
    for q in range(4):
        mine = slice(128 * q, 128 * q + 128)
        out = nt(jnp.concatenate([fd[mine, :], ones], axis=0), weights[mine, :])
        blocks.append(jnp.where(first, out[0:64], out[64:128]))
        sums.append(out[128:129])
    zero = jnp.zeros((14, 128), F32)
    halves = [
        jnp.concatenate([blocks[2 * s], blocks[2 * s + 1], sums[2 * s], sums[2 * s + 1], zero], 0)
        for s in range(2)
    ]
    keep[...] = jnp.where(core == 0, halves[0], halves[1])
    send[...] = jnp.where(core == 0, halves[1], halves[0])


def spread_kernel(mine, other, out):
    total = (mine[...] + other[...]).astype(BF16)
    n = mine.shape[0]
    for k in range(out.shape[0] // n):
        out[n * k : n * k + n, :] = total


def sum_blocks(ref, n):
    total = ref[0:n, :].astype(F32)
    for k in range(1, ref.shape[0] // n):
        total = total + ref[n * k : n * k + n, :].astype(F32)
    return total


def mix_kernel(parts, w_qkv, out):
    total = sum_blocks(parts, ROWS1)
    numer = jnp.concatenate([total[0:32], total[64:96]], axis=1)
    d_mixed = jnp.concatenate([total[32:64], total[96:128]], axis=1)
    denom = jnp.concatenate([total[128:129], total[129:130]], axis=1) + 1e-05
    inverse = 1.0 / denom
    tokens = numer * inverse
    maps = [w_qkv[k].astype(F32) for k in range(3)]
    q, key, val = [nn(m.T, tokens, HIGHEST) for m in maps]
    key_rows, val_rows = key.T, val.T
    scores = nn(key_rows, q, HIGHEST) * (1.0 / math.sqrt(HEAD))
    same = iota((256, 256), 0) // SLICES == iota((256, 256), 1) // SLICES
    t = jnp.tanh(scores * 0.1)
    powers = jnp.where(same, jnp.exp2(t * (10.0 * LOG2E)), 0.0)
    att = powers * (1.0 / jnp.sum(powers, axis=0, keepdims=True))
    mixed = nn(val, att, HIGHEST)
    d_att = nn(val_rows, d_mixed, HIGHEST)
    d_val = nt(d_mixed, att, HIGHEST)
    inner = jnp.sum(att * d_att, axis=0, keepdims=True)
    d_scores = att * (d_att - inner) * ((1.0 - t * t) * (1.0 / math.sqrt(HEAD)))
    d_q = nn(key, d_scores, HIGHEST)
    d_key = nt(q, d_scores, HIGHEST)
    grads = (d_q, d_key, d_val)
    d_tokens = sum(nn(m, g, HIGHEST) for m, g in zip(maps, grads))
    d_numer = d_tokens * inverse
    d_denom = -jnp.sum(d_numer * tokens, axis=0, keepdims=True)
    out[0:32, :] = d_numer.astype(BF16).astype(F32)
    out[32:64, :] = mixed.astype(BF16).astype(F32)
    out[64:72, :] = jnp.broadcast_to(d_denom, (8, 256))
    for k in range(3):
        out[72 + 32 * k : 104 + 32 * k, 0:32] = nt(tokens, grads[k], HIGHEST)
        out[72 + 32 * k : 104 + 32 * k, 32:256] = jnp.zeros((32, 224), F32)


def backward_kernel(
    scale,
    cells, cot, weights, proj, fd, stats, mine, other, w_slice, w_temp,
    hid, dpf, keep, send, grad_qkv,
    dlog, dtemp, lhs_h, lhs_w, dden, wsb, wsd,
):
    core = lax.rem(lax.axis_index("dom"), 2)
    rows = cells.shape[0]
    lower = core == 0
    blocks = slice_blocks(w_slice[...])
    wsd[...] = blocks.astype(BF16)
    wsb[...] = blocks.T.astype(BF16)
    wtb = temp_blocks(w_temp[...]).astype(F32).T
    diag64 = iota((256, 256), 0) // 64 == iota((256, 256), 1) // 64
    diag32 = iota((128, 256), 0) // 32 == iota((128, 256), 1) // 64
    for g in range(2):
        e = jnp.where(lower == (g == 0), mine[0:72, :], other[0:72, :])
        both = jnp.where(diag64, jnp.concatenate([e[0:64]] * 4, axis=0), 0.0)
        lhs_w[g] = both.T.astype(BF16)
        lhs_h[g, 0:128, :] = jnp.where(
            diag32, jnp.concatenate([e[32:64]] * 4, axis=0), 0.0
        ).astype(BF16)
        lhs_h[g, 128:256, :] = jnp.where(
            diag32, jnp.concatenate([e[0:32]] * 4, axis=0), 0.0
        ).astype(BF16)
        column = e[64:72].T[:, 0:1]
        dden[256 * g : 256 * g + 256, :] = jnp.broadcast_to(column, (256, CHUNK))
    for k in range(3):
        block = slice(72 + 32 * k, 104 + 32 * k)
        grad_qkv[k] = (mine[block, 0:32] + other[block, 0:32]) * scale

    def chunk(j, carry):
        at = pl.ds(pl.multiple_of(j * CHUNK, CHUNK), CHUNK)
        a = stats[0:8, at]
        inv = stats[8:16, at]
        slope = stats[16:24, at]
        norm = stats[24:32, at]
        for g in range(2):
            half = slice(128 * g, 128 * g + 128)
            wide = slice(256 * g, 256 * g + 256)
            hf = nn(lhs_h[g], weights[wide, at])
            hid[half, at] = hf[0:128].astype(BF16)
            dpf[WIDTH + 128 * g : WIDTH + 128 * g + 128, at] = hf[128:256].astype(BF16)
            dw = nn(lhs_w[g], fd[wide, at])
            x = nn(wsb[...], proj[half, at])
            outer = []
            for k in range(4):
                h = 4 * g + k
                sub = slice(SLICES * k, SLICES * k + SLICES)
                rng = slice(SLICES * h, SLICES * h + SLICES)
                one = slice(h, h + 1)
                t = jnp.tanh(x[sub] * 0.1)
                soft = jnp.exp2(t * a[one]) * norm[one]
                d = dw[sub] + dden[rng, :]
                inner = jnp.sum(soft * d, axis=0, keepdims=True)
                ds = soft * (d - inner)
                dlog[rng, at] = (ds * ((1.0 - t * t) * inv[one])).astype(BF16)
                dt = jnp.sum(ds * t, axis=0, keepdims=True) * slope[one]
                dt = dt.astype(BF16).astype(F32)
                dtemp[one, at] = dt
                outer.append(wtb[HEAD * h : HEAD * h + HEAD, h : h + 1] * dt)
            dp = nn(wsd[...], dlog[wide, at]) + jnp.concatenate(outer, axis=0)
            dpf[half, at] = dp.astype(BF16)
        return carry

    lax.fori_loop(0, rows // CHUNK, chunk, 0)
    d_out = nn(hid[...], cot[...])
    d_in = nn(dpf[...], cells[...])
    d_x = d_in[0:WIDTH].T
    d_fx = d_in[WIDTH : 2 * WIDTH].T
    even = jnp.zeros((HEAD, 128), F32)
    odd = jnp.zeros((HEAD, 128), F32)
    for q in range(4):
        pair = dlog[128 * q : 128 * q + 128, :]
        even = even + nt(proj[64 * q : 64 * q + 32, :], pair)
        odd = odd + nt(proj[64 * q + 32 : 64 * q + 64, :], pair)
    d_slice = jnp.where(iota((HEAD, 128), 1) < SLICES, even, odd)
    d_slice = jnp.concatenate([d_slice[0:16], d_slice[16:32]], axis=1)
    d_temp = nt(dtemp[...].astype(BF16), proj[...])
    own = iota((HEADS, WIDTH), 0) == iota((HEADS, WIDTH), 1) // HEAD
    d_temp = jnp.where(own, d_temp, 0.0)
    d_temp = jnp.broadcast_to(jnp.sum(d_temp, axis=0, keepdims=True), (HEADS, WIDTH))
    for ref, first in ((keep, lower), (send, jnp.logical_not(lower))):
        for i, grad in enumerate((d_out, d_x, d_fx)):
            ref[128 * i : 128 * i + 128, :] = jnp.where(first, grad[0:128], grad[128:256]).astype(
                BF16
            )
        ref[384:400, :] = jnp.concatenate(
            [jnp.where(first, d_slice[0:8], d_slice[8:16]), d_temp], axis=0
        ).astype(BF16)
        ref[400:, :] = jnp.zeros((ref.shape[0] - 400, WIDTH), BF16)


def write_rows(out, stage, sems, product):
    copies = []
    for j in range(out.shape[0] // CHUNK):
        at = pl.ds(j * CHUNK, CHUNK)
        stage[at, :] = product(at).T.astype(BF16)
        copies.append(pltpu.make_async_copy(stage.at[at, :], out.at[at, :], sems.at[j]))
        copies[-1].start()
    for copy in copies:
        copy.wait()


def result_kernel(hid, w_out, out, stage, sems):
    table = w_out[...].T
    write_rows(out, stage, sems, lambda at: nn(table, hid[:, at]))


def grad_cells_kernel(dpf, w_x, w_fx, out, stage, sems):
    write_rows(
        out,
        stage,
        sems,
        lambda at: nn(w_x[...], dpf[0:WIDTH, at]) + nn(w_fx[...], dpf[WIDTH : 2 * WIDTH, at]),
    )


def add_kernel(mine, other, out):
    out[...] = (mine[...].astype(F32) + other[...].astype(F32)).astype(BF16)


def place_kernel(mine, other, d_x, d_fx, d_slice, d_temp, d_out):
    core = lax.rem(lax.axis_index("dom"), 2)
    lower = core == 0
    small = []
    for s in range(2):
        src = jnp.where(lower == (s == 0), mine[0:400, :], other[0:400, :]).astype(F32)
        for i, ref in enumerate((d_out, d_x, d_fx)):
            ref[128 * s : 128 * s + 128, :] = src[128 * i : 128 * i + 128]
        small.append(src[384:392])
        if s == 0:
            v = src[392:400]
            v = v[:, 0:128] + v[:, 128:256]
            v = v + pltpu.roll(v, 64, 1)
            v = v + pltpu.roll(v, 32, 1)
            d_temp[...] = v[0:1, 0:32]
    rows = jnp.concatenate(
        [small[0][:, 0:128], small[1][:, 0:128], small[0][:, 128:256], small[1][:, 128:256]], axis=0
    )
    rows = rows + pltpu.roll(rows, 64, 1)
    d_slice[...] = rows[:, 0:SLICES]


VMEM = pl.BlockSpec(memory_space=pltpu.VMEM)
SMEM = pl.BlockSpec(memory_space=pltpu.SMEM)
HBM = pl.BlockSpec(memory_space=pltpu.HBM)


def call(kernel, shapes, args, scratch=(), name=None, ins=None, outs=None, flops=0):
    scratch = [pltpu.VMEM(*s) if isinstance(s, tuple) else s for s in scratch]
    estimate = pl.CostEstimate(flops=flops, bytes_accessed=0, transcendentals=0)
    return pl.pallas_call(
        kernel,
        out_shape=[jax.ShapeDtypeStruct(s, d) for s, d in shapes],
        in_specs=ins or [VMEM] * len(args),
        out_specs=outs or [VMEM] * len(shapes),
        scratch_shapes=scratch,
        name=name,
        cost_estimate=estimate if flops else None,
        compiler_params=pltpu.CompilerParams(vmem_limit_bytes=24 << 20),
    )(*args)


def body(devices, cells, counts, w_x, w_fx, w_slice, w_temp, w_qkv, w_out, cotangent):
    rows = cells.shape[0]
    peers = devices // 2
    pairs = [(i, i ^ 1) for i in range(devices)]
    groups = [list(range(c, devices, 2)) for c in range(2)]
    scale = 1.0 / math.sqrt(rows * devices)
    temp = w_temp.reshape(1, HEAD)
    hm = HEADS * SLICES

    def exchange(x):
        return lax.all_to_all(x, "dom", 0, 0, axis_index_groups=groups, tiled=True)

    weights, proj, fd, stats, keep, send = call(
        forward_kernel,
        [
            ((hm, rows), BF16),
            ((WIDTH, rows), BF16),
            ((2 * WIDTH, rows), BF16),
            ((32, rows), F32),
            ((ROWS1, 128), F32),
            ((ROWS1, 128), F32),
        ],
        (counts,)
        + tuple(
            pltpu.with_memory_space_constraint(x, pltpu.HBM)
            for x in (cells, cotangent, w_x, w_fx, w_slice, temp, w_out)
        ),
        scratch=[
            ((rows, WIDTH), BF16),
            ((rows, WIDTH), BF16),
            ((WIDTH, WIDTH), BF16),
            ((WIDTH, WIDTH), BF16),
            ((HEAD, SLICES), BF16),
            ((1, HEAD), BF16),
            ((WIDTH, WIDTH), BF16),
            pltpu.SemaphoreType.DMA((5,)),
            pltpu.SemaphoreType.DMA((2, rows // CHUNK)),
            ((256, 256), BF16),
            ((256, 256), BF16),
            ((256, 128), BF16),
        ],
        ins=[SMEM] + [HBM] * 7,
        name="forward",
    )
    other = lax.ppermute(send, "dom", pairs)
    (spread,) = call(
        spread_kernel, [((peers * ROWS1, 128), BF16)], (keep, other), name="spread"
    )
    parts = exchange(spread)
    (mine,) = call(mix_kernel, [((168, 256), F32)], (parts, w_qkv), name="mix")
    other = lax.ppermute(mine, "dom", pairs)
    chunk = -(-400 // peers)
    chunk = -(-chunk // 8) * 8
    half = chunk * peers
    hid, dpf, keep, send, grad_qkv = call(
        functools.partial(backward_kernel, scale),
        [
            ((WIDTH, rows), BF16),
            ((2 * WIDTH, rows), BF16),
            ((half, WIDTH), BF16),
            ((half, WIDTH), BF16),
            ((3, HEAD, HEAD), F32),
        ],
        (cells, cotangent, weights, proj, fd, stats, mine, other, w_slice, temp),
        scratch=[
            ((hm, rows), BF16),
            ((8, rows), F32),
            ((2, 256, 256), BF16),
            ((2, 256, 256), BF16),
            ((hm, CHUNK), F32),
            ((256, 128), BF16),
            ((128, 256), BF16),
        ],
        name="backward",
    )
    other = lax.ppermute(send, "dom", pairs)
    staging = [((rows, WIDTH), BF16), pltpu.SemaphoreType.DMA((rows // CHUNK,))]
    (result,) = call(
        result_kernel,
        [((rows, WIDTH), BF16)],
        (hid, w_out),
        scratch=staging,
        outs=[HBM],
        name="result",
        flops=2 * rows * WIDTH * WIDTH,
    )
    other, result = lax.optimization_barrier((other, result))
    (grad_cells,) = call(
        grad_cells_kernel,
        [((rows, WIDTH), BF16)],
        (dpf, w_x, w_fx),
        scratch=staging,
        outs=[HBM],
        name="grad_cells",
        flops=4 * rows * WIDTH * WIDTH,
    )
    (summed,) = call(add_kernel, [((half, WIDTH), BF16)], (keep, other), name="pair_add")
    parts = exchange(summed)

    def gather(parts_ref, out):
        total = (sum_blocks(parts_ref, chunk) * scale).astype(BF16)
        for k in range(peers):
            out[chunk * k : chunk * k + chunk, :] = total

    (spread,) = call(gather, [((half, WIDTH), BF16)], (parts,), name="gather")
    mine = exchange(spread)
    other = lax.ppermute(mine, "dom", pairs)
    d_x, d_fx, d_slice, d_temp, d_out = call(
        place_kernel,
        [
            ((WIDTH, WIDTH), F32),
            ((WIDTH, WIDTH), F32),
            ((HEAD, SLICES), F32),
            ((1, HEAD), F32),
            ((WIDTH, WIDTH), F32),
        ],
        (mine, other),
        name="place",
    )
    return result, grad_cells, d_x, d_fx, d_slice, d_temp.reshape(HEAD), grad_qkv, d_out


def solution(mesh):
    cell = P(("groups", "dom"), None)
    return jax.shard_map(
        functools.partial(body, mesh.shape["dom"]),
        mesh=mesh,
        in_specs=(cell, P(("groups", "dom")), P(), P(), P(), P(), P(), P(), cell),
        out_specs=(
            cell,
            cell,
            P("groups", None),
            P("groups", None),
            P("groups", None),
            P("groups"),
            P("groups", None, None),
            P("groups", None),
        ),
        check_vma=False,
    )
```

```python
import functools
import math

import jax
import jax.numpy as jnp
from jax import lax
from jax.experimental import pallas as pl
from jax.experimental.pallas import tpu as pltpu
from jax.sharding import PartitionSpec as P

F32 = jnp.float32
BF16 = jnp.bfloat16
HIGHEST = lax.Precision.HIGHEST
HEADS = 8
SLICES = 64
HEAD = 32
WIDTH = HEADS * HEAD
ROWS1 = 144
LOG2E = math.log2(math.e)
CHUNK = 512


def nn(a, b, precision=None):
    return lax.dot_general(
        a, b, (((1,), (0,)), ((), ())), precision=precision, preferred_element_type=F32
    )


def nt(a, b, precision=None):
    return lax.dot_general(
        a, b, (((1,), (1,)), ((), ())), precision=precision, preferred_element_type=F32
    )


def iota(shape, dim):
    return lax.broadcasted_iota(jnp.int32, shape, dim)


def slice_blocks(w_slice):
    tall = jnp.concatenate([w_slice] * 4, axis=0)
    pick = (iota((SLICES, 256), 1) % SLICES == iota((SLICES, 256), 0)).astype(BF16)
    wide = nn(tall, pick)
    same = iota((128, 256), 0) // HEAD == iota((128, 256), 1) // SLICES
    return jnp.where(same, wide, 0.0)


def temp_blocks(w_temp):
    pick = (iota((HEAD, WIDTH), 1) % HEAD == iota((HEAD, WIDTH), 0)).astype(BF16)
    wide = nn(jnp.broadcast_to(w_temp, (HEADS, HEAD)), pick)
    same = iota((HEADS, WIDTH), 0) == iota((HEADS, WIDTH), 1) // HEAD
    return jnp.where(same, wide, 0.0).astype(BF16)


def forward_kernel(
    counts, cells_hbm, cot_hbm, *refs,
):
    hbm, refs = refs[:5], refs[5:]
    (weights, proj, fd, stats, keep, send, wsb, wsd, wtc), refs = refs[:9], refs[9:]
    cells, cot, w_x, w_fx, w_out, w_slice, w_temp, small, big, wxt, wft = refs
    core = lax.rem(lax.axis_index("dom"), 2)
    rows = cells.shape[0]
    steps = rows // CHUNK

    def load(source, target, slot, j):
        at = pl.ds(pl.multiple_of(j * CHUNK, CHUNK), CHUNK)
        return pltpu.make_async_copy(source.at[at, :], target.at[at, :], big.at[slot, j])

    tables = [
        pltpu.make_async_copy(source, target, small.at[i])
        for i, (source, target) in enumerate(zip(hbm, (w_x, w_fx, w_slice, w_temp, w_out)))
    ]
    for table in tables:
        table.start()
    for j in range(steps):
        load(cells_hbm, cells, 0, j).start()
        load(cot_hbm, cot, 1, j).start()
    for table in tables:
        table.wait()
    wtb = temp_blocks(w_temp[...])
    wxt[...] = w_x[...].T
    wft[...] = w_fx[...].T
    slices = slice_blocks(w_slice[...])
    wsd[...] = slices.astype(BF16)
    wsb[...] = slices.T.astype(BF16)
    wtc[...] = wtb.astype(F32).T
    count = counts[0]

    def chunk(j, carry):
        at = pl.ds(pl.multiple_of(j * CHUNK, CHUNK), CHUNK)
        load(cells_hbm, cells, 0, j).wait()
        load(cot_hbm, cot, 1, j).wait()
        c = cells[at, :]
        projected = nt(wxt[...], c).astype(BF16)
        proj[:, at] = projected
        feat = nt(wft[...], c).astype(BF16)
        dhid = nt(w_out[...], cot[at, :]).astype(BF16)
        for h in range(HEADS):
            mine = slice(HEAD * h, HEAD * h + HEAD)
            fd[2 * HEAD * h : 2 * HEAD * h + HEAD, at] = feat[mine]
            fd[2 * HEAD * h + HEAD : 2 * HEAD * h + 2 * HEAD, at] = dhid[mine]
        lin = nn(wtb, projected)
        e = jnp.exp(-jnp.abs(lin))
        soft = jnp.maximum(lin, 0.0) + jnp.log(1.0 + e)
        inv = 1.0 / (0.5 + soft)
        sig = jnp.where(lin >= 0, 1.0, e) / (1.0 + e)
        a = inv * (10.0 * LOG2E)
        live = jnp.where(j * CHUNK + iota((1, CHUNK), 1) < count, 1.0, 0.0)
        norms = []
        for g in range(2):
            x = nn(wsb[...], projected[128 * g : 128 * g + 128])
            for k in range(4):
                h = 4 * g + k
                t = jnp.tanh(x[SLICES * k : SLICES * k + SLICES] * 0.1)
                p = jnp.exp2(t * a[h : h + 1])
                r = live / jnp.sum(p, axis=0, keepdims=True)
                weights[SLICES * h : SLICES * h + SLICES, at] = (p * r).astype(BF16)
                norms.append(r)
        stats[0:8, at] = a
        stats[8:16, at] = inv
        stats[16:24, at] = inv * inv * sig * (-10.0)
        stats[24:32, at] = jnp.concatenate(norms, axis=0)
        return carry

    lax.fori_loop(0, rows // CHUNK, chunk, 0)
    ones = jnp.ones((16, rows), BF16)
    first = iota((64, 128), 1) < SLICES
    blocks, sums = [], []
    for q in range(4):
        mine = slice(128 * q, 128 * q + 128)
        out = nt(jnp.concatenate([fd[mine, :], ones], axis=0), weights[mine, :])
        blocks.append(jnp.where(first, out[0:64], out[64:128]))
        sums.append(out[128:129])
    zero = jnp.zeros((14, 128), F32)
    halves = [
        jnp.concatenate([blocks[2 * s], blocks[2 * s + 1], sums[2 * s], sums[2 * s + 1], zero], 0)
        for s in range(2)
    ]
    keep[...] = jnp.where(core == 0, halves[0], halves[1])
    send[...] = jnp.where(core == 0, halves[1], halves[0])


def narrow_add_kernel(mine, other, out):
    out[...] = (mine[...].astype(F32) + other[...].astype(F32)).astype(BF16)


def softmax_kernel(proj, stats, wsb, tanhs, soft):
    def chunk(j, carry):
        at = pl.ds(pl.multiple_of(j * CHUNK, CHUNK), CHUNK)
        a = stats[0:8, at]
        norm = stats[24:32, at]
        for g in range(2):
            x = nn(wsb[...], proj[128 * g : 128 * g + 128, at])
            for k in range(4):
                h = 4 * g + k
                rng = slice(SLICES * h, SLICES * h + SLICES)
                t = jnp.tanh(x[SLICES * k : SLICES * k + SLICES] * 0.1)
                tanhs[rng, at] = t
                soft[rng, at] = jnp.exp2(t * a[h : h + 1]) * norm[h : h + 1]
        return carry

    lax.fori_loop(0, proj.shape[1] // CHUNK, chunk, 0)


def sum_blocks(ref, n):
    total = ref[0:n, :].astype(F32)
    for k in range(1, ref.shape[0] // n):
        total = total + ref[n * k : n * k + n, :].astype(F32)
    return total


def mix_kernel(w_qkv, *refs):
    parts, out = refs[:-1], refs[-1]
    total = sum(part[...].astype(F32) for part in parts)
    numer = jnp.concatenate([total[0:32], total[64:96]], axis=1)
    d_mixed = jnp.concatenate([total[32:64], total[96:128]], axis=1)
    denom = jnp.concatenate([total[128:129], total[129:130]], axis=1) + 1e-05
    inverse = 1.0 / denom
    tokens = numer * inverse
    maps = [w_qkv[k].astype(F32) for k in range(3)]
    q, key, val = [nn(m.T, tokens, HIGHEST) for m in maps]
    key_rows, val_rows = key.T, val.T
    scores = nn(key_rows, q, HIGHEST) * (1.0 / math.sqrt(HEAD))
    same = iota((256, 256), 0) // SLICES == iota((256, 256), 1) // SLICES
    t = jnp.tanh(scores * 0.1)
    powers = jnp.where(same, jnp.exp2(t * (10.0 * LOG2E)), 0.0)
    att = powers * (1.0 / jnp.sum(powers, axis=0, keepdims=True))
    mixed = nn(val, att, HIGHEST)
    d_att = nn(val_rows, d_mixed, HIGHEST)
    d_val = nt(d_mixed, att, HIGHEST)
    inner = jnp.sum(att * d_att, axis=0, keepdims=True)
    d_scores = att * (d_att - inner) * ((1.0 - t * t) * (1.0 / math.sqrt(HEAD)))
    d_q = nn(key, d_scores, HIGHEST)
    d_key = nt(q, d_scores, HIGHEST)
    grads = (d_q, d_key, d_val)
    d_tokens = sum(nn(m, g, HIGHEST) for m, g in zip(maps, grads))
    d_numer = d_tokens * inverse
    d_denom = -jnp.sum(d_numer * tokens, axis=0, keepdims=True)
    out[0:32, :] = d_numer.astype(BF16).astype(F32)
    out[32:64, :] = mixed.astype(BF16).astype(F32)
    out[64:72, :] = jnp.broadcast_to(d_denom, (8, 256))
    for k in range(3):
        out[72:104, 32 * k : 32 * k + 32] = nt(tokens, grads[k], HIGHEST)
    out[72:104, 96:256] = jnp.zeros((32, 160), F32)


def backward_kernel(
    scale,
    cells, cot, weights, proj, fd, stats, tanhs, softs, mine, other, wsd, wtc,
    hid, dpf, keep, send, grad_qkv,
    dlog, dtemp, lhs_h, lhs_w, dden,
):
    core = lax.rem(lax.axis_index("dom"), 2)
    rows = cells.shape[0]
    lower = core == 0
    diag64 = iota((256, 256), 0) // 64 == iota((256, 256), 1) // 64
    diag32 = iota((128, 256), 0) // 32 == iota((128, 256), 1) // 64
    for g in range(2):
        e = jnp.where(lower == (g == 0), mine[0:72, :], other[0:72, :])
        both = jnp.where(diag64, jnp.concatenate([e[0:64]] * 4, axis=0), 0.0)
        lhs_w[g] = both.T.astype(BF16)
        lhs_h[g, 0:128, :] = jnp.where(
            diag32, jnp.concatenate([e[32:64]] * 4, axis=0), 0.0
        ).astype(BF16)
        lhs_h[g, 128:256, :] = jnp.where(
            diag32, jnp.concatenate([e[0:32]] * 4, axis=0), 0.0
        ).astype(BF16)
        column = e[64:72].T[:, 0:1]
        dden[256 * g : 256 * g + 256, :] = jnp.broadcast_to(column, (256, CHUNK))
    for k in range(3):
        block = slice(32 * k, 32 * k + 32)
        grad_qkv[k] = (mine[72:104, block] + other[72:104, block]) * scale

    def chunk(j, carry):
        at = pl.ds(pl.multiple_of(j * CHUNK, CHUNK), CHUNK)
        inv = stats[8:16, at]
        slope = stats[16:24, at]
        for g in range(2):
            half = slice(128 * g, 128 * g + 128)
            wide = slice(256 * g, 256 * g + 256)
            hf = nn(lhs_h[g], weights[wide, at])
            hid[half, at] = hf[0:128].astype(BF16)
            dpf[WIDTH + 128 * g : WIDTH + 128 * g + 128, at] = hf[128:256].astype(BF16)
            dw = nn(lhs_w[g], fd[wide, at])
            outer = []
            for k in range(4):
                h = 4 * g + k
                sub = slice(SLICES * k, SLICES * k + SLICES)
                rng = slice(SLICES * h, SLICES * h + SLICES)
                one = slice(h, h + 1)
                t = tanhs[rng, at]
                soft = softs[rng, at]
                d = dw[sub] + dden[rng, :]
                inner = jnp.sum(soft * d, axis=0, keepdims=True)
                ds = soft * (d - inner)
                dlog[rng, at] = (ds * ((1.0 - t * t) * inv[one])).astype(BF16)
                dt = jnp.sum(ds * t, axis=0, keepdims=True) * slope[one]
                dt = dt.astype(BF16).astype(F32)
                dtemp[one, at] = dt
                outer.append(wtc[HEAD * h : HEAD * h + HEAD, h : h + 1] * dt)
            dp = nn(wsd[...], dlog[wide, at]) + jnp.concatenate(outer, axis=0)
            dpf[half, at] = dp.astype(BF16)
        return carry

    lax.fori_loop(0, rows // CHUNK, chunk, 0)
    d_out = nn(hid[...], cot[...])
    d_in = nn(dpf[...], cells[...])
    d_x = d_in[0:WIDTH].T
    d_fx = d_in[WIDTH : 2 * WIDTH].T
    even = jnp.zeros((HEAD, 128), F32)
    odd = jnp.zeros((HEAD, 128), F32)
    for q in range(4):
        pair = dlog[128 * q : 128 * q + 128, :]
        even = even + nt(proj[64 * q : 64 * q + 32, :], pair)
        odd = odd + nt(proj[64 * q + 32 : 64 * q + 64, :], pair)
    d_slice = jnp.where(iota((HEAD, 128), 1) < SLICES, even, odd)
    d_slice = jnp.concatenate([d_slice[0:16], d_slice[16:32]], axis=1)
    d_temp = nt(dtemp[...].astype(BF16), proj[...])
    own = iota((HEADS, WIDTH), 0) == iota((HEADS, WIDTH), 1) // HEAD
    d_temp = jnp.where(own, d_temp, 0.0)
    d_temp = jnp.broadcast_to(jnp.sum(d_temp, axis=0, keepdims=True), (HEADS, WIDTH))
    for ref, first in ((keep, lower), (send, jnp.logical_not(lower))):
        for i, grad in enumerate((d_out, d_x, d_fx)):
            ref[128 * i : 128 * i + 128, :] = jnp.where(first, grad[0:128], grad[128:256]).astype(
                BF16
            )
        ref[384:400, :] = jnp.concatenate(
            [jnp.where(first, d_slice[0:8], d_slice[8:16]), d_temp], axis=0
        ).astype(BF16)
        ref[400:, :] = jnp.zeros((ref.shape[0] - 400, WIDTH), BF16)


def write_rows(out, stage, sems, product):
    copies = []
    for j in range(out.shape[0] // CHUNK):
        at = pl.ds(j * CHUNK, CHUNK)
        stage[at, :] = product(at).T.astype(BF16)
        copies.append(pltpu.make_async_copy(stage.at[at, :], out.at[at, :], sems.at[j]))
        copies[-1].start()
    for copy in copies:
        copy.wait()


def result_kernel(hid, w_out, out, stage, sems):
    table = w_out[...].T
    write_rows(out, stage, sems, lambda at: nn(table, hid[:, at]))


def grad_cells_kernel(dpf, w_x, w_fx, out, stage, sems):
    write_rows(
        out,
        stage,
        sems,
        lambda at: nn(w_x[...], dpf[0:WIDTH, at]) + nn(w_fx[...], dpf[WIDTH : 2 * WIDTH, at]),
    )


def place_kernel(mine, other, d_x, d_fx, d_slice, d_temp, d_out):
    core = lax.rem(lax.axis_index("dom"), 2)
    lower = core == 0
    small = []
    for s in range(2):
        src = jnp.where(lower == (s == 0), mine[0:400, :], other[0:400, :]).astype(F32)
        for i, ref in enumerate((d_out, d_x, d_fx)):
            ref[128 * s : 128 * s + 128, :] = src[128 * i : 128 * i + 128]
        small.append(src[384:392])
        if s == 0:
            v = src[392:400]
            v = v[:, 0:128] + v[:, 128:256]
            v = v + pltpu.roll(v, 64, 1)
            v = v + pltpu.roll(v, 32, 1)
            d_temp[...] = v[0:1, 0:32]
    rows = jnp.concatenate(
        [small[0][:, 0:128], small[1][:, 0:128], small[0][:, 128:256], small[1][:, 128:256]], axis=0
    )
    rows = rows + pltpu.roll(rows, 64, 1)
    d_slice[...] = rows[:, 0:SLICES]


VMEM = pl.BlockSpec(memory_space=pltpu.VMEM)
SMEM = pl.BlockSpec(memory_space=pltpu.SMEM)
HBM = pl.BlockSpec(memory_space=pltpu.HBM)


def call(kernel, shapes, args, scratch=(), name=None, ins=None, outs=None, flops=0):
    scratch = [pltpu.VMEM(*s) if isinstance(s, tuple) else s for s in scratch]
    estimate = pl.CostEstimate(flops=flops, bytes_accessed=0, transcendentals=0)
    return pl.pallas_call(
        kernel,
        out_shape=[jax.ShapeDtypeStruct(s, d) for s, d in shapes],
        in_specs=ins or [VMEM] * len(args),
        out_specs=outs or [VMEM] * len(shapes),
        scratch_shapes=scratch,
        name=name,
        cost_estimate=estimate if flops else None,
        compiler_params=pltpu.CompilerParams(vmem_limit_bytes=24 << 20),
    )(*args)


def body(devices, cells, counts, w_x, w_fx, w_slice, w_temp, w_qkv, w_out, cotangent):
    rows = cells.shape[0]
    peers = devices // 2
    groups = [list(range(c, devices, 2)) for c in range(2)]
    scale = 1.0 / math.sqrt(rows * devices)
    temp = w_temp.reshape(1, HEAD)
    hm = HEADS * SLICES

    def swap(x, mask):
        return lax.ppermute(x, "dom", [(i, i ^ mask) for i in range(devices)])

    def exchange(x):
        return lax.all_to_all(x, "dom", 0, 0, axis_index_groups=groups, tiled=True)

    local = call(
        forward_kernel,
        [
            ((hm, rows), BF16),
            ((WIDTH, rows), BF16),
            ((2 * WIDTH, rows), BF16),
            ((32, rows), F32),
            ((ROWS1, 128), F32),
            ((ROWS1, 128), F32),
            ((256, 128), BF16),
            ((128, 256), BF16),
            ((WIDTH, HEADS), F32),
            ((rows, WIDTH), BF16),
            ((rows, WIDTH), BF16),
            ((WIDTH, WIDTH), BF16),
            ((WIDTH, WIDTH), BF16),
            ((WIDTH, WIDTH), BF16),
        ],
        (counts,)
        + tuple(
            pltpu.with_memory_space_constraint(x, pltpu.HBM)
            for x in (cells, cotangent, w_x, w_fx, w_slice, temp, w_out)
        ),
        scratch=[
            ((HEAD, SLICES), BF16),
            ((1, HEAD), BF16),
            pltpu.SemaphoreType.DMA((5,)),
            pltpu.SemaphoreType.DMA((2, rows // CHUNK)),
            ((256, 256), BF16),
            ((256, 256), BF16),
        ],
        ins=[SMEM] + [HBM] * 7,
        name="forward",
    )
    weights, proj, fd, stats, keep, send, wsb, wsd, wtc = local[:9]
    cells, cotangent, w_x, w_fx, w_out = local[9:]
    other = swap(send, 1)
    part = ((ROWS1, 128), BF16)
    (total,) = call(narrow_add_kernel, [part], (keep, other), name="narrow")
    near = [2**b for b in range(1, devices.bit_length() - 3)]
    far = [devices // 4 * k for k in (1, 2, 3)]
    tanhs = softs = None
    for mask in near:
        other = swap(total, mask)
        if tanhs is None:
            tanhs, softs = call(
                softmax_kernel,
                [((hm, rows), F32)] * 2,
                (proj, stats, wsb),
                name="softmax",
                flops=2 * rows * hm * 128,
            )
            other, tanhs, softs = lax.optimization_barrier((other, tanhs, softs))
        (total,) = call(narrow_add_kernel, [part], (total, other), name="near")
    parts = [total] + [swap(total, mask) for mask in far]
    (mine,) = call(mix_kernel, [((104, 256), F32)], (w_qkv, *parts), name="mix")
    other = swap(mine, 1)
    chunk = -(-400 // peers)
    chunk = -(-chunk // 8) * 8
    half = chunk * peers
    hid, dpf, keep, send, grad_qkv = call(
        functools.partial(backward_kernel, scale),
        [
            ((WIDTH, rows), BF16),
            ((2 * WIDTH, rows), BF16),
            ((half, WIDTH), BF16),
            ((half, WIDTH), BF16),
            ((3, HEAD, HEAD), F32),
        ],
        (cells, cotangent, weights, proj, fd, stats, tanhs, softs, mine, other, wsd, wtc),
        scratch=[
            ((hm, rows), BF16),
            ((8, rows), F32),
            ((2, 256, 256), BF16),
            ((2, 256, 256), BF16),
            ((hm, CHUNK), F32),
        ],
        name="backward",
    )
    other = swap(send, 1)
    staging = [((rows, WIDTH), BF16), pltpu.SemaphoreType.DMA((rows // CHUNK,))]
    (result,) = call(
        result_kernel,
        [((rows, WIDTH), BF16)],
        (hid, w_out),
        scratch=staging,
        outs=[HBM],
        name="result",
        flops=2 * rows * WIDTH * WIDTH,
    )
    other, result = lax.optimization_barrier((other, result))
    (grad_cells,) = call(
        grad_cells_kernel,
        [((rows, WIDTH), BF16)],
        (dpf, w_x, w_fx),
        scratch=staging,
        outs=[HBM],
        name="grad_cells",
        flops=4 * rows * WIDTH * WIDTH,
    )
    (summed,) = call(narrow_add_kernel, [((half, WIDTH), BF16)], (keep, other), name="pair_add")
    parts = exchange(summed)

    def gather(parts_ref, out):
        total = (sum_blocks(parts_ref, chunk) * scale).astype(BF16)
        for k in range(peers):
            out[chunk * k : chunk * k + chunk, :] = total

    (spread,) = call(gather, [((half, WIDTH), BF16)], (parts,), name="gather")
    mine = exchange(spread)
    other = swap(mine, 1)
    d_x, d_fx, d_slice, d_temp, d_out = call(
        place_kernel,
        [
            ((WIDTH, WIDTH), F32),
            ((WIDTH, WIDTH), F32),
            ((HEAD, SLICES), F32),
            ((1, HEAD), F32),
            ((WIDTH, WIDTH), F32),
        ],
        (mine, other),
        name="place",
    )
    return result, grad_cells, d_x, d_fx, d_slice, d_temp.reshape(HEAD), grad_qkv, d_out


def solution(mesh):
    cell = P(("groups", "dom"), None)
    return jax.shard_map(
        functools.partial(body, mesh.shape["dom"]),
        mesh=mesh,
        in_specs=(cell, P(("groups", "dom")), P(), P(), P(), P(), P(), P(), cell),
        out_specs=(
            cell,
            cell,
            P("groups", None),
            P("groups", None),
            P("groups", None),
            P("groups"),
            P("groups", None, None),
            P("groups", None),
        ),
        check_vma=False,
    )
```

```python
import functools
import math

import jax
import jax.numpy as jnp
from jax import lax
from jax.experimental import pallas as pl
from jax.experimental.pallas import tpu as pltpu
from jax.sharding import PartitionSpec as P

F32 = jnp.float32
BF16 = jnp.bfloat16
FINE = lax.Precision.HIGH
HEADS = 8
SLICES = 64
HEAD = 32
WIDTH = HEADS * HEAD
ROWS1 = 136
ROWS2 = 408
LOG2E = math.log2(math.e)
CHUNK = 1024
WRITE = 256


def nn(a, b, precision=None):
    return lax.dot_general(
        a, b, (((1,), (0,)), ((), ())), precision=precision, preferred_element_type=F32
    )


def nt(a, b, precision=None):
    return lax.dot_general(
        a, b, (((1,), (1,)), ((), ())), precision=precision, preferred_element_type=F32
    )


def iota(shape, dim):
    return lax.broadcasted_iota(jnp.int32, shape, dim)


def slice_blocks(w_slice):
    tall = jnp.concatenate([w_slice] * 4, axis=0)
    pick = (iota((SLICES, 256), 1) % SLICES == iota((SLICES, 256), 0)).astype(BF16)
    wide = nn(tall, pick)
    same = iota((128, 256), 0) // HEAD == iota((128, 256), 1) // SLICES
    return jnp.where(same, wide, 0.0)


def temp_blocks(w_temp):
    pick = (iota((HEAD, 128), 1) % HEAD == iota((HEAD, 128), 0)).astype(BF16)
    wide = nn(jnp.broadcast_to(w_temp, (HEADS, HEAD)), pick)
    same = iota((HEADS, 128), 0) == iota((HEADS, 128), 1) // HEAD
    return jnp.where(same, wide, 0.0).astype(BF16)


def group_rows(group):
    return pl.ds(pl.multiple_of(group * 128, 128), 128)


def chunk_of(j):
    return pl.ds(pl.multiple_of(j * CHUNK, CHUNK), CHUNK)


def forward_group(count, operands, outs, tab, group, wait):
    cells, cot, w_out, wxt, wft, wsb, wtb = operands
    weights, proj, fd, stats, payload = outs
    rows = cells.shape[0]
    mine = group_rows(group)
    tab[0:128, :] = wxt[mine, :]
    tab[128:256, :] = wft[mine, :]

    def chunk(j, carry):
        at = chunk_of(j)
        wait(j)
        both = nt(tab[...], cells[at, :]).astype(BF16)
        projected = both[0:128]
        proj[:, at] = projected
        dhid = nt(w_out[mine, :], cot[at, :]).astype(BF16)
        for k in range(4):
            fd[64 * k : 64 * k + 32, at] = both[128 + 32 * k : 160 + 32 * k]
            fd[64 * k + 32 : 64 * k + 64, at] = dhid[32 * k : 32 * k + 32]
        lin = nn(wtb[...], projected)
        e = jnp.exp(-jnp.abs(lin))
        soft = jnp.maximum(lin, 0.0) + jnp.log(1.0 + e)
        inv = 1.0 / (0.5 + soft)
        sig = jnp.where(lin >= 0, 1.0, e) / (1.0 + e)
        a = inv * (10.0 * LOG2E)
        live = jnp.where(j * CHUNK + iota((1, CHUNK), 1) < count, 1.0, 0.0)
        norms = []
        x = nn(wsb[...], projected)
        for k in range(4):
            t = jnp.tanh(x[SLICES * k : SLICES * k + SLICES] * 0.1)
            p = jnp.exp2(t * a[k : k + 1])
            r = live / jnp.sum(p, axis=0, keepdims=True)
            weights[SLICES * k : SLICES * k + SLICES, at] = (p * r).astype(BF16)
            norms.append(r)
        stats[0:8, at] = a
        stats[8:16, at] = inv
        stats[16:24, at] = inv * inv * sig * (-10.0)
        stats[24:32, at] = jnp.concatenate(norms + norms, axis=0)
        return carry

    lax.fori_loop(0, rows // CHUNK, chunk, 0)
    ones = jnp.ones((16, rows), BF16)
    first = iota((64, 128), 1) < SLICES
    for q in range(2):
        pair = slice(128 * q, 128 * q + 128)
        out = nt(jnp.concatenate([fd[pair, :], ones], axis=0), weights[pair, :])
        payload[64 * q : 64 * q + 64, :] = jnp.where(first, out[0:64], out[64:128])
        payload[128 + q : 129 + q, :] = out[128:129]
    payload[130:136, :] = jnp.zeros((6, 128), F32)


def forward_far_kernel(counts, cells_hbm, cot_hbm, *refs):
    hbm, refs = refs[:5], refs[5:]
    outs, refs = refs[:5], refs[5:]
    (wxt, wft, wsb, wsd, wtb, wtc, cells, cot, w_x, w_fx, w_out), refs = refs[:11], refs[11:]
    w_slice, w_temp, small, big, tab = refs
    core = lax.rem(lax.axis_index("dom"), 2)

    def load(source, target, slot, j):
        at = chunk_of(j)
        return pltpu.make_async_copy(source.at[at, :], target.at[at, :], big.at[slot, j])

    tables = [
        pltpu.make_async_copy(source, target, small.at[i])
        for i, (source, target) in enumerate(zip(hbm, (w_x, w_fx, w_slice, w_temp, w_out)))
    ]
    for table in tables:
        table.start()
    for j in range(cells.shape[0] // CHUNK):
        load(cells_hbm, cells, 0, j).start()
        load(cot_hbm, cot, 1, j).start()
    for table in tables:
        table.wait()
    blocks = temp_blocks(w_temp[...])
    wtb[...] = blocks
    wtc[...] = blocks.astype(F32).T
    wxt[...] = w_x[...].T
    wft[...] = w_fx[...].T
    slices = slice_blocks(w_slice[...])
    wsd[...] = slices.astype(BF16)
    wsb[...] = slices.T.astype(BF16)

    def wait(j):
        load(cells_hbm, cells, 0, j).wait()
        load(cot_hbm, cot, 1, j).wait()

    operands = (cells, cot, w_out, wxt, wft, wsb, wtb)
    forward_group(counts[0], operands, outs, tab, 1 - core, wait)


def forward_own_kernel(counts, *refs):
    core = lax.rem(lax.axis_index("dom"), 2)
    forward_group(counts[0], refs[:7], refs[7:12], refs[12], core, lambda j: None)


def narrow_add_kernel(mine, other, out):
    out[...] = (mine[...].astype(F32) + other[...].astype(F32)).astype(BF16)


def softmax_kernel(wsb, *refs):
    def chunk(j, carry):
        at = chunk_of(j)
        for g in range(2):
            proj, stats = refs[2 * g : 2 * g + 2]
            tanhs, soft = refs[4 + 2 * g : 6 + 2 * g]
            x = nn(wsb[...], proj[:, at])
            for k in range(4):
                rng = slice(SLICES * k, SLICES * k + SLICES)
                t = jnp.tanh(x[rng] * 0.1)
                tanhs[rng, at] = t
                soft[rng, at] = jnp.exp2(t * stats[k : k + 1, at]) * stats[24 + k : 25 + k, at]
        return carry

    lax.fori_loop(0, refs[0].shape[1] // CHUNK, chunk, 0)


def sum_blocks(ref, n):
    total = ref[0:n, :].astype(F32)
    for k in range(1, ref.shape[0] // n):
        total = total + ref[n * k : n * k + n, :].astype(F32)
    return total


def mix_kernel(w_qkv, *refs):
    parts, out = refs[:-1], refs[-1]
    total = sum(part[...].astype(F32) for part in parts)
    numer = jnp.concatenate([total[0:32], total[64:96]], axis=1)
    d_mixed = jnp.concatenate([total[32:64], total[96:128]], axis=1)
    denom = jnp.concatenate([total[128:129], total[129:130]], axis=1) + 1e-05
    inverse = 1.0 / denom
    tokens = numer * inverse
    maps = [w_qkv[k].astype(F32) for k in range(3)]
    q, key, val = [nn(m.T, tokens, FINE) for m in maps]
    key_rows, val_rows = key.T, val.T
    scores = nn(key_rows, q, FINE) * (1.0 / math.sqrt(HEAD))
    same = iota((256, 256), 0) // SLICES == iota((256, 256), 1) // SLICES
    t = jnp.tanh(scores * 0.1)
    powers = jnp.where(same, jnp.exp2(t * (10.0 * LOG2E)), 0.0)
    att = powers * (1.0 / jnp.sum(powers, axis=0, keepdims=True))
    mixed = nn(val, att, FINE)
    d_att = nn(val_rows, d_mixed, FINE)
    d_val = nt(d_mixed, att, FINE)
    inner = jnp.sum(att * d_att, axis=0, keepdims=True)
    d_scores = att * (d_att - inner) * ((1.0 - t * t) * (1.0 / math.sqrt(HEAD)))
    d_q = nn(key, d_scores, FINE)
    d_key = nt(q, d_scores, FINE)
    grads = (d_q, d_key, d_val)
    d_tokens = sum(nn(m, g, FINE) for m, g in zip(maps, grads))
    d_numer = d_tokens * inverse
    d_denom = -jnp.sum(d_numer * tokens, axis=0, keepdims=True)
    out[0:32, :] = d_numer.astype(BF16).astype(F32)
    out[32:64, :] = mixed.astype(BF16).astype(F32)
    out[64:72, :] = jnp.broadcast_to(d_denom, (8, 256))
    for k in range(3):
        out[72:104, 32 * k : 32 * k + 32] = nt(tokens, grads[k], FINE)
    out[72:104, 96:256] = jnp.zeros((32, 160), F32)


def backward_kernel(scale, cells, cot, wsd, wtc, weights, proj, fd, stats, tanhs, softs, *refs):
    if scale is None:
        (e,), refs = refs[:1], refs[1:]
    else:
        (own, e, grad_qkv), refs = (*refs[:2], refs[5]), (*refs[2:5], *refs[6:])
        for k in range(3):
            block = slice(32 * k, 32 * k + 32)
            grad_qkv[k] = (own[72:104, block] + e[72:104, block]) * scale
    hid, dpf, payload, dlog, dtemp, lhs_h, lhs_w, dden = refs
    rows = cells.shape[0]
    diag64 = iota((256, 256), 0) // 64 == iota((256, 256), 1) // 64
    diag32 = iota((128, 256), 0) // 32 == iota((128, 256), 1) // 64
    both = jnp.where(diag64, jnp.concatenate([e[0:64, :]] * 4, axis=0), 0.0)
    lhs_w[...] = both.T.astype(BF16)
    for i in range(2):
        part = jnp.concatenate([e[32 - 32 * i : 64 - 32 * i, :]] * 4, axis=0)
        lhs_h[128 * i : 128 * i + 128, :] = jnp.where(diag32, part, 0.0).astype(BF16)
    dden[...] = jnp.broadcast_to(e[64:72, :].T[:, 0:1], (256, CHUNK))
    dtemp[...] = jnp.zeros(dtemp.shape, F32)

    def chunk(j, carry):
        at = chunk_of(j)
        hf = nn(lhs_h[...], weights[:, at])
        hid[:, at] = hf[0:128].astype(BF16)
        dpf[128:256, at] = hf[128:256].astype(BF16)
        dw = nn(lhs_w[...], fd[:, at])
        outer = []
        for k in range(4):
            rng = slice(SLICES * k, SLICES * k + SLICES)
            t = tanhs[rng, at]
            soft = softs[rng, at]
            d = dw[rng] + dden[rng, :]
            inner = jnp.sum(soft * d, axis=0, keepdims=True)
            ds = soft * (d - inner)
            dlog[rng, at] = (ds * ((1.0 - t * t) * stats[8 + k : 9 + k, at])).astype(BF16)
            dt = jnp.sum(ds * t, axis=0, keepdims=True) * stats[16 + k : 17 + k, at]
            dt = dt.astype(BF16).astype(F32)
            dtemp[k : k + 1, at] = dt
            outer.append(wtc[HEAD * k : HEAD * k + HEAD, k : k + 1] * dt)
        dp = nn(wsd[...], dlog[:, at]) + jnp.concatenate(outer, axis=0)
        dpf[0:128, at] = dp.astype(BF16)
        return carry

    lax.fori_loop(0, rows // CHUNK, chunk, 0)
    payload[0:128, :] = nn(hid[...], cot[...]).astype(BF16)
    payload[128:384, :] = nn(dpf[...], cells[...]).astype(BF16)
    even = jnp.zeros((HEAD, 128), F32)
    odd = jnp.zeros((HEAD, 128), F32)
    for q in range(2):
        pair = dlog[128 * q : 128 * q + 128, :]
        even = even + nt(proj[64 * q : 64 * q + 32, :], pair)
        odd = odd + nt(proj[64 * q + 32 : 64 * q + 64, :], pair)
    d_slice = jnp.where(iota((HEAD, 128), 1) < SLICES, even, odd)
    d_slice = jnp.concatenate([d_slice[0:16], d_slice[16:32]], axis=1)
    d_temp = nt(dtemp[...].astype(BF16), proj[...])
    here = iota((HEADS, 128), 0) == iota((HEADS, 128), 1) // HEAD
    d_temp = jnp.sum(jnp.where(here, d_temp, 0.0), axis=0, keepdims=True)
    d_temp = jnp.concatenate(
        [jnp.broadcast_to(d_temp, (8, 128)), jnp.zeros((8, 128), F32)], axis=1
    )
    payload[384:408, :] = jnp.concatenate([d_slice, d_temp], axis=0).astype(BF16)
    payload[ROWS2:, :] = jnp.zeros((payload.shape[0] - ROWS2, WIDTH), BF16)


def write_rows(out, stage, sems, product):
    copies = []
    for j in range(out.shape[0] // WRITE):
        at = pl.ds(j * WRITE, WRITE)
        stage[at, :] = product(at).T.astype(BF16)
        copies.append(pltpu.make_async_copy(stage.at[at, :], out.at[at, :], sems.at[j]))
        copies[-1].start()
    for copy in copies:
        copy.wait()


def result_kernel(own, far, w_out, out, table, stage, sems):
    core = lax.rem(lax.axis_index("dom"), 2)
    order = [w_out[group_rows(g), :] for g in (core, 1 - core)]
    table[...] = jnp.concatenate(order, axis=0).T

    def product(at):
        return nn(table[...], jnp.concatenate([own[:, at], far[:, at]], axis=0))

    write_rows(out, stage, sems, product)


def grad_cells_kernel(own, far, w_x, w_fx, out, table, stage, sems):
    core = lax.rem(lax.axis_index("dom"), 2)
    for i, g in enumerate((core, 1 - core)):
        table[:, 256 * i : 256 * i + 128] = w_x[:, group_rows(g)]
        table[:, 256 * i + 128 : 256 * i + 256] = w_fx[:, group_rows(g)]

    def product(at):
        return nn(table[...], jnp.concatenate([own[:, at], far[:, at]], axis=0))

    write_rows(out, stage, sems, product)


def place_kernel(mine, other, d_x, d_fx, d_slice, d_temp, d_out):
    core = lax.rem(lax.axis_index("dom"), 2)
    for ref, g in ((mine, core), (other, 1 - core)):
        at = group_rows(g)
        d_out[at, :] = ref[0:128, :].astype(F32)
        d_x[:, at] = ref[128:256, :].astype(F32).T
        d_fx[:, at] = ref[256:384, :].astype(F32).T
    small = mine[384:ROWS2, :].astype(F32) + other[384:ROWS2, :].astype(F32)
    rows = jnp.concatenate([small[0:16, 0:128], small[0:16, 128:256]], axis=0)
    rows = rows + pltpu.roll(rows, 64, 1)
    d_slice[...] = rows[:, 0:SLICES]
    v = small[16:24, 0:128]
    v = v + pltpu.roll(v, 64, 1)
    v = v + pltpu.roll(v, 32, 1)
    d_temp[...] = v[0:1, 0:32]


VMEM = pl.BlockSpec(memory_space=pltpu.VMEM)
SMEM = pl.BlockSpec(memory_space=pltpu.SMEM)
HBM = pl.BlockSpec(memory_space=pltpu.HBM)


def call(kernel, shapes, args, scratch=(), name=None, ins=None, outs=None, flops=0):
    scratch = [pltpu.VMEM(*s) if isinstance(s, tuple) else s for s in scratch]
    estimate = pl.CostEstimate(flops=flops, bytes_accessed=0, transcendentals=0)
    return pl.pallas_call(
        kernel,
        out_shape=[jax.ShapeDtypeStruct(s, d) for s, d in shapes],
        in_specs=ins or [VMEM] * len(args),
        out_specs=outs or [VMEM] * len(shapes),
        scratch_shapes=scratch,
        name=name,
        cost_estimate=estimate if flops else None,
        compiler_params=pltpu.CompilerParams(vmem_limit_bytes=24 << 20),
    )(*args)


def body(devices, cells, counts, w_x, w_fx, w_slice, w_temp, w_qkv, w_out, cotangent):
    rows = cells.shape[0]
    peers = devices // 2
    groups = [list(range(c, devices, 2)) for c in range(2)]
    scale = 1.0 / math.sqrt(rows * devices)
    temp = w_temp.reshape(1, HEAD)
    hm = HEADS * SLICES

    def swap(x, mask):
        return lax.ppermute(x, "dom", [(i, i ^ mask) for i in range(devices)])

    def exchange(x):
        return lax.all_to_all(x, "dom", 0, 0, axis_index_groups=groups, tiled=True)

    hgm = hm // 2
    grouped = [
        ((hgm, rows), BF16),
        ((WIDTH // 2, rows), BF16),
        ((WIDTH, rows), BF16),
        ((32, rows), F32),
        ((ROWS1, 128), F32),
    ]
    local = call(
        forward_far_kernel,
        grouped
        + [
            ((WIDTH, WIDTH), BF16),
            ((WIDTH, WIDTH), BF16),
            ((256, 128), BF16),
            ((128, 256), BF16),
            ((HEADS, 128), BF16),
            ((128, HEADS), F32),
            ((rows, WIDTH), BF16),
            ((rows, WIDTH), BF16),
            ((WIDTH, WIDTH), BF16),
            ((WIDTH, WIDTH), BF16),
            ((WIDTH, WIDTH), BF16),
        ],
        (counts,)
        + tuple(
            pltpu.with_memory_space_constraint(x, pltpu.HBM)
            for x in (cells, cotangent, w_x, w_fx, w_slice, temp, w_out)
        ),
        scratch=[
            ((HEAD, SLICES), BF16),
            ((1, HEAD), BF16),
            pltpu.SemaphoreType.DMA((5,)),
            pltpu.SemaphoreType.DMA((2, rows // CHUNK)),
            ((256, 256), BF16),
        ],
        ins=[SMEM] + [HBM] * 7,
        name="forward_far",
    )
    far = local[:4]
    send = local[4]
    wxt, wft, wsb, wsd, wtb, wtc, cells, cotangent, w_x, w_fx, w_out = local[5:]
    other = swap(send, 1)
    *own, keep = call(
        forward_own_kernel,
        grouped,
        (counts, cells, cotangent, w_out, wxt, wft, wsb, wtb),
        scratch=[((256, 256), BF16)],
        ins=[SMEM] + [VMEM] * 7,
        name="forward_own",
        flops=6 * rows * WIDTH * WIDTH,
    )
    other, keep = lax.optimization_barrier((other, keep))
    part = ((ROWS1, 128), BF16)
    (total,) = call(narrow_add_kernel, [part], (keep, other), name="narrow")
    near = [2**b for b in range(1, devices.bit_length() - 3)]
    last = [devices // 4 * k for k in (1, 2, 3)]
    again = None
    for mask in near:
        other = swap(total, mask)
        if again is None:
            again = call(
                softmax_kernel,
                [((hgm, rows), F32)] * 4,
                (wsb, own[1], own[3], far[1], far[3]),
                name="softmax",
                flops=2 * rows * hm * 128,
            )
            other, *again = lax.optimization_barrier((other, *again))
        (total,) = call(narrow_add_kernel, [part], (total, other), name="near")
    parts = [total] + [swap(total, mask) for mask in last]
    (mine,) = call(mix_kernel, [((104, 256), F32)], (w_qkv, *parts), name="mix")
    other = swap(mine, 1)
    chunk = -(-ROWS2 // peers)
    chunk = -(-chunk // 8) * 8
    half = chunk * peers
    grads = [
        ((WIDTH // 2, rows), BF16),
        ((WIDTH, rows), BF16),
        ((half, WIDTH), BF16),
    ]
    scratch = [
        ((hgm, rows), BF16),
        ((8, rows), F32),
        ((256, 256), BF16),
        ((256, 256), BF16),
        ((hgm, CHUNK), F32),
    ]
    hid_own, dpf_own, keep = call(
        functools.partial(backward_kernel, None),
        grads,
        (cells, cotangent, wsd, wtc, *own, *again[:2], mine),
        scratch=scratch,
        name="backward_own",
        flops=8 * rows * WIDTH * WIDTH,
    )
    other, keep = lax.optimization_barrier((other, keep))
    hid_far, dpf_far, send, grad_qkv = call(
        functools.partial(backward_kernel, scale),
        grads + [((3, HEAD, HEAD), F32)],
        (cells, cotangent, wsd, wtc, *far, *again[2:], mine, other),
        scratch=scratch,
        name="backward_far",
    )
    other = swap(send, 1)
    staging = [((rows, WIDTH), BF16), pltpu.SemaphoreType.DMA((rows // WRITE,))]
    (result,) = call(
        result_kernel,
        [((rows, WIDTH), BF16)],
        (hid_own, hid_far, w_out),
        scratch=[((WIDTH, WIDTH), BF16)] + staging,
        outs=[HBM],
        name="result",
        flops=2 * rows * WIDTH * WIDTH,
    )
    other, result = lax.optimization_barrier((other, result))
    (grad_cells,) = call(
        grad_cells_kernel,
        [((rows, WIDTH), BF16)],
        (dpf_own, dpf_far, w_x, w_fx),
        scratch=[((WIDTH, 2 * WIDTH), BF16)] + staging,
        outs=[HBM],
        name="grad_cells",
        flops=4 * rows * WIDTH * WIDTH,
    )
    (summed,) = call(narrow_add_kernel, [((half, WIDTH), BF16)], (keep, other), name="pair_add")
    parts = exchange(summed)

    def gather(parts_ref, out):
        total = (sum_blocks(parts_ref, chunk) * scale).astype(BF16)
        for k in range(peers):
            out[chunk * k : chunk * k + chunk, :] = total

    (spread,) = call(gather, [((half, WIDTH), BF16)], (parts,), name="gather")
    mine = exchange(spread)
    other = swap(mine, 1)
    d_x, d_fx, d_slice, d_temp, d_out = call(
        place_kernel,
        [
            ((WIDTH, WIDTH), F32),
            ((WIDTH, WIDTH), F32),
            ((HEAD, SLICES), F32),
            ((1, HEAD), F32),
            ((WIDTH, WIDTH), F32),
        ],
        (mine, other),
        name="place",
    )
    return result, grad_cells, d_x, d_fx, d_slice, d_temp.reshape(HEAD), grad_qkv, d_out


def solution(mesh):
    cell = P(("groups", "dom"), None)
    return jax.shard_map(
        functools.partial(body, mesh.shape["dom"]),
        mesh=mesh,
        in_specs=(cell, P(("groups", "dom")), P(), P(), P(), P(), P(), P(), cell),
        out_specs=(
            cell,
            cell,
            P("groups", None),
            P("groups", None),
            P("groups", None),
            P("groups"),
            P("groups", None, None),
            P("groups", None),
        ),
        check_vma=False,
    )
```

```python
import functools
import math

import jax
import jax.numpy as jnp
from jax import lax
from jax.experimental import pallas as pl
from jax.experimental.pallas import tpu as pltpu
from jax.sharding import PartitionSpec as P

F32 = jnp.float32
BF16 = jnp.bfloat16
FINE = lax.Precision.HIGH
HEADS = 8
SLICES = 64
HEAD = 32
WIDTH = HEADS * HEAD
ROWS1 = 136
ROWS2 = 808
LOG2E = math.log2(math.e)
CHUNK = 1024
WRITE = 256


def nn(a, b, precision=None):
    return lax.dot_general(
        a, b, (((1,), (0,)), ((), ())), precision=precision, preferred_element_type=F32
    )


def nt(a, b, precision=None):
    return lax.dot_general(
        a, b, (((1,), (1,)), ((), ())), precision=precision, preferred_element_type=F32
    )


def iota(shape, dim):
    return lax.broadcasted_iota(jnp.int32, shape, dim)


def slice_blocks(w_slice):
    tall = jnp.concatenate([w_slice] * 4, axis=0)
    pick = (iota((SLICES, 256), 1) % SLICES == iota((SLICES, 256), 0)).astype(BF16)
    wide = nn(tall, pick)
    same = iota((128, 256), 0) // HEAD == iota((128, 256), 1) // SLICES
    return jnp.where(same, wide, 0.0)


def temp_blocks(w_temp):
    pick = (iota((HEAD, 128), 1) % HEAD == iota((HEAD, 128), 0)).astype(BF16)
    wide = nn(jnp.broadcast_to(w_temp, (HEADS, HEAD)), pick)
    same = iota((HEADS, 128), 0) == iota((HEADS, 128), 1) // HEAD
    return jnp.where(same, wide, 0.0).astype(BF16)


def group_rows(group):
    return pl.ds(pl.multiple_of(group * 128, 128), 128)


def chunk_of(j):
    return pl.ds(pl.multiple_of(j * CHUNK, CHUNK), CHUNK)


def forward_group(count, operands, outs, tab, group, wait):
    cells, cot, w_out, wxt, wft, wsb, wtb = operands
    weights, proj, fd, stats, payload = outs
    rows = cells.shape[0]
    mine = group_rows(group)
    tab[0:128, :] = wxt[mine, :]
    tab[128:256, :] = wft[mine, :]

    def chunk(j, carry):
        at = chunk_of(j)
        wait(j)
        both = nt(tab[...], cells[at, :]).astype(BF16)
        projected = both[0:128]
        proj[:, at] = projected
        dhid = nt(w_out[mine, :], cot[at, :]).astype(BF16)
        for k in range(4):
            fd[64 * k : 64 * k + 32, at] = both[128 + 32 * k : 160 + 32 * k]
            fd[64 * k + 32 : 64 * k + 64, at] = dhid[32 * k : 32 * k + 32]
        lin = nn(wtb[...], projected)
        e = jnp.exp(-jnp.abs(lin))
        soft = jnp.maximum(lin, 0.0) + jnp.log(1.0 + e)
        inv = 1.0 / (0.5 + soft)
        sig = jnp.where(lin >= 0, 1.0, e) / (1.0 + e)
        a = inv * (10.0 * LOG2E)
        live = jnp.where(j * CHUNK + iota((1, CHUNK), 1) < count, 1.0, 0.0)
        norms = []
        x = nn(wsb[...], projected)
        for k in range(4):
            t = jnp.tanh(x[SLICES * k : SLICES * k + SLICES] * 0.1)
            p = jnp.exp2(t * a[k : k + 1])
            r = live / jnp.sum(p, axis=0, keepdims=True)
            weights[SLICES * k : SLICES * k + SLICES, at] = (p * r).astype(BF16)
            norms.append(r)
        stats[0:8, at] = a
        stats[8:16, at] = inv
        stats[16:24, at] = inv * inv * sig * (-10.0)
        stats[24:32, at] = jnp.concatenate(norms + norms, axis=0)
        return carry

    lax.fori_loop(0, rows // CHUNK, chunk, 0)
    ones = jnp.ones((16, rows), BF16)
    first = iota((64, 128), 1) < SLICES
    for q in range(2):
        pair = slice(128 * q, 128 * q + 128)
        out = nt(jnp.concatenate([fd[pair, :], ones], axis=0), weights[pair, :])
        payload[64 * q : 64 * q + 64, :] = jnp.where(first, out[0:64], out[64:128])
        payload[128 + q : 129 + q, :] = out[128:129]
    payload[130:136, :] = jnp.zeros((6, 128), F32)


def forward_far_kernel(counts, cells_hbm, cot_hbm, *refs):
    hbm, refs = refs[:5], refs[5:]
    outs, refs = refs[:5], refs[5:]
    (wxt, wft, wsb, wsd, wtb, wtc, cells, cot, w_x, w_fx, w_out), refs = refs[:11], refs[11:]
    w_slice, w_temp, small, big, tab = refs
    core = lax.rem(lax.axis_index("dom"), 2)

    def load(source, target, slot, j):
        at = chunk_of(j)
        return pltpu.make_async_copy(source.at[at, :], target.at[at, :], big.at[slot, j])

    tables = [
        pltpu.make_async_copy(source, target, small.at[i])
        for i, (source, target) in enumerate(zip(hbm, (w_x, w_fx, w_slice, w_temp, w_out)))
    ]
    for table in tables:
        table.start()
    for j in range(cells.shape[0] // CHUNK):
        load(cells_hbm, cells, 0, j).start()
        load(cot_hbm, cot, 1, j).start()
    for table in tables:
        table.wait()
    blocks = temp_blocks(w_temp[...])
    wtb[...] = blocks
    wtc[...] = blocks.astype(F32).T
    wxt[...] = w_x[...].T
    wft[...] = w_fx[...].T
    slices = slice_blocks(w_slice[...])
    wsd[...] = slices.astype(BF16)
    wsb[...] = slices.T.astype(BF16)

    def wait(j):
        load(cells_hbm, cells, 0, j).wait()
        load(cot_hbm, cot, 1, j).wait()

    operands = (cells, cot, w_out, wxt, wft, wsb, wtb)
    forward_group(counts[0], operands, outs, tab, 1 - core, wait)


def forward_own_kernel(counts, *refs):
    core = lax.rem(lax.axis_index("dom"), 2)
    forward_group(counts[0], refs[:7], refs[7:12], refs[12], core, lambda j: None)


def narrow_add_kernel(mine, other, out):
    out[...] = (mine[...].astype(F32) + other[...].astype(F32)).astype(BF16)


def softmax_kernel(wsb, *refs):
    def chunk(j, carry):
        at = chunk_of(j)
        for g in range(2):
            proj, stats = refs[2 * g : 2 * g + 2]
            tanhs, soft = refs[4 + 2 * g : 6 + 2 * g]
            x = nn(wsb[...], proj[:, at])
            for k in range(4):
                rng = slice(SLICES * k, SLICES * k + SLICES)
                t = jnp.tanh(x[rng] * 0.1)
                tanhs[rng, at] = t
                soft[rng, at] = jnp.exp2(t * stats[k : k + 1, at]) * stats[24 + k : 25 + k, at]
        return carry

    lax.fori_loop(0, refs[0].shape[1] // CHUNK, chunk, 0)


def sum_blocks(ref, n):
    total = ref[0:n, :].astype(F32)
    for k in range(1, ref.shape[0] // n):
        total = total + ref[n * k : n * k + n, :].astype(F32)
    return total


def mix_kernel(w_qkv, *refs):
    parts, out = refs[:-1], refs[-1]
    total = sum(part[...].astype(F32) for part in parts)
    numer = jnp.concatenate([total[0:32], total[64:96]], axis=1)
    d_mixed = jnp.concatenate([total[32:64], total[96:128]], axis=1)
    denom = jnp.concatenate([total[128:129], total[129:130]], axis=1) + 1e-05
    inverse = 1.0 / denom
    tokens = numer * inverse
    maps = [w_qkv[k].astype(F32) for k in range(3)]
    qkv = nn(jnp.concatenate([m.T for m in maps], axis=0), tokens, FINE)
    q, key, val = qkv[0:32], qkv[32:64], qkv[64:96]
    key_rows, val_rows = key.T, val.T
    scores = nn(key_rows, q, FINE) * (1.0 / math.sqrt(HEAD))
    same = iota((256, 256), 0) // SLICES == iota((256, 256), 1) // SLICES
    t = jnp.tanh(scores * 0.1)
    powers = jnp.where(same, jnp.exp2(t * (10.0 * LOG2E)), 0.0)
    att = powers * (1.0 / jnp.sum(powers, axis=0, keepdims=True))
    mixed = nn(val, att, FINE)
    d_att = nn(val_rows, d_mixed, FINE)
    d_val = nt(d_mixed, att, FINE)
    inner = jnp.sum(att * d_att, axis=0, keepdims=True)
    d_scores = att * (d_att - inner) * ((1.0 - t * t) * (1.0 / math.sqrt(HEAD)))
    d_q = nn(key, d_scores, FINE)
    d_key = nt(q, d_scores, FINE)
    grads = (d_q, d_key, d_val)
    d_tokens = sum(nn(m, g, FINE) for m, g in zip(maps, grads))
    d_numer = d_tokens * inverse
    d_denom = -jnp.sum(d_numer * tokens, axis=0, keepdims=True)
    out[0:32, :] = d_numer.astype(BF16).astype(F32)
    out[32:64, :] = mixed.astype(BF16).astype(F32)
    out[64:72, :] = jnp.broadcast_to(d_denom, (8, 256))
    out[72:104, 0:96] = nt(tokens, jnp.concatenate(grads, axis=0), FINE)
    out[72:104, 96:256] = jnp.zeros((32, 160), F32)


def backward_kernel(
    cells, cot, wsd, wtc, weights, proj, fd, stats, tanhs, softs, e,
    hid, dpf, payload,
    dlog, dtemp, lhs_h, lhs_w, dden,
):
    rows = cells.shape[0]
    diag64 = iota((256, 256), 0) // 64 == iota((256, 256), 1) // 64
    diag32 = iota((128, 256), 0) // 32 == iota((128, 256), 1) // 64
    both = jnp.where(diag64, jnp.concatenate([e[0:64, :]] * 4, axis=0), 0.0)
    lhs_w[...] = both.T.astype(BF16)
    for i in range(2):
        part = jnp.concatenate([e[32 - 32 * i : 64 - 32 * i, :]] * 4, axis=0)
        lhs_h[128 * i : 128 * i + 128, :] = jnp.where(diag32, part, 0.0).astype(BF16)
    dden[...] = jnp.broadcast_to(e[64:72, :].T[:, 0:1], (256, CHUNK))
    dtemp[...] = jnp.zeros(dtemp.shape, F32)

    def chunk(j, carry):
        at = chunk_of(j)
        hf = nn(lhs_h[...], weights[:, at])
        hid[:, at] = hf[0:128].astype(BF16)
        dpf[128:256, at] = hf[128:256].astype(BF16)
        dw = nn(lhs_w[...], fd[:, at])
        outer = []
        for k in range(4):
            rng = slice(SLICES * k, SLICES * k + SLICES)
            t = tanhs[rng, at]
            soft = softs[rng, at]
            d = dw[rng] + dden[rng, :]
            inner = jnp.sum(soft * d, axis=0, keepdims=True)
            ds = soft * (d - inner)
            dlog[rng, at] = (ds * ((1.0 - t * t) * stats[8 + k : 9 + k, at])).astype(BF16)
            dt = jnp.sum(ds * t, axis=0, keepdims=True) * stats[16 + k : 17 + k, at]
            dt = dt.astype(BF16).astype(F32)
            dtemp[k : k + 1, at] = dt
            outer.append(wtc[HEAD * k : HEAD * k + HEAD, k : k + 1] * dt)
        dp = nn(wsd[...], dlog[:, at]) + jnp.concatenate(outer, axis=0)
        dpf[0:128, at] = dp.astype(BF16)
        return carry

    lax.fori_loop(0, rows // CHUNK, chunk, 0)
    d_out = nn(hid[...], cot[...]).astype(BF16)
    d_in = nn(dpf[...], cells[...]).astype(BF16)
    for i, grad in enumerate((d_out, d_in[0:128], d_in[128:256])):
        payload[256 * i : 256 * i + 128, :] = grad[:, 0:128]
        payload[256 * i + 128 : 256 * i + 256, :] = grad[:, 128:256]
    even = jnp.zeros((HEAD, 128), F32)
    odd = jnp.zeros((HEAD, 128), F32)
    for q in range(2):
        pair = dlog[128 * q : 128 * q + 128, :]
        even = even + nt(proj[64 * q : 64 * q + 32, :], pair)
        odd = odd + nt(proj[64 * q + 32 : 64 * q + 64, :], pair)
    d_slice = jnp.where(iota((HEAD, 128), 1) < SLICES, even, odd)
    d_temp = nt(dtemp[...].astype(BF16), proj[...])
    here = iota((HEADS, 128), 0) == iota((HEADS, 128), 1) // HEAD
    d_temp = jnp.sum(jnp.where(here, d_temp, 0.0), axis=0, keepdims=True)
    d_temp = jnp.broadcast_to(d_temp, (8, 128))
    payload[768:ROWS2, :] = jnp.concatenate([d_slice, d_temp], axis=0).astype(BF16)
    payload[ROWS2:, :] = jnp.zeros((payload.shape[0] - ROWS2, 128), BF16)


def write_rows(out, stage, sems, product, copies=()):
    copies = list(copies)
    for j in range(out.shape[0] // WRITE):
        at = pl.ds(j * WRITE, WRITE)
        stage[at, :] = product(at).T.astype(BF16)
        copies.append(pltpu.make_async_copy(stage.at[at, :], out.at[at, :], sems.at[j]))
        copies[-1].start()
    for copy in copies:
        copy.wait()


def result_kernel(
    scale, own, far, w_out, e_own, e_far, out, grad_qkv, qkv, sem, table, stage, sems,
):
    core = lax.rem(lax.axis_index("dom"), 2)
    for k in range(3):
        block = slice(32 * k, 32 * k + 32)
        qkv[k] = (e_own[72:104, block] + e_far[72:104, block]) * scale
    copy = pltpu.make_async_copy(qkv, grad_qkv, sem.at[0])
    copy.start()
    order = [w_out[group_rows(g), :] for g in (core, 1 - core)]
    table[...] = jnp.concatenate(order, axis=0).T

    def product(at):
        return nn(table[...], jnp.concatenate([own[:, at], far[:, at]], axis=0))

    write_rows(out, stage, sems, product, [copy])


def grad_cells_kernel(own, far, w_x, w_fx, out, table, stage, sems):
    core = lax.rem(lax.axis_index("dom"), 2)
    for i, g in enumerate((core, 1 - core)):
        table[:, 256 * i : 256 * i + 128] = w_x[:, group_rows(g)]
        table[:, 256 * i + 128 : 256 * i + 256] = w_fx[:, group_rows(g)]

    def product(at):
        return nn(table[...], jnp.concatenate([own[:, at], far[:, at]], axis=0))

    write_rows(out, stage, sems, product)


def place_kernel(mine, other, *refs):
    outs, (d_x, d_fx, d_slice, d_temp, d_out), sems = refs[:5], refs[5:10], refs[10]
    core = lax.rem(lax.axis_index("dom"), 2)
    copies = []

    def copy_out(i):
        copies.append(pltpu.make_async_copy(refs[5 + i], outs[i], sems.at[i]))
        copies[-1].start()

    parts = ((mine, group_rows(core)), (other, group_rows(1 - core)))
    for ref, at in parts:
        d_out[at, 0:128] = ref[0:128, :].astype(F32)
        d_out[at, 128:256] = ref[128:256, :].astype(F32)
    copy_out(4)
    for i, grad in enumerate((d_x, d_fx)):
        first = 256 * i + 256
        for ref, at in parts:
            grad[0:128, at] = ref[first : first + 128, :].astype(F32).T
            grad[128:256, at] = ref[first + 128 : first + 256, :].astype(F32).T
        copy_out(i)
    small = mine[768:ROWS2, :].astype(F32) + other[768:ROWS2, :].astype(F32)
    rows = small[0:32] + pltpu.roll(small[0:32], 64, 1)
    d_slice[...] = rows[:, 0:SLICES]
    copy_out(2)
    v = small[32:40]
    v = v + pltpu.roll(v, 64, 1)
    v = v + pltpu.roll(v, 32, 1)
    d_temp[...] = v[0:1, 0:HEAD]
    copy_out(3)
    for copy in copies:
        copy.wait()


VMEM = pl.BlockSpec(memory_space=pltpu.VMEM)
SMEM = pl.BlockSpec(memory_space=pltpu.SMEM)
HBM = pl.BlockSpec(memory_space=pltpu.HBM)


def call(kernel, shapes, args, scratch=(), name=None, ins=None, outs=None, flops=0):
    scratch = [pltpu.VMEM(*s) if isinstance(s, tuple) else s for s in scratch]
    estimate = pl.CostEstimate(flops=flops, bytes_accessed=0, transcendentals=0)
    return pl.pallas_call(
        kernel,
        out_shape=[jax.ShapeDtypeStruct(s, d) for s, d in shapes],
        in_specs=ins or [VMEM] * len(args),
        out_specs=outs or [VMEM] * len(shapes),
        scratch_shapes=scratch,
        name=name,
        cost_estimate=estimate if flops else None,
        compiler_params=pltpu.CompilerParams(vmem_limit_bytes=24 << 20),
    )(*args)


def body(devices, cells, counts, w_x, w_fx, w_slice, w_temp, w_qkv, w_out, cotangent):
    rows = cells.shape[0]
    peers = devices // 2
    groups = [list(range(c, devices, 2)) for c in range(2)]
    scale = 1.0 / math.sqrt(rows * devices)
    temp = w_temp.reshape(1, HEAD)
    hm = HEADS * SLICES

    def swap(x, mask):
        return lax.ppermute(x, "dom", [(i, i ^ mask) for i in range(devices)])

    def exchange(x):
        return lax.all_to_all(x, "dom", 0, 0, axis_index_groups=groups, tiled=True)

    hgm = hm // 2
    grouped = [
        ((hgm, rows), BF16),
        ((WIDTH // 2, rows), BF16),
        ((WIDTH, rows), BF16),
        ((32, rows), F32),
        ((ROWS1, 128), F32),
    ]
    local = call(
        forward_far_kernel,
        grouped
        + [
            ((WIDTH, WIDTH), BF16),
            ((WIDTH, WIDTH), BF16),
            ((256, 128), BF16),
            ((128, 256), BF16),
            ((HEADS, 128), BF16),
            ((128, HEADS), F32),
            ((rows, WIDTH), BF16),
            ((rows, WIDTH), BF16),
            ((WIDTH, WIDTH), BF16),
            ((WIDTH, WIDTH), BF16),
            ((WIDTH, WIDTH), BF16),
        ],
        (counts,)
        + tuple(
            pltpu.with_memory_space_constraint(x, pltpu.HBM)
            for x in (cells, cotangent, w_x, w_fx, w_slice, temp, w_out)
        ),
        scratch=[
            ((HEAD, SLICES), BF16),
            ((1, HEAD), BF16),
            pltpu.SemaphoreType.DMA((5,)),
            pltpu.SemaphoreType.DMA((2, rows // CHUNK)),
            ((256, 256), BF16),
        ],
        ins=[SMEM] + [HBM] * 7,
        name="forward_far",
    )
    far = local[:4]
    send = local[4]
    wxt, wft, wsb, wsd, wtb, wtc, cells, cotangent, w_x, w_fx, w_out = local[5:]
    other = swap(send, 1)
    *own, keep = call(
        forward_own_kernel,
        grouped,
        (counts, cells, cotangent, w_out, wxt, wft, wsb, wtb),
        scratch=[((256, 256), BF16)],
        ins=[SMEM] + [VMEM] * 7,
        name="forward_own",
        flops=6 * rows * WIDTH * WIDTH,
    )
    other, keep = lax.optimization_barrier((other, keep))
    part = ((ROWS1, 128), BF16)
    (total,) = call(narrow_add_kernel, [part], (keep, other), name="narrow")
    near = [2**b for b in range(1, devices.bit_length() - 3)]
    last = [devices // 4 * k for k in (1, 2, 3)]
    again = None
    for mask in near:
        other = swap(total, mask)
        if again is None:
            again = call(
                softmax_kernel,
                [((hgm, rows), F32)] * 4,
                (wsb, own[1], own[3], far[1], far[3]),
                name="softmax",
                flops=2 * rows * hm * 128,
            )
            other, *again = lax.optimization_barrier((other, *again))
        (total,) = call(narrow_add_kernel, [part], (total, other), name="near")
    parts = [total] + [swap(total, mask) for mask in last]
    (mine,) = call(mix_kernel, [((104, 256), F32)], (w_qkv, *parts), name="mix")
    other = swap(mine, 1)
    chunk = -(-ROWS2 // peers)
    chunk = -(-chunk // 8) * 8
    half = chunk * peers
    grads = [
        ((WIDTH // 2, rows), BF16),
        ((WIDTH, rows), BF16),
        ((half, 128), BF16),
    ]
    scratch = [
        ((hgm, rows), BF16),
        ((8, rows), F32),
        ((256, 256), BF16),
        ((256, 256), BF16),
        ((hgm, CHUNK), F32),
    ]
    hid_own, dpf_own, keep = call(
        backward_kernel,
        grads,
        (cells, cotangent, wsd, wtc, *own, *again[:2], mine),
        scratch=scratch,
        name="backward_own",
        flops=8 * rows * WIDTH * WIDTH,
    )
    other, keep = lax.optimization_barrier((other, keep))
    maps = other
    hid_far, dpf_far, send = call(
        backward_kernel,
        grads,
        (cells, cotangent, wsd, wtc, *far, *again[2:], maps),
        scratch=scratch,
        name="backward_far",
    )
    other = swap(send, 1)
    staging = [((rows, WIDTH), BF16), pltpu.SemaphoreType.DMA((rows // WRITE,))]
    result, grad_qkv = call(
        functools.partial(result_kernel, scale),
        [((rows, WIDTH), BF16), ((3, HEAD, HEAD), F32)],
        (hid_own, hid_far, w_out, mine, maps),
        scratch=[((3, HEAD, HEAD), F32), pltpu.SemaphoreType.DMA((1,)), ((WIDTH, WIDTH), BF16)]
        + staging,
        outs=[HBM, HBM],
        name="result",
        flops=2 * rows * WIDTH * WIDTH,
    )
    other, result = lax.optimization_barrier((other, result))
    (grad_cells,) = call(
        grad_cells_kernel,
        [((rows, WIDTH), BF16)],
        (dpf_own, dpf_far, w_x, w_fx),
        scratch=[((WIDTH, 2 * WIDTH), BF16)] + staging,
        outs=[HBM],
        name="grad_cells",
        flops=4 * rows * WIDTH * WIDTH,
    )
    (summed,) = call(narrow_add_kernel, [((half, 128), BF16)], (keep, other), name="pair_add")
    parts = exchange(summed)

    def gather(parts_ref, out):
        total = (sum_blocks(parts_ref, chunk) * scale).astype(BF16)
        for k in range(peers):
            out[chunk * k : chunk * k + chunk, :] = total

    (spread,) = call(gather, [((half, 128), BF16)], (parts,), name="gather")
    mine = exchange(spread)
    other = swap(mine, 1)
    shapes = [
        ((WIDTH, WIDTH), F32),
        ((WIDTH, WIDTH), F32),
        ((HEAD, SLICES), F32),
        ((1, HEAD), F32),
        ((WIDTH, WIDTH), F32),
    ]
    d_x, d_fx, d_slice, d_temp, d_out = call(
        place_kernel,
        shapes,
        (mine, other),
        scratch=[*shapes, pltpu.SemaphoreType.DMA((5,))],
        outs=[HBM] * 5,
        name="place",
    )
    return result, grad_cells, d_x, d_fx, d_slice, d_temp.reshape(HEAD), grad_qkv, d_out


def solution(mesh):
    cell = P(("groups", "dom"), None)
    return jax.shard_map(
        functools.partial(body, mesh.shape["dom"]),
        mesh=mesh,
        in_specs=(cell, P(("groups", "dom")), P(), P(), P(), P(), P(), P(), cell),
        out_specs=(
            cell,
            cell,
            P("groups", None),
            P("groups", None),
            P("groups", None),
            P("groups"),
            P("groups", None, None),
            P("groups", None),
        ),
        check_vma=False,
    )
```

```python
import functools
import math

import jax
import jax.numpy as jnp
from jax import lax
from jax.experimental import pallas as pl
from jax.experimental.pallas import tpu as pltpu
from jax.sharding import PartitionSpec as P

F32 = jnp.float32
BF16 = jnp.bfloat16
FINE = lax.Precision.HIGH
HEADS = 8
SLICES = 64
HEAD = 32
WIDTH = HEADS * HEAD
ROWS1 = 136
ROWS2 = 808
LOG2E = math.log2(math.e)
CHUNK = 1024
WRITE = 256


def nn(a, b, precision=None):
    return lax.dot_general(
        a, b, (((1,), (0,)), ((), ())), precision=precision, preferred_element_type=F32
    )


def nt(a, b, precision=None):
    return lax.dot_general(
        a, b, (((1,), (1,)), ((), ())), precision=precision, preferred_element_type=F32
    )


def iota(shape, dim):
    return lax.broadcasted_iota(jnp.int32, shape, dim)


def slice_blocks(w_slice):
    tall = jnp.concatenate([w_slice] * 4, axis=0)
    pick = (iota((SLICES, 256), 1) % SLICES == iota((SLICES, 256), 0)).astype(BF16)
    wide = nn(tall, pick)
    same = iota((128, 256), 0) // HEAD == iota((128, 256), 1) // SLICES
    return jnp.where(same, wide, 0.0)


def temp_blocks(w_temp):
    pick = (iota((HEAD, 128), 1) % HEAD == iota((HEAD, 128), 0)).astype(BF16)
    wide = nn(jnp.broadcast_to(w_temp, (HEADS, HEAD)), pick)
    same = iota((HEADS, 128), 0) == iota((HEADS, 128), 1) // HEAD
    return jnp.where(same, wide, 0.0).astype(BF16)


def group_rows(group):
    return pl.ds(pl.multiple_of(group * 128, 128), 128)


def chunk_of(j):
    return pl.ds(pl.multiple_of(j * CHUNK, CHUNK), CHUNK)


def forward_group(count, operands, outs, tab, group, wait):
    cells, cot, w_out, wxt, wft, wsb, wtb = operands
    weights, proj, fd, stats, payload = outs
    rows = cells.shape[0]
    mine = group_rows(group)
    tab[0:128, :] = wxt[mine, :]
    tab[128:256, :] = wft[mine, :]

    def chunk(j, carry):
        at = chunk_of(j)
        wait(j)
        both = nt(tab[...], cells[at, :]).astype(BF16)
        projected = both[0:128]
        proj[:, at] = projected
        dhid = nt(w_out[mine, :], cot[at, :]).astype(BF16)
        for k in range(4):
            fd[64 * k : 64 * k + 32, at] = both[128 + 32 * k : 160 + 32 * k]
            fd[64 * k + 32 : 64 * k + 64, at] = dhid[32 * k : 32 * k + 32]
        lin = nn(wtb[...], projected)
        e = jnp.exp(-jnp.abs(lin))
        soft = jnp.maximum(lin, 0.0) + jnp.log(1.0 + e)
        inv = 1.0 / (0.5 + soft)
        sig = jnp.where(lin >= 0, 1.0, e) / (1.0 + e)
        a = inv * (10.0 * LOG2E)
        live = jnp.where(j * CHUNK + iota((1, CHUNK), 1) < count, 1.0, 0.0)
        norms = []
        x = nn(wsb[...], projected)
        for k in range(4):
            t = jnp.tanh(x[SLICES * k : SLICES * k + SLICES] * 0.1)
            p = jnp.exp2(t * a[k : k + 1])
            r = live / jnp.sum(p, axis=0, keepdims=True)
            weights[SLICES * k : SLICES * k + SLICES, at] = (p * r).astype(BF16)
            norms.append(r)
        stats[0:8, at] = a
        stats[8:16, at] = inv
        stats[16:24, at] = inv * inv * sig * (-10.0)
        stats[24:32, at] = jnp.concatenate(norms + norms, axis=0)
        return carry

    lax.fori_loop(0, rows // CHUNK, chunk, 0)
    ones = jnp.ones((16, rows), BF16)
    first = iota((64, 128), 1) < SLICES
    for q in range(2):
        pair = slice(128 * q, 128 * q + 128)
        out = nt(jnp.concatenate([fd[pair, :], ones], axis=0), weights[pair, :])
        payload[64 * q : 64 * q + 64, :] = jnp.where(first, out[0:64], out[64:128])
        payload[128 + q : 129 + q, :] = out[128:129]
    payload[130:136, :] = jnp.zeros((6, 128), F32)


def forward_far_kernel(counts, cells_hbm, cot_hbm, *refs):
    hbm, refs = refs[:5], refs[5:]
    outs, refs = refs[:5], refs[5:]
    (wxt, wft, wsb, wsd, wtb, wtc, cells, cot, w_x, w_fx, w_out), refs = refs[:11], refs[11:]
    w_slice, w_temp, small, big, tab = refs
    core = lax.rem(lax.axis_index("dom"), 2)

    def load(source, target, slot, j):
        at = chunk_of(j)
        return pltpu.make_async_copy(source.at[at, :], target.at[at, :], big.at[slot, j])

    tables = [
        pltpu.make_async_copy(source, target, small.at[i])
        for i, (source, target) in enumerate(zip(hbm, (w_x, w_fx, w_slice, w_temp, w_out)))
    ]
    for table in tables:
        table.start()
    for j in range(cells.shape[0] // CHUNK):
        load(cells_hbm, cells, 0, j).start()
        load(cot_hbm, cot, 1, j).start()
    for table in tables:
        table.wait()
    blocks = temp_blocks(w_temp[...])
    wtb[...] = blocks
    wtc[...] = blocks.astype(F32).T
    wxt[...] = w_x[...].T
    wft[...] = w_fx[...].T
    slices = slice_blocks(w_slice[...])
    wsd[...] = slices.astype(BF16)
    wsb[...] = slices.T.astype(BF16)

    def wait(j):
        load(cells_hbm, cells, 0, j).wait()
        load(cot_hbm, cot, 1, j).wait()

    operands = (cells, cot, w_out, wxt, wft, wsb, wtb)
    forward_group(counts[0], operands, outs, tab, 1 - core, wait)


def forward_own_kernel(counts, *refs):
    core = lax.rem(lax.axis_index("dom"), 2)
    forward_group(counts[0], refs[:7], refs[7:12], refs[12], core, lambda j: None)


def narrow_add_kernel(mine, other, out):
    out[...] = (mine[...].astype(F32) + other[...].astype(F32)).astype(BF16)


def softmax_kernel(wsb, w_qkv, *refs):
    for k in range(3):
        refs[10][HEAD * k : HEAD * k + HEAD, :] = w_qkv[k].astype(F32).T

    def chunk(j, carry):
        at = chunk_of(j)
        for g in range(2):
            proj, stats = refs[2 * g : 2 * g + 2]
            tanhs, soft, slope = refs[4 + 3 * g : 7 + 3 * g]
            x = nn(wsb[...], proj[:, at])
            for k in range(4):
                rng = slice(SLICES * k, SLICES * k + SLICES)
                t = jnp.tanh(x[rng] * 0.1)
                tanhs[rng, at] = t
                slope[rng, at] = (1.0 - t * t) * stats[8 + k : 9 + k, at]
                soft[rng, at] = jnp.exp2(t * stats[k : k + 1, at]) * stats[24 + k : 25 + k, at]
        return carry

    lax.fori_loop(0, refs[0].shape[1] // CHUNK, chunk, 0)


def sum_blocks(ref, n):
    total = ref[0:n, :].astype(F32)
    for k in range(1, ref.shape[0] // n):
        total = total + ref[n * k : n * k + n, :].astype(F32)
    return total


def mix_kernel(w_qkv, turned, *refs):
    parts, out = refs[:-1], refs[-1]
    total = sum(part[...].astype(F32) for part in parts)
    numer = jnp.concatenate([total[0:32], total[64:96]], axis=1)
    d_mixed = jnp.concatenate([total[32:64], total[96:128]], axis=1)
    denom = jnp.concatenate([total[128:129], total[129:130]], axis=1) + 1e-05
    inverse = 1.0 / denom
    tokens = numer * inverse
    maps = [w_qkv[k].astype(F32) for k in range(3)]
    qkv = nn(turned[...], tokens, FINE)
    q, key, val = qkv[0:32], qkv[32:64], qkv[64:96]
    key_rows, val_rows = key.T, val.T
    scores = nn(key_rows, q, FINE) * (1.0 / math.sqrt(HEAD))
    same = iota((256, 256), 0) // SLICES == iota((256, 256), 1) // SLICES
    t = jnp.tanh(scores * 0.1)
    powers = jnp.where(same, jnp.exp2(t * (10.0 * LOG2E)), 0.0)
    att = powers * (1.0 / jnp.sum(powers, axis=0, keepdims=True))
    mixed = nn(val, att, FINE)
    d_att = nn(val_rows, d_mixed, FINE)
    d_val = nt(d_mixed, att, FINE)
    inner = jnp.sum(att * d_att, axis=0, keepdims=True)
    d_scores = att * (d_att - inner) * ((1.0 - t * t) * (1.0 / math.sqrt(HEAD)))
    d_q = nn(key, d_scores, FINE)
    d_key = nt(q, d_scores, FINE)
    grads = (d_q, d_key, d_val)
    d_tokens = sum(nn(m, g, FINE) for m, g in zip(maps, grads))
    d_numer = d_tokens * inverse
    d_denom = -jnp.sum(d_numer * tokens, axis=0, keepdims=True)
    out[0:32, :] = d_numer.astype(BF16).astype(F32)
    out[32:64, :] = mixed.astype(BF16).astype(F32)
    out[64:72, :] = jnp.broadcast_to(d_denom, (8, 256))
    out[72:104, 0:96] = nt(tokens, jnp.concatenate(grads, axis=0), FINE)
    out[72:104, 96:256] = jnp.zeros((32, 160), F32)


def backward_kernel(
    cells, cot, wsd, wtc, weights, proj, fd, stats, tanhs, softs, slopes, e,
    hid, dpf, payload,
    dlog, dtemp, lhs_h, lhs_w, dden,
):
    rows = cells.shape[0]
    diag64 = iota((256, 256), 0) // 64 == iota((256, 256), 1) // 64
    diag32 = iota((128, 256), 0) // 32 == iota((128, 256), 1) // 64
    both = jnp.where(diag64, jnp.concatenate([e[0:64, :]] * 4, axis=0), 0.0)
    lhs_w[...] = both.T.astype(BF16)
    for i in range(2):
        part = jnp.concatenate([e[32 - 32 * i : 64 - 32 * i, :]] * 4, axis=0)
        lhs_h[128 * i : 128 * i + 128, :] = jnp.where(diag32, part, 0.0).astype(BF16)
    dden[...] = jnp.broadcast_to(e[64:72, :].T[:, 0:1], (256, 128))
    dtemp[...] = jnp.zeros(dtemp.shape, F32)

    def chunk(j, carry):
        at = chunk_of(j)
        hf = nn(lhs_h[...], weights[:, at])
        hid[:, at] = hf[0:128].astype(BF16)
        dpf[128:256, at] = hf[128:256].astype(BF16)
        dw = nn(lhs_w[...], fd[:, at])
        outer = []
        for k in range(4):
            rng = slice(SLICES * k, SLICES * k + SLICES)
            t = tanhs[rng, at]
            soft = softs[rng, at]
            d = dw[rng] + jnp.concatenate([dden[rng, :]] * (CHUNK // 128), axis=1)
            inner = jnp.sum(soft * d, axis=0, keepdims=True)
            ds = soft * (d - inner)
            dlog[rng, at] = (ds * slopes[rng, at]).astype(BF16)
            dt = jnp.sum(ds * t, axis=0, keepdims=True) * stats[16 + k : 17 + k, at]
            dt = dt.astype(BF16).astype(F32)
            dtemp[k : k + 1, at] = dt
            outer.append(wtc[HEAD * k : HEAD * k + HEAD, k : k + 1] * dt)
        dp = nn(wsd[...], dlog[:, at]) + jnp.concatenate(outer, axis=0)
        dpf[0:128, at] = dp.astype(BF16)
        return carry

    lax.fori_loop(0, rows // CHUNK, chunk, 0)
    d_out = nn(hid[...], cot[...]).astype(BF16)
    d_in = nn(dpf[...], cells[...]).astype(BF16)
    for i, grad in enumerate((d_out, d_in[0:128], d_in[128:256])):
        payload[256 * i : 256 * i + 128, :] = grad[:, 0:128]
        payload[256 * i + 128 : 256 * i + 256, :] = grad[:, 128:256]
    every = nt(proj[...], dlog[...])
    even = every[0:32, 0:128] + every[64:96, 128:256]
    odd = every[32:64, 0:128] + every[96:128, 128:256]
    d_slice = jnp.where(iota((HEAD, 128), 1) < SLICES, even, odd)
    d_temp = nt(dtemp[...].astype(BF16), proj[...])
    here = iota((HEADS, 128), 0) == iota((HEADS, 128), 1) // HEAD
    d_temp = jnp.sum(jnp.where(here, d_temp, 0.0), axis=0, keepdims=True)
    d_temp = jnp.broadcast_to(d_temp, (8, 128))
    payload[768:ROWS2, :] = jnp.concatenate([d_slice, d_temp], axis=0).astype(BF16)
    payload[ROWS2:, :] = jnp.zeros((payload.shape[0] - ROWS2, 128), BF16)


def write_rows(out, stage, sems, product, copies=()):
    copies = list(copies)
    for j in range(out.shape[0] // WRITE):
        at = pl.ds(j * WRITE, WRITE)
        stage[at, :] = product(at).T.astype(BF16)
        copies.append(pltpu.make_async_copy(stage.at[at, :], out.at[at, :], sems.at[j]))
        copies[-1].start()
    for copy in copies:
        copy.wait()


def result_kernel(
    scale, own, far, w_out, e_own, e_far, out, grad_qkv, qkv, sem, table, stage, sems,
):
    core = lax.rem(lax.axis_index("dom"), 2)
    for k in range(3):
        block = slice(32 * k, 32 * k + 32)
        qkv[k] = (e_own[72:104, block] + e_far[72:104, block]) * scale
    copy = pltpu.make_async_copy(qkv, grad_qkv, sem.at[0])
    copy.start()
    order = [w_out[group_rows(g), :] for g in (core, 1 - core)]
    table[...] = jnp.concatenate(order, axis=0).T

    def product(at):
        return nn(table[...], jnp.concatenate([own[:, at], far[:, at]], axis=0))

    write_rows(out, stage, sems, product, [copy])


def grad_cells_kernel(own, far, w_x, w_fx, out, table, stage, sems):
    core = lax.rem(lax.axis_index("dom"), 2)
    for i, g in enumerate((core, 1 - core)):
        table[:, 256 * i : 256 * i + 128] = w_x[:, group_rows(g)]
        table[:, 256 * i + 128 : 256 * i + 256] = w_fx[:, group_rows(g)]

    def product(at):
        return nn(table[...], jnp.concatenate([own[:, at], far[:, at]], axis=0))

    write_rows(out, stage, sems, product)


def place_kernel(mine, other, *refs):
    outs, (d_x, d_fx, d_slice, d_temp, d_out), sems = refs[:5], refs[5:10], refs[10]
    core = lax.rem(lax.axis_index("dom"), 2)
    copies = []

    def copy_out(i):
        copies.append(pltpu.make_async_copy(refs[5 + i], outs[i], sems.at[i]))
        copies[-1].start()

    parts = ((mine, group_rows(core)), (other, group_rows(1 - core)))
    for ref, at in parts:
        d_out[at, 0:128] = ref[0:128, :].astype(F32)
        d_out[at, 128:256] = ref[128:256, :].astype(F32)
    copy_out(4)
    for i, grad in enumerate((d_x, d_fx)):
        first = 256 * i + 256
        for ref, at in parts:
            grad[0:128, at] = ref[first : first + 128, :].astype(F32).T
            grad[128:256, at] = ref[first + 128 : first + 256, :].astype(F32).T
        copy_out(i)
    small = mine[768:ROWS2, :].astype(F32) + other[768:ROWS2, :].astype(F32)
    rows = small[0:32] + pltpu.roll(small[0:32], 64, 1)
    d_slice[...] = rows[:, 0:SLICES]
    copy_out(2)
    v = small[32:40]
    v = v + pltpu.roll(v, 64, 1)
    v = v + pltpu.roll(v, 32, 1)
    d_temp[...] = v[0:1, 0:HEAD]
    copy_out(3)
    for copy in copies:
        copy.wait()


VMEM = pl.BlockSpec(memory_space=pltpu.VMEM)
SMEM = pl.BlockSpec(memory_space=pltpu.SMEM)
HBM = pl.BlockSpec(memory_space=pltpu.HBM)


def call(kernel, shapes, args, scratch=(), name=None, ins=None, outs=None, flops=0):
    scratch = [pltpu.VMEM(*s) if isinstance(s, tuple) else s for s in scratch]
    estimate = pl.CostEstimate(flops=flops, bytes_accessed=0, transcendentals=0)
    return pl.pallas_call(
        kernel,
        out_shape=[jax.ShapeDtypeStruct(s, d) for s, d in shapes],
        in_specs=ins or [VMEM] * len(args),
        out_specs=outs or [VMEM] * len(shapes),
        scratch_shapes=scratch,
        name=name,
        cost_estimate=estimate if flops else None,
        compiler_params=pltpu.CompilerParams(vmem_limit_bytes=24 << 20),
    )(*args)


def body(devices, cells, counts, w_x, w_fx, w_slice, w_temp, w_qkv, w_out, cotangent):
    rows = cells.shape[0]
    peers = devices // 2
    groups = [list(range(c, devices, 2)) for c in range(2)]
    scale = 1.0 / math.sqrt(rows * devices)
    temp = w_temp.reshape(1, HEAD)
    hm = HEADS * SLICES

    def swap(x, mask):
        return lax.ppermute(x, "dom", [(i, i ^ mask) for i in range(devices)])

    def exchange(x):
        return lax.all_to_all(x, "dom", 0, 0, axis_index_groups=groups, tiled=True)

    hgm = hm // 2
    grouped = [
        ((hgm, rows), BF16),
        ((WIDTH // 2, rows), BF16),
        ((WIDTH, rows), BF16),
        ((32, rows), F32),
        ((ROWS1, 128), F32),
    ]
    local = call(
        forward_far_kernel,
        grouped
        + [
            ((WIDTH, WIDTH), BF16),
            ((WIDTH, WIDTH), BF16),
            ((256, 128), BF16),
            ((128, 256), BF16),
            ((HEADS, 128), BF16),
            ((128, HEADS), F32),
            ((rows, WIDTH), BF16),
            ((rows, WIDTH), BF16),
            ((WIDTH, WIDTH), BF16),
            ((WIDTH, WIDTH), BF16),
            ((WIDTH, WIDTH), BF16),
        ],
        (counts,)
        + tuple(
            pltpu.with_memory_space_constraint(x, pltpu.HBM)
            for x in (cells, cotangent, w_x, w_fx, w_slice, temp, w_out)
        ),
        scratch=[
            ((HEAD, SLICES), BF16),
            ((1, HEAD), BF16),
            pltpu.SemaphoreType.DMA((5,)),
            pltpu.SemaphoreType.DMA((2, rows // CHUNK)),
            ((256, 256), BF16),
        ],
        ins=[SMEM] + [HBM] * 7,
        name="forward_far",
    )
    far = local[:4]
    send = local[4]
    wxt, wft, wsb, wsd, wtb, wtc, cells, cotangent, w_x, w_fx, w_out = local[5:]
    other = swap(send, 1)
    *own, keep = call(
        forward_own_kernel,
        grouped,
        (counts, cells, cotangent, w_out, wxt, wft, wsb, wtb),
        scratch=[((256, 256), BF16)],
        ins=[SMEM] + [VMEM] * 7,
        name="forward_own",
        flops=6 * rows * WIDTH * WIDTH,
    )
    other, keep = lax.optimization_barrier((other, keep))
    part = ((ROWS1, 128), BF16)
    (total,) = call(narrow_add_kernel, [part], (keep, other), name="narrow")
    near = [2**b for b in range(1, devices.bit_length() - 3)]
    last = [devices // 4 * k for k in (1, 2, 3)]
    again = None
    for mask in near:
        other = swap(total, mask)
        if again is None:
            again = call(
                softmax_kernel,
                [((hgm, rows), F32)] * 6 + [((3 * HEAD, HEAD), F32)],
                (wsb, w_qkv, own[1], own[3], far[1], far[3]),
                name="softmax",
                flops=2 * rows * hm * 128,
            )
            other, *again = lax.optimization_barrier((other, *again))
        (total,) = call(narrow_add_kernel, [part], (total, other), name="near")
    parts = [total] + [swap(total, mask) for mask in last]
    (mine,) = call(mix_kernel, [((104, 256), F32)], (w_qkv, again[6], *parts), name="mix")
    other = swap(mine, 1)
    chunk = -(-ROWS2 // peers)
    chunk = -(-chunk // 8) * 8
    half = chunk * peers
    grads = [
        ((WIDTH // 2, rows), BF16),
        ((WIDTH, rows), BF16),
        ((half, 128), BF16),
    ]
    scratch = [
        ((hgm, rows), BF16),
        ((8, rows), F32),
        ((256, 256), BF16),
        ((256, 256), BF16),
        ((hgm, 128), F32),
    ]
    hid_own, dpf_own, keep = call(
        backward_kernel,
        grads,
        (cells, cotangent, wsd, wtc, *own, *again[:3], mine),
        scratch=scratch,
        name="backward_own",
        flops=8 * rows * WIDTH * WIDTH,
    )
    other, keep = lax.optimization_barrier((other, keep))
    maps = other
    hid_far, dpf_far, send = call(
        backward_kernel,
        grads,
        (cells, cotangent, wsd, wtc, *far, *again[3:6], maps),
        scratch=scratch,
        name="backward_far",
    )
    other = swap(send, 1)
    staging = [((rows, WIDTH), BF16), pltpu.SemaphoreType.DMA((rows // WRITE,))]
    result, grad_qkv = call(
        functools.partial(result_kernel, scale),
        [((rows, WIDTH), BF16), ((3, HEAD, HEAD), F32)],
        (hid_own, hid_far, w_out, mine, maps),
        scratch=[((3, HEAD, HEAD), F32), pltpu.SemaphoreType.DMA((1,)), ((WIDTH, WIDTH), BF16)]
        + staging,
        outs=[HBM, HBM],
        name="result",
        flops=2 * rows * WIDTH * WIDTH,
    )
    other, result = lax.optimization_barrier((other, result))
    (grad_cells,) = call(
        grad_cells_kernel,
        [((rows, WIDTH), BF16)],
        (dpf_own, dpf_far, w_x, w_fx),
        scratch=[((WIDTH, 2 * WIDTH), BF16)] + staging,
        outs=[HBM],
        name="grad_cells",
        flops=4 * rows * WIDTH * WIDTH,
    )
    (summed,) = call(narrow_add_kernel, [((half, 128), BF16)], (keep, other), name="pair_add")
    parts = exchange(summed)

    def gather(parts_ref, out):
        total = (sum_blocks(parts_ref, chunk) * scale).astype(BF16)
        for k in range(peers):
            out[chunk * k : chunk * k + chunk, :] = total

    (spread,) = call(gather, [((half, 128), BF16)], (parts,), name="gather")
    mine = exchange(spread)
    other = swap(mine, 1)
    shapes = [
        ((WIDTH, WIDTH), F32),
        ((WIDTH, WIDTH), F32),
        ((HEAD, SLICES), F32),
        ((1, HEAD), F32),
        ((WIDTH, WIDTH), F32),
    ]
    d_x, d_fx, d_slice, d_temp, d_out = call(
        place_kernel,
        shapes,
        (mine, other),
        scratch=[*shapes, pltpu.SemaphoreType.DMA((5,))],
        outs=[HBM] * 5,
        name="place",
    )
    return result, grad_cells, d_x, d_fx, d_slice, d_temp.reshape(HEAD), grad_qkv, d_out


def solution(mesh):
    cell = P(("groups", "dom"), None)
    return jax.shard_map(
        functools.partial(body, mesh.shape["dom"]),
        mesh=mesh,
        in_specs=(cell, P(("groups", "dom")), P(), P(), P(), P(), P(), P(), cell),
        out_specs=(
            cell,
            cell,
            P("groups", None),
            P("groups", None),
            P("groups", None),
            P("groups"),
            P("groups", None, None),
            P("groups", None),
        ),
        check_vma=False,
    )
```

```python
import functools
import math

import jax
import jax.numpy as jnp
from jax import lax
from jax.experimental import pallas as pl
from jax.experimental.pallas import tpu as pltpu
from jax.sharding import PartitionSpec as P

F32 = jnp.float32
BF16 = jnp.bfloat16
FINE = lax.Precision.HIGH
HEADS = 8
SLICES = 64
HEAD = 32
WIDTH = HEADS * HEAD
ROWS1 = 136
ROWS2 = 808
LOG2E = math.log2(math.e)
CHUNK = 1024
WRITE = 256


def nn(a, b, precision=None):
    return lax.dot_general(
        a, b, (((1,), (0,)), ((), ())), precision=precision, preferred_element_type=F32
    )


def nt(a, b, precision=None):
    return lax.dot_general(
        a, b, (((1,), (1,)), ((), ())), precision=precision, preferred_element_type=F32
    )


def iota(shape, dim):
    return lax.broadcasted_iota(jnp.int32, shape, dim)


def slice_blocks(w_slice):
    tall = jnp.concatenate([w_slice] * 4, axis=0)
    pick = (iota((SLICES, 256), 1) % SLICES == iota((SLICES, 256), 0)).astype(BF16)
    wide = nn(tall, pick)
    same = iota((128, 256), 0) // HEAD == iota((128, 256), 1) // SLICES
    return jnp.where(same, wide, 0.0)


def temp_blocks(w_temp):
    pick = (iota((HEAD, 128), 1) % HEAD == iota((HEAD, 128), 0)).astype(BF16)
    wide = nn(jnp.broadcast_to(w_temp, (HEADS, HEAD)), pick)
    same = iota((HEADS, 128), 0) == iota((HEADS, 128), 1) // HEAD
    return jnp.where(same, wide, 0.0).astype(BF16)


def group_rows(group):
    return pl.ds(pl.multiple_of(group * 128, 128), 128)


def chunk_of(j):
    return pl.ds(pl.multiple_of(j * CHUNK, CHUNK), CHUNK)


def forward_group(count, operands, outs, tab, group, wait):
    cells, cot, w_out, wxt, wft, wsb, wtb = operands
    weights, proj, fd, stats, payload = outs
    rows = cells.shape[0]
    mine = group_rows(group)
    tab[0:128, :] = wxt[mine, :]
    tab[128:256, :] = wft[mine, :]

    def chunk(j, carry):
        at = chunk_of(j)
        wait(j)
        both = nt(tab[...], cells[at, :]).astype(BF16)
        projected = both[0:128]
        proj[:, at] = projected
        dhid = nt(w_out[mine, :], cot[at, :]).astype(BF16)
        for k in range(4):
            fd[64 * k : 64 * k + 32, at] = both[128 + 32 * k : 160 + 32 * k]
            fd[64 * k + 32 : 64 * k + 64, at] = dhid[32 * k : 32 * k + 32]
        lin = nn(wtb[...], projected)
        e = jnp.exp(-jnp.abs(lin))
        soft = jnp.maximum(lin, 0.0) + jnp.log(1.0 + e)
        inv = 1.0 / (0.5 + soft)
        sig = jnp.where(lin >= 0, 1.0, e) / (1.0 + e)
        a = inv * (10.0 * LOG2E)
        live = jnp.where(j * CHUNK + iota((1, CHUNK), 1) < count, 1.0, 0.0)
        norms = []
        x = nn(wsb[...], projected)
        for k in range(4):
            t = jnp.tanh(x[SLICES * k : SLICES * k + SLICES] * 0.1)
            p = jnp.exp2(t * a[k : k + 1])
            r = live / jnp.sum(p, axis=0, keepdims=True)
            weights[SLICES * k : SLICES * k + SLICES, at] = (p * r).astype(BF16)
            norms.append(r)
        stats[0:8, at] = a
        stats[8:16, at] = inv
        stats[16:24, at] = inv * inv * sig * (-10.0)
        stats[24:32, at] = jnp.concatenate(norms + norms, axis=0)
        return carry

    lax.fori_loop(0, rows // CHUNK, chunk, 0)
    ones = jnp.ones((16, rows), BF16)
    first = iota((64, 128), 1) < SLICES
    for q in range(2):
        pair = slice(128 * q, 128 * q + 128)
        out = nt(jnp.concatenate([fd[pair, :], ones], axis=0), weights[pair, :])
        payload[64 * q : 64 * q + 64, :] = jnp.where(first, out[0:64], out[64:128])
        payload[128 + q : 129 + q, :] = out[128:129]
    payload[130:136, :] = jnp.zeros((6, 128), F32)


def forward_far_kernel(counts, cells_hbm, cot_hbm, *refs):
    hbm, refs = refs[:5], refs[5:]
    outs, refs = refs[:5], refs[5:]
    (wxt, wft, wsb, wsd, wtb, wtc, cells, cot, w_x, w_fx, w_out), refs = refs[:11], refs[11:]
    w_slice, w_temp, small, big, tab = refs
    core = lax.rem(lax.axis_index("dom"), 2)

    def load(source, target, slot, j):
        at = chunk_of(j)
        return pltpu.make_async_copy(source.at[at, :], target.at[at, :], big.at[slot, j])

    tables = [
        pltpu.make_async_copy(source, target, small.at[i])
        for i, (source, target) in enumerate(zip(hbm, (w_x, w_fx, w_slice, w_temp, w_out)))
    ]
    for table in tables:
        table.start()
    for j in range(cells.shape[0] // CHUNK):
        load(cells_hbm, cells, 0, j).start()
        load(cot_hbm, cot, 1, j).start()
    for table in tables:
        table.wait()
    blocks = temp_blocks(w_temp[...])
    wtb[...] = blocks
    wtc[...] = blocks.astype(F32).T
    wxt[...] = w_x[...].T
    wft[...] = w_fx[...].T
    slices = slice_blocks(w_slice[...])
    wsd[...] = slices.astype(BF16)
    wsb[...] = slices.T.astype(BF16)

    def wait(j):
        load(cells_hbm, cells, 0, j).wait()
        load(cot_hbm, cot, 1, j).wait()

    operands = (cells, cot, w_out, wxt, wft, wsb, wtb)
    forward_group(counts[0], operands, outs, tab, 1 - core, wait)


def forward_own_kernel(counts, *refs):
    core = lax.rem(lax.axis_index("dom"), 2)
    forward_group(counts[0], refs[:7], refs[7:12], refs[12], core, lambda j: None)


def narrow_add_kernel(mine, other, out):
    out[...] = (mine[...].astype(F32) + other[...].astype(F32)).astype(BF16)


def softmax_kernel(wsb, w_qkv, *refs):
    for k in range(3):
        refs[10][HEAD * k : HEAD * k + HEAD, :] = w_qkv[k].astype(F32).T

    def chunk(j, carry):
        at = chunk_of(j)
        for g in range(2):
            proj, stats = refs[2 * g : 2 * g + 2]
            tanhs, soft, slope = refs[4 + 3 * g : 7 + 3 * g]
            x = nn(wsb[...], proj[:, at])
            for k in range(4):
                rng = slice(SLICES * k, SLICES * k + SLICES)
                t = jnp.tanh(x[rng] * 0.1)
                tanhs[rng, at] = t
                slope[rng, at] = (1.0 - t * t) * stats[8 + k : 9 + k, at]
                soft[rng, at] = jnp.exp2(t * stats[k : k + 1, at]) * stats[24 + k : 25 + k, at]
        return carry

    lax.fori_loop(0, refs[0].shape[1] // CHUNK, chunk, 0)


def sum_blocks(ref, n):
    total = ref[0:n, :].astype(F32)
    for k in range(1, ref.shape[0] // n):
        total = total + ref[n * k : n * k + n, :].astype(F32)
    return total


def mix_kernel(w_qkv, turned, *refs):
    parts, out = refs[:-1], refs[-1]
    total = sum(part[...].astype(F32) for part in parts)
    numer = jnp.concatenate([total[0:32], total[64:96]], axis=1)
    d_mixed = jnp.concatenate([total[32:64], total[96:128]], axis=1)
    denom = jnp.concatenate([total[128:129], total[129:130]], axis=1) + 1e-05
    inverse = 1.0 / denom
    tokens = numer * inverse
    maps = [w_qkv[k].astype(F32) for k in range(3)]
    qkv = nn(turned[...], tokens, FINE)
    same = iota((128, 128), 0) // SLICES == iota((128, 128), 1) // SLICES
    pairs = []
    for i in range(2):
        q, key, val = (qkv[32 * k : 32 * k + 32, 128 * i : 128 * i + 128] for k in range(3))
        d_mix = d_mixed[:, 128 * i : 128 * i + 128]
        scores = nn(key.T, q, FINE) * (1.0 / math.sqrt(HEAD))
        t = jnp.tanh(scores * 0.1)
        powers = jnp.where(same, jnp.exp2(t * (10.0 * LOG2E)), 0.0)
        att = powers * (1.0 / jnp.sum(powers, axis=0, keepdims=True))
        d_att = nn(val.T, d_mix, FINE)
        inner = jnp.sum(att * d_att, axis=0, keepdims=True)
        d_scores = att * (d_att - inner) * ((1.0 - t * t) * (1.0 / math.sqrt(HEAD)))
        d_qkv = (nn(key, d_scores, FINE), nt(q, d_scores, FINE), nt(d_mix, att, FINE))
        pairs.append((nn(val, att, FINE), *d_qkv))
    mixed, *grads = (jnp.concatenate(both, axis=1) for both in zip(*pairs))
    d_tokens = sum(nn(m, g, FINE) for m, g in zip(maps, grads))
    d_numer = d_tokens * inverse
    d_denom = -jnp.sum(d_numer * tokens, axis=0, keepdims=True)
    out[0:32, :] = d_numer.astype(BF16).astype(F32)
    out[32:64, :] = mixed.astype(BF16).astype(F32)
    out[64:72, :] = jnp.broadcast_to(d_denom, (8, 256))
    out[72:104, 0:96] = nt(tokens, jnp.concatenate(grads, axis=0), FINE)
    out[72:104, 96:256] = jnp.zeros((32, 160), F32)


def backward_kernel(
    cells, cot, wsd, wtc, weights, proj, fd, stats, tanhs, softs, slopes, e,
    hid, dpf, payload,
    dlog, dtemp, lhs_h, lhs_w, dden,
):
    rows = cells.shape[0]
    diag64 = iota((256, 256), 0) // 64 == iota((256, 256), 1) // 64
    diag32 = iota((128, 256), 0) // 32 == iota((128, 256), 1) // 64
    both = jnp.where(diag64, jnp.concatenate([e[0:64, :]] * 4, axis=0), 0.0)
    lhs_w[...] = both.T.astype(BF16)
    for i in range(2):
        part = jnp.concatenate([e[32 - 32 * i : 64 - 32 * i, :]] * 4, axis=0)
        lhs_h[128 * i : 128 * i + 128, :] = jnp.where(diag32, part, 0.0).astype(BF16)
    dden[...] = jnp.broadcast_to(e[64:72, :].T[:, 0:1], (256, 128))
    dtemp[...] = jnp.zeros(dtemp.shape, F32)

    def chunk(j, carry):
        at = chunk_of(j)
        hf = nn(lhs_h[...], weights[:, at])
        hid[:, at] = hf[0:128].astype(BF16)
        dpf[128:256, at] = hf[128:256].astype(BF16)
        dw = nn(lhs_w[...], fd[:, at])
        outer = []
        for k in range(4):
            rng = slice(SLICES * k, SLICES * k + SLICES)
            t = tanhs[rng, at]
            soft = softs[rng, at]
            d = dw[rng] + jnp.concatenate([dden[rng, :]] * (CHUNK // 128), axis=1)
            inner = jnp.sum(soft * d, axis=0, keepdims=True)
            ds = soft * (d - inner)
            dlog[rng, at] = (ds * slopes[rng, at]).astype(BF16)
            dt = jnp.sum(ds * t, axis=0, keepdims=True) * stats[16 + k : 17 + k, at]
            dt = dt.astype(BF16).astype(F32)
            dtemp[k : k + 1, at] = dt
            outer.append(wtc[HEAD * k : HEAD * k + HEAD, k : k + 1] * dt)
        dp = nn(wsd[...], dlog[:, at]) + jnp.concatenate(outer, axis=0)
        dpf[0:128, at] = dp.astype(BF16)
        return carry

    lax.fori_loop(0, rows // CHUNK, chunk, 0)
    d_out = nn(hid[...], cot[...]).astype(BF16)
    d_in = nn(dpf[...], cells[...]).astype(BF16)
    for i, grad in enumerate((d_out, d_in[0:128], d_in[128:256])):
        payload[256 * i : 256 * i + 128, :] = grad[:, 0:128]
        payload[256 * i + 128 : 256 * i + 256, :] = grad[:, 128:256]
    every = nt(proj[...], dlog[...])
    even = every[0:32, 0:128] + every[64:96, 128:256]
    odd = every[32:64, 0:128] + every[96:128, 128:256]
    d_slice = jnp.where(iota((HEAD, 128), 1) < SLICES, even, odd)
    d_temp = nt(dtemp[...].astype(BF16), proj[...])
    here = iota((HEADS, 128), 0) == iota((HEADS, 128), 1) // HEAD
    d_temp = jnp.sum(jnp.where(here, d_temp, 0.0), axis=0, keepdims=True)
    d_temp = jnp.broadcast_to(d_temp, (8, 128))
    payload[768:ROWS2, :] = jnp.concatenate([d_slice, d_temp], axis=0).astype(BF16)
    payload[ROWS2:, :] = jnp.zeros((payload.shape[0] - ROWS2, 128), BF16)


def write_rows(out, stage, sems, product, copies=()):
    copies = list(copies)
    for j in range(out.shape[0] // WRITE):
        at = pl.ds(j * WRITE, WRITE)
        stage[at, :] = product(at).T.astype(BF16)
        copies.append(pltpu.make_async_copy(stage.at[at, :], out.at[at, :], sems.at[j]))
        copies[-1].start()
    for copy in copies:
        copy.wait()


def result_kernel(
    scale, own, far, w_out, e_own, e_far, out, grad_qkv, qkv, sem, table, stage, sems,
):
    core = lax.rem(lax.axis_index("dom"), 2)
    for k in range(3):
        block = slice(32 * k, 32 * k + 32)
        qkv[k] = (e_own[72:104, block] + e_far[72:104, block]) * scale
    copy = pltpu.make_async_copy(qkv, grad_qkv, sem.at[0])
    copy.start()
    order = [w_out[group_rows(g), :] for g in (core, 1 - core)]
    table[...] = jnp.concatenate(order, axis=0).T

    def product(at):
        return nn(table[...], jnp.concatenate([own[:, at], far[:, at]], axis=0))

    write_rows(out, stage, sems, product, [copy])


def grad_cells_kernel(own, far, w_x, w_fx, out, table, stage, sems):
    core = lax.rem(lax.axis_index("dom"), 2)
    for i, g in enumerate((core, 1 - core)):
        table[:, 256 * i : 256 * i + 128] = w_x[:, group_rows(g)]
        table[:, 256 * i + 128 : 256 * i + 256] = w_fx[:, group_rows(g)]

    def product(at):
        return nn(table[...], jnp.concatenate([own[:, at], far[:, at]], axis=0))

    write_rows(out, stage, sems, product)


def place_kernel(mine, other, *refs):
    outs, (d_x, d_fx, d_slice, d_temp, d_out), sems = refs[:5], refs[5:10], refs[10]
    core = lax.rem(lax.axis_index("dom"), 2)
    copies = []

    def copy_out(i):
        copies.append(pltpu.make_async_copy(refs[5 + i], outs[i], sems.at[i]))
        copies[-1].start()

    parts = ((mine, group_rows(core)), (other, group_rows(1 - core)))
    for ref, at in parts:
        d_out[at, 0:128] = ref[0:128, :].astype(F32)
        d_out[at, 128:256] = ref[128:256, :].astype(F32)
    copy_out(4)
    for i, grad in enumerate((d_x, d_fx)):
        first = 256 * i + 256
        for ref, at in parts:
            grad[0:128, at] = ref[first : first + 128, :].astype(F32).T
            grad[128:256, at] = ref[first + 128 : first + 256, :].astype(F32).T
        copy_out(i)
    small = mine[768:ROWS2, :].astype(F32) + other[768:ROWS2, :].astype(F32)
    rows = small[0:32] + pltpu.roll(small[0:32], 64, 1)
    d_slice[...] = rows[:, 0:SLICES]
    copy_out(2)
    v = small[32:40]
    v = v + pltpu.roll(v, 64, 1)
    v = v + pltpu.roll(v, 32, 1)
    d_temp[...] = v[0:1, 0:HEAD]
    copy_out(3)
    for copy in copies:
        copy.wait()


VMEM = pl.BlockSpec(memory_space=pltpu.VMEM)
SMEM = pl.BlockSpec(memory_space=pltpu.SMEM)
HBM = pl.BlockSpec(memory_space=pltpu.HBM)


def call(kernel, shapes, args, scratch=(), name=None, ins=None, outs=None, flops=0):
    scratch = [pltpu.VMEM(*s) if isinstance(s, tuple) else s for s in scratch]
    estimate = pl.CostEstimate(flops=flops, bytes_accessed=0, transcendentals=0)
    return pl.pallas_call(
        kernel,
        out_shape=[jax.ShapeDtypeStruct(s, d) for s, d in shapes],
        in_specs=ins or [VMEM] * len(args),
        out_specs=outs or [VMEM] * len(shapes),
        scratch_shapes=scratch,
        name=name,
        cost_estimate=estimate if flops else None,
        compiler_params=pltpu.CompilerParams(vmem_limit_bytes=24 << 20),
    )(*args)


def body(devices, cells, counts, w_x, w_fx, w_slice, w_temp, w_qkv, w_out, cotangent):
    rows = cells.shape[0]
    peers = devices // 2
    groups = [list(range(c, devices, 2)) for c in range(2)]
    scale = 1.0 / math.sqrt(rows * devices)
    temp = w_temp.reshape(1, HEAD)
    hm = HEADS * SLICES

    def swap(x, mask):
        return lax.ppermute(x, "dom", [(i, i ^ mask) for i in range(devices)])

    def exchange(x):
        return lax.all_to_all(x, "dom", 0, 0, axis_index_groups=groups, tiled=True)

    hgm = hm // 2
    grouped = [
        ((hgm, rows), BF16),
        ((WIDTH // 2, rows), BF16),
        ((WIDTH, rows), BF16),
        ((32, rows), F32),
        ((ROWS1, 128), F32),
    ]
    local = call(
        forward_far_kernel,
        grouped
        + [
            ((WIDTH, WIDTH), BF16),
            ((WIDTH, WIDTH), BF16),
            ((256, 128), BF16),
            ((128, 256), BF16),
            ((HEADS, 128), BF16),
            ((128, HEADS), F32),
            ((rows, WIDTH), BF16),
            ((rows, WIDTH), BF16),
            ((WIDTH, WIDTH), BF16),
            ((WIDTH, WIDTH), BF16),
            ((WIDTH, WIDTH), BF16),
        ],
        (counts,)
        + tuple(
            pltpu.with_memory_space_constraint(x, pltpu.HBM)
            for x in (cells, cotangent, w_x, w_fx, w_slice, temp, w_out)
        ),
        scratch=[
            ((HEAD, SLICES), BF16),
            ((1, HEAD), BF16),
            pltpu.SemaphoreType.DMA((5,)),
            pltpu.SemaphoreType.DMA((2, rows // CHUNK)),
            ((256, 256), BF16),
        ],
        ins=[SMEM] + [HBM] * 7,
        name="forward_far",
    )
    far = local[:4]
    send = local[4]
    wxt, wft, wsb, wsd, wtb, wtc, cells, cotangent, w_x, w_fx, w_out = local[5:]
    other = swap(send, 1)
    *own, keep = call(
        forward_own_kernel,
        grouped,
        (counts, cells, cotangent, w_out, wxt, wft, wsb, wtb),
        scratch=[((256, 256), BF16)],
        ins=[SMEM] + [VMEM] * 7,
        name="forward_own",
        flops=6 * rows * WIDTH * WIDTH,
    )
    other, keep = lax.optimization_barrier((other, keep))
    part = ((ROWS1, 128), BF16)
    (total,) = call(narrow_add_kernel, [part], (keep, other), name="narrow")
    near = [2**b for b in range(1, devices.bit_length() - 3)]
    last = [devices // 4 * k for k in (1, 2, 3)]
    again = None
    for mask in near:
        other = swap(total, mask)
        if again is None:
            again = call(
                softmax_kernel,
                [((hgm, rows), F32)] * 6 + [((3 * HEAD, HEAD), F32)],
                (wsb, w_qkv, own[1], own[3], far[1], far[3]),
                name="softmax",
                flops=2 * rows * hm * 128,
            )
            other, *again = lax.optimization_barrier((other, *again))
        (total,) = call(narrow_add_kernel, [part], (total, other), name="near")
    parts = [total] + [swap(total, mask) for mask in last]
    (mine,) = call(mix_kernel, [((104, 256), F32)], (w_qkv, again[6], *parts), name="mix")
    other = swap(mine, 1)
    chunk = -(-ROWS2 // peers)
    chunk = -(-chunk // 8) * 8
    half = chunk * peers
    grads = [
        ((WIDTH // 2, rows), BF16),
        ((WIDTH, rows), BF16),
        ((half, 128), BF16),
    ]
    scratch = [
        ((hgm, rows), BF16),
        ((8, rows), F32),
        ((256, 256), BF16),
        ((256, 256), BF16),
        ((hgm, 128), F32),
    ]
    hid_own, dpf_own, keep = call(
        backward_kernel,
        grads,
        (cells, cotangent, wsd, wtc, *own, *again[:3], mine),
        scratch=scratch,
        name="backward_own",
        flops=8 * rows * WIDTH * WIDTH,
    )
    other, keep = lax.optimization_barrier((other, keep))
    maps = other
    hid_far, dpf_far, send = call(
        backward_kernel,
        grads,
        (cells, cotangent, wsd, wtc, *far, *again[3:6], maps),
        scratch=scratch,
        name="backward_far",
    )
    other = swap(send, 1)
    staging = [((rows, WIDTH), BF16), pltpu.SemaphoreType.DMA((rows // WRITE,))]
    result, grad_qkv = call(
        functools.partial(result_kernel, scale),
        [((rows, WIDTH), BF16), ((3, HEAD, HEAD), F32)],
        (hid_own, hid_far, w_out, mine, maps),
        scratch=[((3, HEAD, HEAD), F32), pltpu.SemaphoreType.DMA((1,)), ((WIDTH, WIDTH), BF16)]
        + staging,
        outs=[HBM, HBM],
        name="result",
        flops=2 * rows * WIDTH * WIDTH,
    )
    other, result = lax.optimization_barrier((other, result))
    (grad_cells,) = call(
        grad_cells_kernel,
        [((rows, WIDTH), BF16)],
        (dpf_own, dpf_far, w_x, w_fx),
        scratch=[((WIDTH, 2 * WIDTH), BF16)] + staging,
        outs=[HBM],
        name="grad_cells",
        flops=4 * rows * WIDTH * WIDTH,
    )
    (summed,) = call(narrow_add_kernel, [((half, 128), BF16)], (keep, other), name="pair_add")
    parts = exchange(summed)

    def gather(parts_ref, out):
        total = (sum_blocks(parts_ref, chunk) * scale).astype(BF16)
        for k in range(peers):
            out[chunk * k : chunk * k + chunk, :] = total

    (spread,) = call(gather, [((half, 128), BF16)], (parts,), name="gather")
    mine = exchange(spread)
    other = swap(mine, 1)
    shapes = [
        ((WIDTH, WIDTH), F32),
        ((WIDTH, WIDTH), F32),
        ((HEAD, SLICES), F32),
        ((1, HEAD), F32),
        ((WIDTH, WIDTH), F32),
    ]
    d_x, d_fx, d_slice, d_temp, d_out = call(
        place_kernel,
        shapes,
        (mine, other),
        scratch=[*shapes, pltpu.SemaphoreType.DMA((5,))],
        outs=[HBM] * 5,
        name="place",
    )
    return result, grad_cells, d_x, d_fx, d_slice, d_temp.reshape(HEAD), grad_qkv, d_out


def solution(mesh):
    cell = P(("groups", "dom"), None)
    return jax.shard_map(
        functools.partial(body, mesh.shape["dom"]),
        mesh=mesh,
        in_specs=(cell, P(("groups", "dom")), P(), P(), P(), P(), P(), P(), cell),
        out_specs=(
            cell,
            cell,
            P("groups", None),
            P("groups", None),
            P("groups", None),
            P("groups"),
            P("groups", None, None),
            P("groups", None),
        ),
        check_vma=False,
    )
```

```python
import functools
import math

import jax
import jax.numpy as jnp
from jax import lax
from jax.experimental import pallas as pl
from jax.experimental.pallas import tpu as pltpu
from jax.sharding import PartitionSpec as P

F32 = jnp.float32
BF16 = jnp.bfloat16
FINE = lax.Precision.HIGH
HEADS = 8
SLICES = 64
HEAD = 32
WIDTH = HEADS * HEAD
ROWS1 = 136
ROWS2 = 808
LOG2E = math.log2(math.e)
CHUNK = 1024
WRITE = 256


def nn(a, b, precision=None):
    return lax.dot_general(
        a, b, (((1,), (0,)), ((), ())), precision=precision, preferred_element_type=F32
    )


def nt(a, b, precision=None):
    return lax.dot_general(
        a, b, (((1,), (1,)), ((), ())), precision=precision, preferred_element_type=F32
    )


def iota(shape, dim):
    return lax.broadcasted_iota(jnp.int32, shape, dim)


def slice_blocks(w_slice):
    tall = jnp.concatenate([w_slice] * 4, axis=0)
    pick = (iota((SLICES, 256), 1) % SLICES == iota((SLICES, 256), 0)).astype(BF16)
    wide = nn(tall, pick)
    same = iota((128, 256), 0) // HEAD == iota((128, 256), 1) // SLICES
    return jnp.where(same, wide, 0.0)


def temp_blocks(w_temp):
    pick = (iota((HEAD, 128), 1) % HEAD == iota((HEAD, 128), 0)).astype(BF16)
    wide = nn(jnp.broadcast_to(w_temp, (HEADS, HEAD)), pick)
    same = iota((HEADS, 128), 0) == iota((HEADS, 128), 1) // HEAD
    return jnp.where(same, wide, 0.0).astype(BF16)


def group_rows(group):
    return pl.ds(pl.multiple_of(group * 128, 128), 128)


def chunk_of(j):
    return pl.ds(pl.multiple_of(j * CHUNK, CHUNK), CHUNK)


def forward_group(count, operands, outs, tab, group):
    cells, cot, w_out, wxt, wft, wsb, wtb = operands
    weights, proj, fd, stats, payload = outs
    rows = cells.shape[0]
    mine = group_rows(group)
    tab[0:128, :] = wxt[mine, :]
    tab[128:256, :] = wft[mine, :]

    def chunk(j, carry):
        at = chunk_of(j)
        both = nt(tab[...], cells[at, :]).astype(BF16)
        projected = both[0:128]
        proj[:, at] = projected
        dhid = nt(w_out[mine, :], cot[at, :]).astype(BF16)
        for k in range(4):
            fd[64 * k : 64 * k + 32, at] = both[128 + 32 * k : 160 + 32 * k]
            fd[64 * k + 32 : 64 * k + 64, at] = dhid[32 * k : 32 * k + 32]
        lin = nn(wtb[...], projected)
        e = jnp.exp(-jnp.abs(lin))
        soft = jnp.maximum(lin, 0.0) + jnp.log(1.0 + e)
        inv = 1.0 / (0.5 + soft)
        sig = jnp.where(lin >= 0, 1.0, e) / (1.0 + e)
        a = inv * (10.0 * LOG2E)
        live = jnp.where(j * CHUNK + iota((1, CHUNK), 1) < count, 1.0, 0.0)
        norms = []
        x = nn(wsb[...], projected)
        for k in range(4):
            t = jnp.tanh(x[SLICES * k : SLICES * k + SLICES] * 0.1)
            p = jnp.exp2(t * a[k : k + 1])
            r = live / jnp.sum(p, axis=0, keepdims=True)
            weights[SLICES * k : SLICES * k + SLICES, at] = (p * r).astype(BF16)
            norms.append(r)
        stats[0:8, at] = a
        stats[8:16, at] = inv
        stats[16:24, at] = inv * inv * sig * (-10.0)
        stats[24:32, at] = jnp.concatenate(norms + norms, axis=0)
        return carry

    lax.fori_loop(0, rows // CHUNK, chunk, 0)
    ones = jnp.ones((16, rows), BF16)
    first = iota((64, 128), 1) < SLICES
    for q in range(2):
        pair = slice(128 * q, 128 * q + 128)
        out = nt(jnp.concatenate([fd[pair, :], ones], axis=0), weights[pair, :])
        payload[64 * q : 64 * q + 64, :] = jnp.where(first, out[0:64], out[64:128])
        payload[128 + q : 129 + q, :] = out[128:129]
    payload[130:136, :] = jnp.zeros((6, 128), F32)


def forward_far_kernel(counts, cells_hbm, cot_hbm, *refs):
    hbm, refs = refs[:5], refs[5:]
    outs, refs = refs[:5], refs[5:]
    (wxt, wft, wsb, wsd, wtb, wtc, cells, cot, w_x, w_fx, w_out), refs = refs[:11], refs[11:]
    w_slice, w_temp, small, big, tab = refs
    core = lax.rem(lax.axis_index("dom"), 2)

    def load(source, target, slot, j):
        at = chunk_of(j)
        return pltpu.make_async_copy(source.at[at, :], target.at[at, :], big.at[slot, j])

    tables = [
        pltpu.make_async_copy(source, target, small.at[i])
        for i, (source, target) in enumerate(zip(hbm, (w_x, w_fx, w_slice, w_temp, w_out)))
    ]
    for table in tables:
        table.start()
    for j in range(cells.shape[0] // CHUNK):
        load(cells_hbm, cells, 0, j).start()
        load(cot_hbm, cot, 1, j).start()
    for table in tables:
        table.wait()
    for j in range(cells.shape[0] // CHUNK):
        load(cells_hbm, cells, 0, j).wait()
        load(cot_hbm, cot, 1, j).wait()
    blocks = temp_blocks(w_temp[...])
    wtb[...] = blocks
    wtc[...] = blocks.astype(F32).T
    wxt[...] = w_x[...].T
    wft[...] = w_fx[...].T
    slices = slice_blocks(w_slice[...])
    wsd[...] = slices.astype(BF16)
    wsb[...] = slices.T.astype(BF16)

    operands = (cells, cot, w_out, wxt, wft, wsb, wtb)
    forward_group(counts[0], operands, outs, tab, 1 - core)


def forward_own_kernel(counts, *refs):
    core = lax.rem(lax.axis_index("dom"), 2)
    forward_group(counts[0], refs[:7], refs[7:12], refs[12], core)


def narrow_add_kernel(mine, other, out):
    out[...] = (mine[...].astype(F32) + other[...].astype(F32)).astype(BF16)


def softmax_kernel(wsb, w_qkv, *refs):
    for k in range(3):
        refs[10][HEAD * k : HEAD * k + HEAD, :] = w_qkv[k].astype(F32).T

    def chunk(j, carry):
        at = chunk_of(j)
        for g in range(2):
            proj, stats = refs[2 * g : 2 * g + 2]
            tanhs, soft, slope = refs[4 + 3 * g : 7 + 3 * g]
            x = nn(wsb[...], proj[:, at])
            for k in range(4):
                rng = slice(SLICES * k, SLICES * k + SLICES)
                t = jnp.tanh(x[rng] * 0.1)
                tanhs[rng, at] = t
                slope[rng, at] = (1.0 - t * t) * stats[8 + k : 9 + k, at]
                soft[rng, at] = jnp.exp2(t * stats[k : k + 1, at]) * stats[24 + k : 25 + k, at]
        return carry

    lax.fori_loop(0, refs[0].shape[1] // CHUNK, chunk, 0)


def sum_blocks(ref, n):
    total = ref[0:n, :].astype(F32)
    for k in range(1, ref.shape[0] // n):
        total = total + ref[n * k : n * k + n, :].astype(F32)
    return total


def mix_kernel(w_qkv, turned, *refs):
    parts, out = refs[:-1], refs[-1]
    total = sum(part[...].astype(F32) for part in parts)
    numer = jnp.concatenate([total[0:32], total[64:96]], axis=1)
    d_mixed = jnp.concatenate([total[32:64], total[96:128]], axis=1)
    denom = jnp.concatenate([total[128:129], total[129:130]], axis=1) + 1e-05
    inverse = 1.0 / denom
    tokens = numer * inverse
    maps = [w_qkv[k].astype(F32) for k in range(3)]
    qkv = nn(turned[...], tokens, FINE)
    same = iota((128, 128), 0) // SLICES == iota((128, 128), 1) // SLICES
    pairs = []
    for i in range(2):
        q, key, val = (qkv[32 * k : 32 * k + 32, 128 * i : 128 * i + 128] for k in range(3))
        d_mix = d_mixed[:, 128 * i : 128 * i + 128]
        scores = nn(key.T, q, FINE) * (1.0 / math.sqrt(HEAD))
        t = jnp.tanh(scores * 0.1)
        powers = jnp.where(same, jnp.exp2(t * (10.0 * LOG2E)), 0.0)
        att = powers * (1.0 / jnp.sum(powers, axis=0, keepdims=True))
        d_att = nn(val.T, d_mix, FINE)
        inner = jnp.sum(att * d_att, axis=0, keepdims=True)
        d_scores = att * (d_att - inner) * ((1.0 - t * t) * (1.0 / math.sqrt(HEAD)))
        d_qkv = (nn(key, d_scores, FINE), nt(q, d_scores, FINE), nt(d_mix, att, FINE))
        pairs.append((nn(val, att, FINE), *d_qkv))
    mixed, *grads = (jnp.concatenate(both, axis=1) for both in zip(*pairs))
    d_tokens = sum(nn(m, g, FINE) for m, g in zip(maps, grads))
    d_numer = d_tokens * inverse
    d_denom = -jnp.sum(d_numer * tokens, axis=0, keepdims=True)
    out[0:32, :] = d_numer.astype(BF16).astype(F32)
    out[32:64, :] = mixed.astype(BF16).astype(F32)
    out[64:72, :] = jnp.broadcast_to(d_denom, (8, 256))
    out[72:104, 0:96] = nt(tokens, jnp.concatenate(grads, axis=0), FINE)
    out[72:104, 96:256] = jnp.zeros((32, 160), F32)


def backward_kernel(
    cells, cot, wsd, wtc, weights, proj, fd, stats, tanhs, softs, slopes, e,
    hid, dpf, payload,
    dlog, dtemp, lhs_h, lhs_w, dden,
):
    rows = cells.shape[0]
    diag64 = iota((256, 256), 0) // 64 == iota((256, 256), 1) // 64
    diag32 = iota((128, 256), 0) // 32 == iota((128, 256), 1) // 64
    both = jnp.where(diag64, jnp.concatenate([e[0:64, :]] * 4, axis=0), 0.0)
    lhs_w[...] = both.T.astype(BF16)
    for i in range(2):
        part = jnp.concatenate([e[32 - 32 * i : 64 - 32 * i, :]] * 4, axis=0)
        lhs_h[128 * i : 128 * i + 128, :] = jnp.where(diag32, part, 0.0).astype(BF16)
    dden[...] = jnp.broadcast_to(e[64:72, :].T[:, 0:1], (256, 128))
    dtemp[...] = jnp.zeros(dtemp.shape, F32)

    def chunk(j, carry):
        at = chunk_of(j)
        hf = nn(lhs_h[...], weights[:, at])
        hid[:, at] = hf[0:128].astype(BF16)
        dpf[128:256, at] = hf[128:256].astype(BF16)
        dw = nn(lhs_w[...], fd[:, at])
        outer = []
        for k in range(4):
            rng = slice(SLICES * k, SLICES * k + SLICES)
            t = tanhs[rng, at]
            soft = softs[rng, at]
            d = dw[rng] + jnp.concatenate([dden[rng, :]] * (CHUNK // 128), axis=1)
            inner = jnp.sum(soft * d, axis=0, keepdims=True)
            ds = soft * (d - inner)
            dlog[rng, at] = (ds * slopes[rng, at]).astype(BF16)
            dt = jnp.sum(ds * t, axis=0, keepdims=True) * stats[16 + k : 17 + k, at]
            dt = dt.astype(BF16).astype(F32)
            dtemp[k : k + 1, at] = dt
            outer.append(wtc[HEAD * k : HEAD * k + HEAD, k : k + 1] * dt)
        dp = nn(wsd[...], dlog[:, at]) + jnp.concatenate(outer, axis=0)
        dpf[0:128, at] = dp.astype(BF16)
        return carry

    lax.fori_loop(0, rows // CHUNK, chunk, 0)
    d_out = nn(hid[...], cot[...]).astype(BF16)
    d_in = nn(dpf[...], cells[...]).astype(BF16)
    for i, grad in enumerate((d_out, d_in[0:128], d_in[128:256])):
        payload[256 * i : 256 * i + 128, :] = grad[:, 0:128]
        payload[256 * i + 128 : 256 * i + 256, :] = grad[:, 128:256]
    every = nt(proj[...], dlog[...])
    even = every[0:32, 0:128] + every[64:96, 128:256]
    odd = every[32:64, 0:128] + every[96:128, 128:256]
    d_slice = jnp.where(iota((HEAD, 128), 1) < SLICES, even, odd)
    d_temp = nt(dtemp[...].astype(BF16), proj[...])
    here = iota((HEADS, 128), 0) == iota((HEADS, 128), 1) // HEAD
    d_temp = jnp.sum(jnp.where(here, d_temp, 0.0), axis=0, keepdims=True)
    d_temp = jnp.broadcast_to(d_temp, (8, 128))
    payload[768:ROWS2, :] = jnp.concatenate([d_slice, d_temp], axis=0).astype(BF16)
    payload[ROWS2:, :] = jnp.zeros((payload.shape[0] - ROWS2, 128), BF16)


def write_rows(out, stage, sems, product, copies=()):
    copies = list(copies)
    for j in range(out.shape[0] // WRITE):
        at = pl.ds(j * WRITE, WRITE)
        stage[at, :] = product(at).T.astype(BF16)
        copies.append(pltpu.make_async_copy(stage.at[at, :], out.at[at, :], sems.at[j]))
        copies[-1].start()
    for copy in copies:
        copy.wait()


def result_kernel(
    scale, own, far, w_out, e_own, e_far, out, grad_qkv, qkv, sem, table, stage, sems,
):
    core = lax.rem(lax.axis_index("dom"), 2)
    for k in range(3):
        block = slice(32 * k, 32 * k + 32)
        qkv[k] = (e_own[72:104, block] + e_far[72:104, block]) * scale
    copy = pltpu.make_async_copy(qkv, grad_qkv, sem.at[0])
    copy.start()
    order = [w_out[group_rows(g), :] for g in (core, 1 - core)]
    table[...] = jnp.concatenate(order, axis=0).T

    def product(at):
        return nn(table[...], jnp.concatenate([own[:, at], far[:, at]], axis=0))

    write_rows(out, stage, sems, product, [copy])


def grad_cells_kernel(own, far, w_x, w_fx, out, table, stage, sems):
    core = lax.rem(lax.axis_index("dom"), 2)
    for i, g in enumerate((core, 1 - core)):
        table[:, 256 * i : 256 * i + 128] = w_x[:, group_rows(g)]
        table[:, 256 * i + 128 : 256 * i + 256] = w_fx[:, group_rows(g)]

    def product(at):
        return nn(table[...], jnp.concatenate([own[:, at], far[:, at]], axis=0))

    write_rows(out, stage, sems, product)


def place_kernel(mine, other, *refs):
    outs, (d_x, d_fx, d_slice, d_temp, d_out), sems = refs[:5], refs[5:10], refs[10]
    core = lax.rem(lax.axis_index("dom"), 2)
    copies = []

    def copy_out(i):
        copies.append(pltpu.make_async_copy(refs[5 + i], outs[i], sems.at[i]))
        copies[-1].start()

    parts = ((mine, group_rows(core)), (other, group_rows(1 - core)))
    for ref, at in parts:
        d_out[at, 0:128] = ref[0:128, :].astype(F32)
        d_out[at, 128:256] = ref[128:256, :].astype(F32)
    copy_out(4)
    for i, grad in enumerate((d_x, d_fx)):
        first = 256 * i + 256
        for ref, at in parts:
            grad[0:128, at] = ref[first : first + 128, :].astype(F32).T
            grad[128:256, at] = ref[first + 128 : first + 256, :].astype(F32).T
        copy_out(i)
    small = mine[768:ROWS2, :].astype(F32) + other[768:ROWS2, :].astype(F32)
    rows = small[0:32] + pltpu.roll(small[0:32], 64, 1)
    d_slice[...] = rows[:, 0:SLICES]
    copy_out(2)
    v = small[32:40]
    v = v + pltpu.roll(v, 64, 1)
    v = v + pltpu.roll(v, 32, 1)
    d_temp[...] = v[0:1, 0:HEAD]
    copy_out(3)
    for copy in copies:
        copy.wait()


VMEM = pl.BlockSpec(memory_space=pltpu.VMEM)
SMEM = pl.BlockSpec(memory_space=pltpu.SMEM)
HBM = pl.BlockSpec(memory_space=pltpu.HBM)


def call(kernel, shapes, args, scratch=(), name=None, ins=None, outs=None, flops=0, flags=None):
    scratch = [pltpu.VMEM(*s) if isinstance(s, tuple) else s for s in scratch]
    estimate = pl.CostEstimate(flops=flops, bytes_accessed=0, transcendentals=0)
    return pl.pallas_call(
        kernel,
        out_shape=[jax.ShapeDtypeStruct(s, d) for s, d in shapes],
        in_specs=ins or [VMEM] * len(args),
        out_specs=outs or [VMEM] * len(shapes),
        scratch_shapes=scratch,
        name=name,
        cost_estimate=estimate if flops else None,
        compiler_params=pltpu.CompilerParams(vmem_limit_bytes=24 << 20, flags=flags),
    )(*args)


def body(devices, cells, counts, w_x, w_fx, w_slice, w_temp, w_qkv, w_out, cotangent):
    rows = cells.shape[0]
    peers = devices // 2
    groups = [list(range(c, devices, 2)) for c in range(2)]
    scale = 1.0 / math.sqrt(rows * devices)
    temp = w_temp.reshape(1, HEAD)
    hm = HEADS * SLICES

    def swap(x, mask):
        return lax.ppermute(x, "dom", [(i, i ^ mask) for i in range(devices)])

    def exchange(x):
        return lax.all_to_all(x, "dom", 0, 0, axis_index_groups=groups, tiled=True)

    hgm = hm // 2
    grouped = [
        ((hgm, rows), BF16),
        ((WIDTH // 2, rows), BF16),
        ((WIDTH, rows), BF16),
        ((32, rows), F32),
        ((ROWS1, 128), F32),
    ]
    local = call(
        forward_far_kernel,
        grouped
        + [
            ((WIDTH, WIDTH), BF16),
            ((WIDTH, WIDTH), BF16),
            ((256, 128), BF16),
            ((128, 256), BF16),
            ((HEADS, 128), BF16),
            ((128, HEADS), F32),
            ((rows, WIDTH), BF16),
            ((rows, WIDTH), BF16),
            ((WIDTH, WIDTH), BF16),
            ((WIDTH, WIDTH), BF16),
            ((WIDTH, WIDTH), BF16),
        ],
        (counts,)
        + tuple(
            pltpu.with_memory_space_constraint(x, pltpu.HBM)
            for x in (cells, cotangent, w_x, w_fx, w_slice, temp, w_out)
        ),
        scratch=[
            ((HEAD, SLICES), BF16),
            ((1, HEAD), BF16),
            pltpu.SemaphoreType.DMA((5,)),
            pltpu.SemaphoreType.DMA((2, rows // CHUNK)),
            ((256, 256), BF16),
        ],
        ins=[SMEM] + [HBM] * 7,
        name="forward_far",
    )
    far = local[:4]
    send = local[4]
    wxt, wft, wsb, wsd, wtb, wtc, cells, cotangent, w_x, w_fx, w_out = local[5:]
    other = swap(send, 1)
    *own, keep = call(
        forward_own_kernel,
        grouped,
        (counts, cells, cotangent, w_out, wxt, wft, wsb, wtb),
        scratch=[((256, 256), BF16)],
        ins=[SMEM] + [VMEM] * 7,
        name="forward_own",
        flops=6 * rows * WIDTH * WIDTH,
    )
    other, keep = lax.optimization_barrier((other, keep))
    part = ((ROWS1, 128), BF16)
    (total,) = call(narrow_add_kernel, [part], (keep, other), name="narrow")
    near = [2**b for b in range(1, devices.bit_length() - 3)]
    last = [devices // 4 * k for k in (1, 2, 3)]
    again = None
    for mask in near:
        other = swap(total, mask)
        if again is None:
            again = call(
                softmax_kernel,
                [((hgm, rows), F32)] * 6 + [((3 * HEAD, HEAD), F32)],
                (wsb, w_qkv, own[1], own[3], far[1], far[3]),
                name="softmax",
                flops=2 * rows * hm * 128,
            )
            other, *again = lax.optimization_barrier((other, *again))
        (total,) = call(narrow_add_kernel, [part], (total, other), name="near")
    parts = [total] + [swap(total, mask) for mask in last]
    (mine,) = call(mix_kernel, [((104, 256), F32)], (w_qkv, again[6], *parts), name="mix")
    other = swap(mine, 1)
    chunk = -(-ROWS2 // peers)
    chunk = -(-chunk // 8) * 8
    half = chunk * peers
    grads = [
        ((WIDTH // 2, rows), BF16),
        ((WIDTH, rows), BF16),
        ((half, 128), BF16),
    ]
    scratch = [
        ((hgm, rows), BF16),
        ((8, rows), F32),
        ((256, 256), BF16),
        ((256, 256), BF16),
        ((hgm, 128), F32),
    ]
    hid_own, dpf_own, keep = call(
        backward_kernel,
        grads,
        (cells, cotangent, wsd, wtc, *own, *again[:3], mine),
        scratch=scratch,
        name="backward_own",
        flops=8 * rows * WIDTH * WIDTH,
    )
    other, keep = lax.optimization_barrier((other, keep))
    maps = other
    hid_far, dpf_far, send = call(
        backward_kernel,
        grads,
        (cells, cotangent, wsd, wtc, *far, *again[3:6], maps),
        scratch=scratch,
        name="backward_far",
    )
    other = swap(send, 1)
    staging = [((rows, WIDTH), BF16), pltpu.SemaphoreType.DMA((rows // WRITE,))]
    result, grad_qkv = call(
        functools.partial(result_kernel, scale),
        [((rows, WIDTH), BF16), ((3, HEAD, HEAD), F32)],
        (hid_own, hid_far, w_out, mine, maps),
        scratch=[((3, HEAD, HEAD), F32), pltpu.SemaphoreType.DMA((1,)), ((WIDTH, WIDTH), BF16)]
        + staging,
        outs=[HBM, HBM],
        name="result",
        flops=2 * rows * WIDTH * WIDTH,
    )
    other, result = lax.optimization_barrier((other, result))
    (grad_cells,) = call(
        grad_cells_kernel,
        [((rows, WIDTH), BF16)],
        (dpf_own, dpf_far, w_x, w_fx),
        scratch=[((WIDTH, 2 * WIDTH), BF16)] + staging,
        outs=[HBM],
        name="grad_cells",
        flops=4 * rows * WIDTH * WIDTH,
    )
    (summed,) = call(narrow_add_kernel, [((half, 128), BF16)], (keep, other), name="pair_add")
    parts = exchange(summed)

    def gather(parts_ref, out):
        total = (sum_blocks(parts_ref, chunk) * scale).astype(BF16)
        for k in range(peers):
            out[chunk * k : chunk * k + chunk, :] = total

    (spread,) = call(gather, [((half, 128), BF16)], (parts,), name="gather")
    mine = exchange(spread)
    other = swap(mine, 1)
    shapes = [
        ((WIDTH, WIDTH), F32),
        ((WIDTH, WIDTH), F32),
        ((HEAD, SLICES), F32),
        ((1, HEAD), F32),
        ((WIDTH, WIDTH), F32),
    ]
    d_x, d_fx, d_slice, d_temp, d_out = call(
        place_kernel,
        shapes,
        (mine, other),
        scratch=[*shapes, pltpu.SemaphoreType.DMA((5,))],
        outs=[HBM] * 5,
        name="place",
    )
    return result, grad_cells, d_x, d_fx, d_slice, d_temp.reshape(HEAD), grad_qkv, d_out


def solution(mesh):
    cell = P(("groups", "dom"), None)
    return jax.shard_map(
        functools.partial(body, mesh.shape["dom"]),
        mesh=mesh,
        in_specs=(cell, P(("groups", "dom")), P(), P(), P(), P(), P(), P(), cell),
        out_specs=(
            cell,
            cell,
            P("groups", None),
            P("groups", None),
            P("groups", None),
            P("groups"),
            P("groups", None, None),
            P("groups", None),
        ),
        check_vma=False,
    )
```

```python
import functools
import math

import jax
import jax.numpy as jnp
from jax import lax
from jax.experimental import pallas as pl
from jax.experimental.pallas import tpu as pltpu
from jax.sharding import PartitionSpec as P

F32 = jnp.float32
BF16 = jnp.bfloat16
FINE = lax.Precision.HIGH
HEADS = 8
SLICES = 64
HEAD = 32
WIDTH = HEADS * HEAD
ROWS1 = 136
ROWS2 = 808
LOG2E = math.log2(math.e)
CHUNK = 1024
WRITE = 512


def nn(a, b, precision=None):
    return lax.dot_general(
        a, b, (((1,), (0,)), ((), ())), precision=precision, preferred_element_type=F32
    )


def nt(a, b, precision=None):
    return lax.dot_general(
        a, b, (((1,), (1,)), ((), ())), precision=precision, preferred_element_type=F32
    )


def iota(shape, dim):
    return lax.broadcasted_iota(jnp.int32, shape, dim)


def slice_blocks(w_slice):
    tall = jnp.concatenate([w_slice] * 4, axis=0)
    pick = (iota((SLICES, 256), 1) % SLICES == iota((SLICES, 256), 0)).astype(BF16)
    wide = nn(tall, pick)
    same = iota((128, 256), 0) // HEAD == iota((128, 256), 1) // SLICES
    return jnp.where(same, wide, 0.0)


def temp_blocks(w_temp):
    pick = (iota((HEAD, 128), 1) % HEAD == iota((HEAD, 128), 0)).astype(BF16)
    wide = nn(jnp.broadcast_to(w_temp, (HEADS, HEAD)), pick)
    same = iota((HEADS, 128), 0) == iota((HEADS, 128), 1) // HEAD
    return jnp.where(same, wide, 0.0).astype(BF16)


def group_rows(group):
    return pl.ds(pl.multiple_of(group * 128, 128), 128)


def chunk_of(j):
    return pl.ds(pl.multiple_of(j * CHUNK, CHUNK), CHUNK)


def forward_group(count, operands, outs, tab, group):
    cells, cot, w_out, wxt, wft, wsb, wtb = operands
    weights, proj, fd, stats, payload = outs
    rows = cells.shape[0]
    mine = group_rows(group)
    tab[0:128, :] = wxt[mine, :]
    tab[128:256, :] = wft[mine, :]

    def chunk(j, carry):
        at = chunk_of(j)
        both = nt(tab[...], cells[at, :]).astype(BF16)
        projected = both[0:128]
        proj[:, at] = projected
        dhid = nt(w_out[mine, :], cot[at, :]).astype(BF16)
        for k in range(4):
            fd[64 * k : 64 * k + 32, at] = both[128 + 32 * k : 160 + 32 * k]
            fd[64 * k + 32 : 64 * k + 64, at] = dhid[32 * k : 32 * k + 32]
        lin = nn(wtb[...], projected)
        e = jnp.exp(-jnp.abs(lin))
        soft = jnp.maximum(lin, 0.0) + jnp.log(1.0 + e)
        inv = 1.0 / (0.5 + soft)
        sig = jnp.where(lin >= 0, 1.0, e) / (1.0 + e)
        a = inv * (10.0 * LOG2E)
        live = jnp.where(j * CHUNK + iota((1, CHUNK), 1) < count, 1.0, 0.0)
        norms = []
        x = nn(wsb[...], projected)
        for k in range(4):
            t = jnp.tanh(x[SLICES * k : SLICES * k + SLICES] * 0.1)
            p = jnp.exp2(t * a[k : k + 1])
            r = live / jnp.sum(p, axis=0, keepdims=True)
            weights[SLICES * k : SLICES * k + SLICES, at] = (p * r).astype(BF16)
            norms.append(r)
        stats[0:8, at] = a
        stats[8:16, at] = inv
        stats[16:24, at] = inv * inv * sig * (-10.0)
        stats[24:32, at] = jnp.concatenate(norms + norms, axis=0)
        return carry

    lax.fori_loop(0, rows // CHUNK, chunk, 0)
    ones = jnp.ones((16, rows), BF16)
    first = iota((64, 128), 1) < SLICES
    for q in range(2):
        pair = slice(128 * q, 128 * q + 128)
        out = nt(jnp.concatenate([fd[pair, :], ones], axis=0), weights[pair, :])
        payload[64 * q : 64 * q + 64, :] = jnp.where(first, out[0:64], out[64:128])
        payload[128 + q : 129 + q, :] = out[128:129]
    payload[130:136, :] = jnp.zeros((6, 128), F32)


def forward_far_kernel(counts, cells_hbm, cot_hbm, *refs):
    hbm, refs = refs[:5], refs[5:]
    outs, refs = refs[:5], refs[5:]
    (wxt, wft, wsb, wsd, wtb, wtc, cells, cot, w_x, w_fx, w_out), refs = refs[:11], refs[11:]
    w_slice, w_temp, small, big, tab = refs
    core = lax.rem(lax.axis_index("dom"), 2)

    def load(source, target, slot, j):
        at = chunk_of(j)
        return pltpu.make_async_copy(source.at[at, :], target.at[at, :], big.at[slot, j])

    tables = [
        pltpu.make_async_copy(source, target, small.at[i])
        for i, (source, target) in enumerate(zip(hbm, (w_x, w_fx, w_slice, w_temp, w_out)))
    ]
    for table in tables:
        table.start()
    for j in range(cells.shape[0] // CHUNK):
        load(cells_hbm, cells, 0, j).start()
        load(cot_hbm, cot, 1, j).start()
    for table in tables:
        table.wait()
    for j in range(cells.shape[0] // CHUNK):
        load(cells_hbm, cells, 0, j).wait()
        load(cot_hbm, cot, 1, j).wait()
    blocks = temp_blocks(w_temp[...])
    wtb[...] = blocks
    wtc[...] = blocks.astype(F32).T
    wxt[...] = w_x[...].T
    wft[...] = w_fx[...].T
    slices = slice_blocks(w_slice[...])
    wsd[...] = slices.astype(BF16)
    wsb[...] = slices.T.astype(BF16)

    operands = (cells, cot, w_out, wxt, wft, wsb, wtb)
    forward_group(counts[0], operands, outs, tab, 1 - core)


def forward_own_kernel(counts, *refs):
    core = lax.rem(lax.axis_index("dom"), 2)
    forward_group(counts[0], refs[:7], refs[7:12], refs[12], core)


def narrow_add_kernel(mine, other, out):
    out[...] = (mine[...].astype(F32) + other[...].astype(F32)).astype(BF16)


def softmax_kernel(wsb, w_qkv, *refs):
    for k in range(3):
        refs[10][HEAD * k : HEAD * k + HEAD, :] = w_qkv[k].astype(F32).T

    def chunk(j, carry):
        at = chunk_of(j)
        for g in range(2):
            proj, stats = refs[2 * g : 2 * g + 2]
            tanhs, soft, slope = refs[4 + 3 * g : 7 + 3 * g]
            x = nn(wsb[...], proj[:, at])
            for k in range(4):
                rng = slice(SLICES * k, SLICES * k + SLICES)
                t = jnp.tanh(x[rng] * 0.1)
                tanhs[rng, at] = t
                slope[rng, at] = (1.0 - t * t) * stats[8 + k : 9 + k, at]
                soft[rng, at] = jnp.exp2(t * stats[k : k + 1, at]) * stats[24 + k : 25 + k, at]
        return carry

    lax.fori_loop(0, refs[0].shape[1] // CHUNK, chunk, 0)


def sum_blocks(ref, n):
    total = ref[0:n, :].astype(F32)
    for k in range(1, ref.shape[0] // n):
        total = total + ref[n * k : n * k + n, :].astype(F32)
    return total


def mix_kernel(w_qkv, turned, *refs):
    parts, out = refs[:-1], refs[-1]
    total = sum(part[...].astype(F32) for part in parts)
    numer = jnp.concatenate([total[0:32], total[64:96]], axis=1)
    d_mixed = jnp.concatenate([total[32:64], total[96:128]], axis=1)
    denom = jnp.concatenate([total[128:129], total[129:130]], axis=1) + 1e-05
    inverse = 1.0 / denom
    tokens = numer * inverse
    maps = [w_qkv[k].astype(F32) for k in range(3)]
    qkv = nn(turned[...], tokens, FINE)
    same = iota((128, 128), 0) // SLICES == iota((128, 128), 1) // SLICES
    pairs = []
    for i in range(2):
        q, key, val = (qkv[32 * k : 32 * k + 32, 128 * i : 128 * i + 128] for k in range(3))
        d_mix = d_mixed[:, 128 * i : 128 * i + 128]
        scores = nn(key.T, q, FINE) * (1.0 / math.sqrt(HEAD))
        t = jnp.tanh(scores * 0.1)
        powers = jnp.where(same, jnp.exp2(t * (10.0 * LOG2E)), 0.0)
        att = powers * (1.0 / jnp.sum(powers, axis=0, keepdims=True))
        d_att = nn(val.T, d_mix, FINE)
        inner = jnp.sum(att * d_att, axis=0, keepdims=True)
        d_scores = att * (d_att - inner) * ((1.0 - t * t) * (1.0 / math.sqrt(HEAD)))
        d_qkv = (nn(key, d_scores, FINE), nt(q, d_scores, FINE), nt(d_mix, att, FINE))
        pairs.append((nn(val, att, FINE), *d_qkv))
    mixed, *grads = (jnp.concatenate(both, axis=1) for both in zip(*pairs))
    d_tokens = sum(nn(m, g, FINE) for m, g in zip(maps, grads))
    d_numer = d_tokens * inverse
    d_denom = -jnp.sum(d_numer * tokens, axis=0, keepdims=True)
    out[0:32, :] = d_numer.astype(BF16).astype(F32)
    out[32:64, :] = mixed.astype(BF16).astype(F32)
    out[64:72, :] = jnp.broadcast_to(d_denom, (8, 256))
    out[72:104, 0:96] = nt(tokens, jnp.concatenate(grads, axis=0), FINE)
    out[72:104, 96:256] = jnp.zeros((32, 160), F32)


def backward_kernel(
    cells, cot, wsd, wtc, weights, proj, fd, stats, tanhs, softs, slopes, e,
    hid, dpf, payload,
    dlog, dtemp, lhs_h, lhs_w, dden,
):
    rows = cells.shape[0]
    diag64 = iota((256, 256), 0) // 64 == iota((256, 256), 1) // 64
    diag32 = iota((128, 256), 0) // 32 == iota((128, 256), 1) // 64
    both = jnp.where(diag64, jnp.concatenate([e[0:64, :]] * 4, axis=0), 0.0)
    lhs_w[...] = both.T.astype(BF16)
    for i in range(2):
        part = jnp.concatenate([e[32 - 32 * i : 64 - 32 * i, :]] * 4, axis=0)
        lhs_h[128 * i : 128 * i + 128, :] = jnp.where(diag32, part, 0.0).astype(BF16)
    dden[...] = jnp.broadcast_to(e[64:72, :].T[:, 0:1], (256, 128))
    dtemp[...] = jnp.zeros(dtemp.shape, F32)

    def chunk(j, carry):
        at = chunk_of(j)
        hf = nn(lhs_h[...], weights[:, at])
        hid[:, at] = hf[0:128].astype(BF16)
        dpf[128:256, at] = hf[128:256].astype(BF16)
        dw = nn(lhs_w[...], fd[:, at])
        outer = []
        for k in range(4):
            rng = slice(SLICES * k, SLICES * k + SLICES)
            t = tanhs[rng, at]
            soft = softs[rng, at]
            d = dw[rng] + jnp.concatenate([dden[rng, :]] * (CHUNK // 128), axis=1)
            inner = jnp.sum(soft * d, axis=0, keepdims=True)
            ds = soft * (d - inner)
            dlog[rng, at] = (ds * slopes[rng, at]).astype(BF16)
            dt = jnp.sum(ds * t, axis=0, keepdims=True) * stats[16 + k : 17 + k, at]
            dt = dt.astype(BF16).astype(F32)
            dtemp[k : k + 1, at] = dt
            outer.append(wtc[HEAD * k : HEAD * k + HEAD, k : k + 1] * dt)
        dp = nn(wsd[...], dlog[:, at]) + jnp.concatenate(outer, axis=0)
        dpf[0:128, at] = dp.astype(BF16)
        return carry

    lax.fori_loop(0, rows // CHUNK, chunk, 0)
    d_out = nn(hid[...], cot[...]).astype(BF16)
    d_in = nn(dpf[...], cells[...]).astype(BF16)
    for i, grad in enumerate((d_out, d_in[0:128], d_in[128:256])):
        payload[256 * i : 256 * i + 128, :] = grad[:, 0:128]
        payload[256 * i + 128 : 256 * i + 256, :] = grad[:, 128:256]
    every = nt(proj[...], dlog[...])
    even = every[0:32, 0:128] + every[64:96, 128:256]
    odd = every[32:64, 0:128] + every[96:128, 128:256]
    d_slice = jnp.where(iota((HEAD, 128), 1) < SLICES, even, odd)
    d_temp = nt(dtemp[...].astype(BF16), proj[...])
    here = iota((HEADS, 128), 0) == iota((HEADS, 128), 1) // HEAD
    d_temp = jnp.sum(jnp.where(here, d_temp, 0.0), axis=0, keepdims=True)
    d_temp = jnp.broadcast_to(d_temp, (8, 128))
    payload[768:ROWS2, :] = jnp.concatenate([d_slice, d_temp], axis=0).astype(BF16)
    payload[ROWS2:, :] = jnp.zeros((payload.shape[0] - ROWS2, 128), BF16)


def write_rows(out, stage, sems, product, copies=()):
    copies = list(copies)
    for j in range(out.shape[0] // WRITE):
        at = pl.ds(j * WRITE, WRITE)
        stage[at, :] = product(at).T.astype(BF16)
        copies.append(pltpu.make_async_copy(stage.at[at, :], out.at[at, :], sems.at[j]))
        copies[-1].start()
    for copy in copies:
        copy.wait()


def result_kernel(
    scale, own, far, w_out, e_own, e_far, out, grad_qkv, qkv, sem, table, stage, sems,
):
    core = lax.rem(lax.axis_index("dom"), 2)
    for k in range(3):
        block = slice(32 * k, 32 * k + 32)
        qkv[k] = (e_own[72:104, block] + e_far[72:104, block]) * scale
    copy = pltpu.make_async_copy(qkv, grad_qkv, sem.at[0])
    copy.start()
    order = [w_out[group_rows(g), :] for g in (core, 1 - core)]
    table[...] = jnp.concatenate(order, axis=0).T

    def product(at):
        return nn(table[...], jnp.concatenate([own[:, at], far[:, at]], axis=0))

    write_rows(out, stage, sems, product, [copy])


def grad_cells_kernel(own, far, w_x, w_fx, out, table, stage, sems):
    core = lax.rem(lax.axis_index("dom"), 2)
    for i, g in enumerate((core, 1 - core)):
        table[:, 256 * i : 256 * i + 128] = w_x[:, group_rows(g)]
        table[:, 256 * i + 128 : 256 * i + 256] = w_fx[:, group_rows(g)]

    def product(at):
        return nn(table[...], jnp.concatenate([own[:, at], far[:, at]], axis=0))

    write_rows(out, stage, sems, product)


def place_kernel(mine, other, *refs):
    outs, (d_x, d_fx, d_slice, d_temp, d_out), sems = refs[:5], refs[5:10], refs[10]
    core = lax.rem(lax.axis_index("dom"), 2)
    copies = []

    def copy_out(i):
        copies.append(pltpu.make_async_copy(refs[5 + i], outs[i], sems.at[i]))
        copies[-1].start()

    parts = ((mine, group_rows(core)), (other, group_rows(1 - core)))
    for ref, at in parts:
        d_out[at, 0:128] = ref[0:128, :].astype(F32)
        d_out[at, 128:256] = ref[128:256, :].astype(F32)
    copy_out(4)
    for i, grad in enumerate((d_x, d_fx)):
        first = 256 * i + 256
        for ref, at in parts:
            grad[0:128, at] = ref[first : first + 128, :].astype(F32).T
            grad[128:256, at] = ref[first + 128 : first + 256, :].astype(F32).T
        copy_out(i)
    small = mine[768:ROWS2, :].astype(F32) + other[768:ROWS2, :].astype(F32)
    rows = small[0:32] + pltpu.roll(small[0:32], 64, 1)
    d_slice[...] = rows[:, 0:SLICES]
    copy_out(2)
    v = small[32:40]
    v = v + pltpu.roll(v, 64, 1)
    v = v + pltpu.roll(v, 32, 1)
    d_temp[...] = v[0:1, 0:HEAD]
    copy_out(3)
    for copy in copies:
        copy.wait()


VMEM = pl.BlockSpec(memory_space=pltpu.VMEM)
SMEM = pl.BlockSpec(memory_space=pltpu.SMEM)
HBM = pl.BlockSpec(memory_space=pltpu.HBM)


def call(kernel, shapes, args, scratch=(), name=None, ins=None, outs=None, flops=0, flags=None):
    scratch = [pltpu.VMEM(*s) if isinstance(s, tuple) else s for s in scratch]
    estimate = pl.CostEstimate(flops=flops, bytes_accessed=0, transcendentals=0)
    return pl.pallas_call(
        kernel,
        out_shape=[jax.ShapeDtypeStruct(s, d) for s, d in shapes],
        in_specs=ins or [VMEM] * len(args),
        out_specs=outs or [VMEM] * len(shapes),
        scratch_shapes=scratch,
        name=name,
        cost_estimate=estimate if flops else None,
        compiler_params=pltpu.CompilerParams(vmem_limit_bytes=24 << 20, flags=flags),
    )(*args)


def body(devices, cells, counts, w_x, w_fx, w_slice, w_temp, w_qkv, w_out, cotangent):
    rows = cells.shape[0]
    peers = devices // 2
    groups = [list(range(c, devices, 2)) for c in range(2)]
    scale = 1.0 / math.sqrt(rows * devices)
    temp = w_temp.reshape(1, HEAD)
    hm = HEADS * SLICES

    def swap(x, mask):
        return lax.ppermute(x, "dom", [(i, i ^ mask) for i in range(devices)])

    def exchange(x):
        return lax.all_to_all(x, "dom", 0, 0, axis_index_groups=groups, tiled=True)

    hgm = hm // 2
    grouped = [
        ((hgm, rows), BF16),
        ((WIDTH // 2, rows), BF16),
        ((WIDTH, rows), BF16),
        ((32, rows), F32),
        ((ROWS1, 128), F32),
    ]
    local = call(
        forward_far_kernel,
        grouped
        + [
            ((WIDTH, WIDTH), BF16),
            ((WIDTH, WIDTH), BF16),
            ((256, 128), BF16),
            ((128, 256), BF16),
            ((HEADS, 128), BF16),
            ((128, HEADS), F32),
            ((rows, WIDTH), BF16),
            ((rows, WIDTH), BF16),
            ((WIDTH, WIDTH), BF16),
            ((WIDTH, WIDTH), BF16),
            ((WIDTH, WIDTH), BF16),
        ],
        (counts,)
        + tuple(
            pltpu.with_memory_space_constraint(x, pltpu.HBM)
            for x in (cells, cotangent, w_x, w_fx, w_slice, temp, w_out)
        ),
        scratch=[
            ((HEAD, SLICES), BF16),
            ((1, HEAD), BF16),
            pltpu.SemaphoreType.DMA((5,)),
            pltpu.SemaphoreType.DMA((2, rows // CHUNK)),
            ((256, 256), BF16),
        ],
        ins=[SMEM] + [HBM] * 7,
        name="forward_far",
    )
    far = local[:4]
    send = local[4]
    wxt, wft, wsb, wsd, wtb, wtc, cells, cotangent, w_x, w_fx, w_out = local[5:]
    other = swap(send, 1)
    *own, keep = call(
        forward_own_kernel,
        grouped,
        (counts, cells, cotangent, w_out, wxt, wft, wsb, wtb),
        scratch=[((256, 256), BF16)],
        ins=[SMEM] + [VMEM] * 7,
        name="forward_own",
        flops=6 * rows * WIDTH * WIDTH,
    )
    other, keep = lax.optimization_barrier((other, keep))
    part = ((ROWS1, 128), BF16)
    (total,) = call(narrow_add_kernel, [part], (keep, other), name="narrow")
    near = [2**b for b in range(1, devices.bit_length() - 3)]
    last = [devices // 4 * k for k in (1, 2, 3)]
    again = None
    for mask in near:
        other = swap(total, mask)
        if again is None:
            again = call(
                softmax_kernel,
                [((hgm, rows), F32)] * 6 + [((3 * HEAD, HEAD), F32)],
                (wsb, w_qkv, own[1], own[3], far[1], far[3]),
                name="softmax",
                flops=2 * rows * hm * 128,
            )
            other, *again = lax.optimization_barrier((other, *again))
        (total,) = call(narrow_add_kernel, [part], (total, other), name="near")
    parts = [total] + [swap(total, mask) for mask in last]
    (mine,) = call(mix_kernel, [((104, 256), F32)], (w_qkv, again[6], *parts), name="mix")
    other = swap(mine, 1)
    chunk = -(-ROWS2 // peers)
    chunk = -(-chunk // 8) * 8
    half = chunk * peers
    grads = [
        ((WIDTH // 2, rows), BF16),
        ((WIDTH, rows), BF16),
        ((half, 128), BF16),
    ]
    scratch = [
        ((hgm, rows), BF16),
        ((8, rows), F32),
        ((256, 256), BF16),
        ((256, 256), BF16),
        ((hgm, 128), F32),
    ]
    hid_own, dpf_own, keep = call(
        backward_kernel,
        grads,
        (cells, cotangent, wsd, wtc, *own, *again[:3], mine),
        scratch=scratch,
        name="backward_own",
        flops=8 * rows * WIDTH * WIDTH,
    )
    other, keep = lax.optimization_barrier((other, keep))
    maps = other
    hid_far, dpf_far, send = call(
        backward_kernel,
        grads,
        (cells, cotangent, wsd, wtc, *far, *again[3:6], maps),
        scratch=scratch,
        name="backward_far",
    )
    other = swap(send, 1)
    staging = [((rows, WIDTH), BF16), pltpu.SemaphoreType.DMA((rows // WRITE,))]
    result, grad_qkv = call(
        functools.partial(result_kernel, scale),
        [((rows, WIDTH), BF16), ((3, HEAD, HEAD), F32)],
        (hid_own, hid_far, w_out, mine, maps),
        scratch=[((3, HEAD, HEAD), F32), pltpu.SemaphoreType.DMA((1,)), ((WIDTH, WIDTH), BF16)]
        + staging,
        outs=[HBM, HBM],
        name="result",
        flops=2 * rows * WIDTH * WIDTH,
    )
    other, result = lax.optimization_barrier((other, result))
    (grad_cells,) = call(
        grad_cells_kernel,
        [((rows, WIDTH), BF16)],
        (dpf_own, dpf_far, w_x, w_fx),
        scratch=[((WIDTH, 2 * WIDTH), BF16)] + staging,
        outs=[HBM],
        name="grad_cells",
        flops=4 * rows * WIDTH * WIDTH,
    )
    (summed,) = call(narrow_add_kernel, [((half, 128), BF16)], (keep, other), name="pair_add")
    parts = exchange(summed)

    def gather(parts_ref, out):
        total = (sum_blocks(parts_ref, chunk) * scale).astype(BF16)
        for k in range(peers):
            out[chunk * k : chunk * k + chunk, :] = total

    (spread,) = call(gather, [((half, 128), BF16)], (parts,), name="gather")
    mine = exchange(spread)
    other = swap(mine, 1)
    shapes = [
        ((WIDTH, WIDTH), F32),
        ((WIDTH, WIDTH), F32),
        ((HEAD, SLICES), F32),
        ((1, HEAD), F32),
        ((WIDTH, WIDTH), F32),
    ]
    d_x, d_fx, d_slice, d_temp, d_out = call(
        place_kernel,
        shapes,
        (mine, other),
        scratch=[*shapes, pltpu.SemaphoreType.DMA((5,))],
        outs=[HBM] * 5,
        name="place",
    )
    return result, grad_cells, d_x, d_fx, d_slice, d_temp.reshape(HEAD), grad_qkv, d_out


def solution(mesh):
    cell = P(("groups", "dom"), None)
    return jax.shard_map(
        functools.partial(body, mesh.shape["dom"]),
        mesh=mesh,
        in_specs=(cell, P(("groups", "dom")), P(), P(), P(), P(), P(), P(), cell),
        out_specs=(
            cell,
            cell,
            P("groups", None),
            P("groups", None),
            P("groups", None),
            P("groups"),
            P("groups", None, None),
            P("groups", None),
        ),
        check_vma=False,
    )
```
